32 devices in a mesh: groups: 2 (over y), tm: 4 (over x, core), space: 4 (over z).
Axes of the slice: x: 2, y: 2, z: 4, core: 2. Of those that a mesh axis runs over, the one named last changes fastest.
Arguments:
- features: bfloat16 [8, 32, 128, 256], P(('groups', 'tm'), 'space'), parts along dimension 0, may hold values from -6 to 6
- pair_order: int32 [8], P(('groups', 'tm')), parts along dimension 0, may hold values 0 or 1
- flow_now: bfloat16 [8, 2, 32, 128], P(('groups', 'tm'), None, 'space'), parts along dimension 0, may hold values from -8 to 8
- targets: int32 [8, 2, 32, 128], P(('groups', 'tm'), None, 'space'), parts along dimension 0, may hold values from -4 to 4
- w_volume: bfloat16 [162, 128], replicated, may hold values from -0.5 to 0.5
- b_volume: float32 [128], replicated, may hold values from -3 to 3
- w_code: bfloat16 [3, 3, 128, 128], replicated, may hold values from -0.1875 to 0.1875
- b_code: float32 [128], replicated, may hold values from -3 to 3
- w_flow: bfloat16 [7, 7, 2, 128], replicated, may hold values from -0.625 to 0.625
- b_flow: float32 [128], replicated, may hold values from -3 to 3
- w_joint: bfloat16 [3, 3, 256, 128], replicated, may hold values from -0.125 to 0.125
- b_joint: float32 [128], replicated, may hold values from -3 to 3
- w_head: bfloat16 [128, 2], replicated, may hold values from -0.5 to 0.5
- b_head: float32 [2], replicated, may hold values from -3 to 3
Outputs:
- loss: float32 [2], P('groups'), parts along dimension 0
- flow_error: float32 [8, 2, 32, 128], P(('groups', 'tm'), None, 'space'), parts along dimension 0
- grad_w_volume: float32 [324, 128], P('groups'), parts along dimension 0
- grad_b_volume: float32 [256], P('groups'), parts along dimension 0
- grad_w_code: float32 [6, 3, 128, 128], P('groups'), parts along dimension 0
- grad_b_code: float32 [256], P('groups'), parts along dimension 0
- grad_w_flow: float32 [14, 7, 2, 128], P('groups'), parts along dimension 0
- grad_b_flow: float32 [256], P('groups'), parts along dimension 0
- grad_w_joint: float32 [6, 3, 256, 128], P('groups'), parts along dimension 0
- grad_b_joint: float32 [256], P('groups'), parts along dimension 0
- grad_w_head: float32 [256, 2], P('groups'), parts along dimension 0
- grad_b_head: float32 [4], P('groups'), parts along dimension 0
The draws below stay inside these ranges and needn't reach their ends.
There are 2 independent parts, one for each index of `groups`. The reference program is written for one: setup_inputs(seed, part) draws one part's arguments, and reference() takes and returns one part's arrays. A program takes and returns all parts, laid end to end along the dimension named above; an argument that names none is the same for every part. Nothing has to cross between parts.
All inputs are finite; a program needn't handle non-finite values. No bound on the sum of `pair_order` on one device may be relied on, other than what follows from the above.
Results may differ from the reference program's by a relative error of at most 0.0032.
Values may be sent and summed in bfloat16 or wider, within the bound.
No kernel may reach another device: no remote copies, remote signals or barrier semaphores. Data moves between devices by JAX's collectives and lax.ppermute only.
A program may use at most 64 MiB of HBM per device.

```python
import jax
import jax.numpy as jnp
from jax import lax

C = 256
CM = 128
RADIUS = 4
COLS = 128
OFF = 81
FRAMES = 4
HEIGHT = 32


def touch_ends(values, rng, low, largest):
    longest = values.shape.index(max(values.shape))
    spots = []
    for shift in (0, 1):
        where = [jax.random.randint(jax.random.fold_in(rng, axis), (), 0, length) for axis, length in enumerate(values.shape)]
        where[longest] = (where[longest] + shift) % values.shape[longest]
        spots.append(tuple(where))
    return values.at[spots[0]].set(low).at[spots[1]].set(largest)


def level_of(own_key, dims, cuts, least, top_value):
    gain, own = 1.0, jax.random.fold_in(own_key, 6)
    for position, shards_of in cuts:
        draws = jnp.exp(jax.random.uniform(jax.random.fold_in(own, position), (shards_of,), jnp.float32, least / len(cuts), top_value / len(cuts)))
        gain = gain * jnp.repeat(draws, dims[position] // shards_of).reshape([-1 if axis == position else 1 for axis in range(len(dims))])
    return gain


def gaussian(stream_key, shape, scale, most, pieces=(), dtype=jnp.bfloat16):
    factor_of = level_of(stream_key, shape, pieces, -0.22, 0.18) if pieces else 1.0
    drawn = jax.random.normal(stream_key, shape, jnp.float32) * scale * factor_of
    return jnp.minimum(jnp.maximum(drawn, -most), most).astype(dtype)


def setup_inputs(seed: int = 0, part: int = 0) -> dict:
    key_list = jax.random.split(jax.random.key(seed), 15)
    part_keys = jax.random.split(jax.random.fold_in(key_list[14], part), 15)
    return {
        "features": gaussian(part_keys[0], (FRAMES, HEIGHT, COLS, C), 1.0, 6.0, ((0, 4), (1, 4))),
        "pair_order": touch_ends((jax.random.randint(part_keys[1], (FRAMES,), 0, 2) < 1).astype(jnp.int32), jax.random.fold_in(part_keys[1], 1), 0, 1),
        "flow_now": gaussian(part_keys[2], (FRAMES, 2, HEIGHT, COLS), 2.0, 8.0, ((0, 4), (2, 4))),
        "targets": touch_ends(jax.random.randint(part_keys[3], (FRAMES, 2, HEIGHT, COLS), -4, 5), jax.random.fold_in(part_keys[3], 1), -4, 4).astype(jnp.int32),
        "w_volume": gaussian(key_list[4], (2 * OFF, CM), (2 * OFF) ** -0.5, 0.5),
        "b_volume": gaussian(key_list[5], (CM,), 0.5, 3.0, (), jnp.float32),
        "w_code": gaussian(key_list[6], (3, 3, CM, CM), (9 * CM) ** -0.5, 0.1875),
        "b_code": gaussian(key_list[7], (CM,), 0.5, 3.0, (), jnp.float32),
        "w_flow": gaussian(key_list[8], (7, 7, 2, CM), 98 ** -0.5, 0.625),
        "b_flow": gaussian(key_list[9], (CM,), 0.5, 3.0, (), jnp.float32),
        "w_joint": gaussian(key_list[10], (3, 3, 2 * CM, CM), (18 * CM) ** -0.5, 0.125),
        "b_joint": gaussian(key_list[11], (CM,), 0.5, 3.0, (), jnp.float32),
        "w_head": gaussian(key_list[12], (CM, 2), CM ** -0.5, 0.5),
        "b_head": gaussian(key_list[13], (2,), 1.0, 3.0, (), jnp.float32),
    }


highest_precision = lax.Precision.HIGHEST

def silu_slope(values):
    sigma = jax.nn.sigmoid(values)
    return sigma * (1.0 + values * (1.0 - sigma))

def frame_volume(first_tile, second_tile):
    height = first_tile.shape[0]
    width = first_tile.shape[1]
    padded = jnp.pad(second_tile, ((RADIUS, RADIUS), (RADIUS, RADIUS), (0, 0)))
    first_float = first_tile.astype(jnp.float32)
    planes = []
    for row_off in range(2 * RADIUS + 1):
        for col_off in range(2 * RADIUS + 1):
            shifted = padded[row_off:row_off + height, col_off:col_off + width].astype(jnp.float32)
            planes.append(lax.optimization_barrier(jnp.sum(first_float * shifted, axis=-1)))
    return (jnp.stack(planes, axis=-1) * C ** (-0.5)).astype(jnp.bfloat16)

def conv_same(inputs, weight):
    ksize = weight.shape[0]
    half_k = ksize // 2
    height = inputs.shape[1]
    width = inputs.shape[2]
    padded = jnp.pad(inputs, ((0, 0), (half_k, half_k), (half_k, half_k), (0, 0)))
    summed = jnp.zeros(inputs.shape[:3] + (weight.shape[3],), jnp.float32)
    for i in range(ksize):
        for j in range(ksize):
            summed = summed + jnp.einsum('fhwc,cd->fhwd', padded[:, i:i + height, j:j + width].astype(jnp.float32), weight[i, j].astype(jnp.float32), precision=highest_precision)
    return summed

def conv_back(slope, weight):
    ksize = weight.shape[0]
    half_k = ksize // 2
    height = slope.shape[1]
    width = slope.shape[2]
    padded = jnp.pad(slope, ((0, 0), (half_k, half_k), (half_k, half_k), (0, 0)))
    summed = jnp.zeros(slope.shape[:3] + (weight.shape[2],), jnp.float32)
    for i in range(ksize):
        for j in range(ksize):
            row_at = ksize - 1 - i
            col_at = ksize - 1 - j
            summed = summed + jnp.einsum('fhwd,cd->fhwc', padded[:, row_at:row_at + height, col_at:col_at + width].astype(jnp.float32), weight[i, j].astype(jnp.float32), precision=highest_precision)
    return summed

def conv_grad(inputs, slope, ksize):
    half_k = ksize // 2
    height = inputs.shape[1]
    width = inputs.shape[2]
    padded = jnp.pad(inputs, ((0, 0), (half_k, half_k), (half_k, half_k), (0, 0)))
    slope_float = slope.astype(jnp.float32)
    taps = []
    for i in range(ksize):
        for j in range(ksize):
            taps.append(jnp.einsum('fhwc,fhwd->cd', padded[:, i:i + height, j:j + width].astype(jnp.float32), slope_float, precision=highest_precision))
    return jnp.stack(taps, axis=0).reshape(ksize, ksize, inputs.shape[3], slope.shape[3])

def reference(features, pair_order, flow_now, targets, w_volume, b_volume, w_code, b_code, w_flow, b_flow, w_joint, b_joint, w_head, b_head):
    blank = jnp.zeros_like(features[:1])
    later = jnp.concatenate([features[1:], blank], axis=0)
    earlier = jnp.concatenate([blank, features[:-1]], axis=0)
    forward = lax.map(lambda pair: frame_volume(pair[0], pair[1]), (features, later))
    backward = lax.map(lambda pair: frame_volume(pair[0], pair[1]), (features, earlier))
    swapped = (pair_order == 1)[:, None, None, None]
    volume = jnp.where(swapped, jnp.concatenate([backward, forward], axis=-1), jnp.concatenate([forward, backward], axis=-1))
    code_pre = jnp.einsum('fhwk,kd->fhwd', volume.astype(jnp.float32), w_volume.astype(jnp.float32), precision=highest_precision) + b_volume
    code = jax.nn.silu(code_pre).astype(jnp.bfloat16)
    motion_pre = conv_same(code, w_code) + b_code
    motion = jax.nn.silu(motion_pre).astype(jnp.bfloat16)
    flow_last = jnp.transpose(flow_now, (0, 2, 3, 1))
    flow_pre = conv_same(flow_last, w_flow) + b_flow
    flow_code = jax.nn.silu(flow_pre).astype(jnp.bfloat16)
    joint = jnp.concatenate([motion, flow_code], axis=-1)
    hidden_pre = conv_same(joint, w_joint) + b_joint
    hidden = jax.nn.silu(hidden_pre).astype(jnp.bfloat16)
    pred = jnp.einsum('fhwd,dk->fhwk', hidden.astype(jnp.float32), w_head.astype(jnp.float32), precision=highest_precision) + b_head
    target_last = jnp.transpose(targets, (0, 2, 3, 1)).astype(jnp.float32)
    error_last = pred - target_last
    flow_error = jnp.transpose(error_last, (0, 3, 1, 2))
    frame_index = jnp.arange(FRAMES).astype(jnp.float32)
    frame_weight = jnp.power(jnp.float32(0.25), (FRAMES - 1 - frame_index) / (FRAMES - 1))
    count = 2.0 * FRAMES * HEIGHT * COLS
    weighted = frame_weight[:, None, None, None]
    loss = jnp.reshape(jnp.sum(weighted * error_last * error_last) / count, (1,))
    slope_pred = 2.0 * weighted * error_last / count
    grad_w_head = jnp.einsum('fhwd,fhwk->dk', hidden.astype(jnp.float32), slope_pred, precision=highest_precision)
    grad_b_head = lax.optimization_barrier(jnp.sum(slope_pred, axis=(0, 1, 2)))
    slope_hidden = (jnp.einsum('fhwk,dk->fhwd', slope_pred, w_head.astype(jnp.float32), precision=highest_precision) * silu_slope(hidden_pre)).astype(jnp.bfloat16)
    grad_w_joint = conv_grad(joint, slope_hidden, 3)
    grad_b_joint = lax.optimization_barrier(jnp.sum(slope_hidden.astype(jnp.float32), axis=(0, 1, 2)))
    slope_joint = conv_back(slope_hidden, w_joint)
    slope_motion = (slope_joint[..., :CM] * silu_slope(motion_pre)).astype(jnp.bfloat16)
    slope_flow = (slope_joint[..., CM:] * silu_slope(flow_pre)).astype(jnp.bfloat16)
    grad_w_code = conv_grad(code, slope_motion, 3)
    grad_b_code = lax.optimization_barrier(jnp.sum(slope_motion.astype(jnp.float32), axis=(0, 1, 2)))
    grad_w_flow = conv_grad(flow_last, slope_flow, 7)
    grad_b_flow = lax.optimization_barrier(jnp.sum(slope_flow.astype(jnp.float32), axis=(0, 1, 2)))
    slope_code = (conv_back(slope_motion, w_code) * silu_slope(code_pre)).astype(jnp.bfloat16)
    grad_w_volume = jnp.einsum('fhwk,fhwd->kd', volume.astype(jnp.float32), slope_code.astype(jnp.float32), precision=highest_precision)
    grad_b_volume = lax.optimization_barrier(jnp.sum(slope_code.astype(jnp.float32), axis=(0, 1, 2)))
    return (loss, flow_error, grad_w_volume, grad_b_volume, grad_w_code, grad_b_code, grad_w_flow, grad_b_flow, grad_w_joint, grad_b_joint, grad_w_head, grad_b_head)
```

```python
import functools

import jax
import jax.numpy as jnp
from jax import lax
from jax.experimental import pallas as pl
from jax.experimental.pallas import tpu as pltpu
from jax.sharding import PartitionSpec as P

RADIUS = 4
SIDE = 2 * RADIUS + 1
OFF = SIDE * SIDE
HALO = 4
FLOW_HALO = 6
TARGET_HALO = 2
BF = jnp.bfloat16
F32 = jnp.float32
NT = (((1,), (1,)), ((), ()))
TN = (((0,), (0,)), ((), ()))

AT_CODE = 2304
AT_VOLUME = 3456
AT_FLOW = 3632
AT_MISC = 3744
GRAD_ROWS = 3840


def dot(a, b):
    return jnp.dot(a, b, preferred_element_type=F32)


def rows(start, count, unit):
    return pl.ds(pl.multiple_of(start * unit, unit), count * unit)


def split3(s):
    hi = s.astype(BF)
    rest = s - hi.astype(F32)
    mid = rest.astype(BF)
    return jnp.concatenate([hi, mid, (rest - mid.astype(F32)).astype(BF)], axis=0)


def silu_pair(v):
    s = jax.nn.sigmoid(v)
    return v * s, s * (1.0 + v * (1.0 - s))


def correlate_kernel(
    n_rows, n_cols,
    swap_ref, own_hbm, mid_n, top_n, bot_n, mid_p, top_p, bot_p,
    wv_ref, bias_ref, up_x, dn_x,
    vol_ref, code_ref, up_ref, dn_ref,
    own, near, sems,
):
    n_chan = own.shape[1]
    swap = swap_ref[0]
    halo = RADIUS * n_cols
    body = n_rows * n_cols
    copies = [pltpu.make_async_copy(own_hbm, own, sems.at[0])]
    for at, (slot, parts) in enumerate(((swap, (mid_n, top_n, bot_n)), (1 - swap, (mid_p, top_p, bot_p)))):
        mid, top, bot = parts
        copies.append(pltpu.make_async_copy(mid, near.at[slot, pl.ds(halo, body)], sems.at[3 * at + 1]))
        copies.append(pltpu.make_async_copy(top, near.at[slot, pl.ds(0, halo)], sems.at[3 * at + 2]))
        copies.append(pltpu.make_async_copy(bot, near.at[slot, pl.ds(halo + body, halo)], sems.at[3 * at + 3]))
    for copy in copies:
        copy.start()
    for copy in copies:
        copy.wait()
    x_at = lax.broadcasted_iota(jnp.int32, (n_cols, n_cols), 0)
    y_at = lax.broadcasted_iota(jnp.int32, (n_cols, n_cols), 1)
    band = jnp.abs(x_at - y_at) <= RADIUS
    scale = n_chan ** (-0.5)

    def one_row(r, carry):
        tile = own[rows(r, 1, n_cols), :]
        for half in range(2):
            scores = lax.dot_general(
                tile, near[half, rows(r, SIDE, n_cols), :], NT, preferred_element_type=F32
            )
            total = [jnp.zeros((8, n_cols), F32) for _ in range(n_cols // 8)]
            for off in range(SIDE):
                part = jnp.where(band, scores[:, off * n_cols : (off + 1) * n_cols], 0.0)
                for g in range(n_cols // 8):
                    shift = (off * SIDE + RADIUS - 8 * g) % n_cols
                    piece = part[8 * g : 8 * g + 8]
                    total[g] = total[g] + (pltpu.roll(piece, shift, 1) if shift else piece)
            full = jnp.concatenate(total, axis=0)
            for bit in (1, 2, 4):
                full = jnp.where((x_at & bit) != 0, pltpu.roll(full, n_cols - bit, 1), full)
            vol_ref[rows(r, 1, n_cols), half * n_cols : (half + 1) * n_cols] = (full * scale).astype(BF)
        return carry

    lax.fori_loop(0, n_rows, one_row, 0)

    def one_code(r, carry):
        pre = dot(vol_ref[rows(r, 2, n_cols), :], wv_ref[...]) + bias_ref[0:1, :]
        code_ref[rows(r, 2, n_cols), :] = (pre * jax.nn.sigmoid(pre)).astype(BF)
        return carry

    lax.fori_loop(0, n_rows // 2, lambda b, c: one_code(2 * b, c), 0)
    up_ref[0:halo, :] = code_ref[0:halo, :]
    up_ref[halo : halo + 16, :] = up_x[...]
    dn_ref[0:halo, :] = code_ref[body - halo : body, :]
    dn_ref[halo : halo + 16, :] = dn_x[...]


def train_kernel(
    n_rows, n_cols,
    ints, floats, vol, code, top, bot, flow, targets,
    wv, wc, wcb, wj, wjb, wf, wht, bias,
    error_out, grads,
    c3, j3, d_motion, d_flow, s3, m3, xf, xx, xb, err, tgt, hid, s_flow, s_code, jt, acc, g_head,
):
    W = n_cols
    C = wc.shape[2]
    body = n_rows * W
    halo = HALO * W
    row0 = ints[0]
    height = ints[1]
    x_at = lax.broadcasted_iota(jnp.int32, (W, C), 0)
    first = x_at == 0
    last = x_at == W - 1

    def inside(ext):
        at = row0 + ext
        return jnp.logical_and(at >= 0, at < height)

    def stack(ref, at, v, cols):
        left = jnp.where(first, 0.0, pltpu.roll(v, 1, 0))
        right = jnp.where(last, 0.0, pltpu.roll(v, W - 1, 0))
        for col, part in zip(cols, (left, v, right)):
            ref[rows(at, 1, W), col : col + C] = part.astype(BF)

    acc[...] = jnp.zeros_like(acc)
    g_head[...] = jnp.zeros_like(g_head)

    def add_rows(k, v):
        acc[8 * k : 8 * k + 8, :] += jnp.sum(v.reshape(v.shape[0] // 8, 8, C), axis=0)

    fwd = (0, C, 2 * C)
    bwd = (2 * C, C, 0)

    def load_halo(y, carry):
        stack(c3, y, top[rows(y, 1, W), :].astype(F32), fwd)
        stack(c3, y + HALO + n_rows, bot[rows(y, 1, W), :].astype(F32), fwd)
        return carry

    def load_code(y, carry):
        stack(c3, y + HALO, code[rows(y, 1, W), :].astype(F32), fwd)
        return carry

    lax.fori_loop(0, HALO, load_halo, 0)
    lax.fori_loop(0, n_rows, load_code, 0)

    xx[...] = jnp.zeros_like(xx)
    above = top[halo : halo + 16, :].astype(F32)
    below = bot[halo : halo + 16, :].astype(F32)
    n_flow = n_rows + 2 * FLOW_HALO
    lane = lax.broadcasted_iota(jnp.int32, (n_flow, W), 1)
    for k in range(2):
        xf[0:FLOW_HALO, :] = above[8 * k : 8 * k + FLOW_HALO, :]
        xf[FLOW_HALO : FLOW_HALO + n_rows, :] = flow[k].astype(F32)
        xf[FLOW_HALO + n_rows : n_flow, :] = below[8 * k : 8 * k + FLOW_HALO, :]
        own_flow = xf[0:n_flow, :]
        for j in range(7):
            shift = (3 - j) % W
            moved = pltpu.roll(own_flow, shift, 1) if shift else own_flow
            ok = jnp.logical_and(lane + (j - 3) >= 0, lane + (j - 3) < W)
            xx[pl.ds(j * 2 + k, n_flow, stride=16), :] = jnp.where(ok, moved, 0.0)
    xb[...] = xx[...].astype(BF)

    tgt[...] = jnp.zeros_like(tgt)
    for k in range(2):
        for y in range(TARGET_HALO):
            tgt[k : k + 1, y * W : (y + 1) * W] = above[8 * k + 6 + y : 8 * k + 7 + y, :]
            lo = (TARGET_HALO + n_rows + y) * W
            tgt[k : k + 1, lo : lo + W] = below[8 * k + 6 + y : 8 * k + 7 + y, :]
        for y in range(n_rows):
            lo = (TARGET_HALO + y) * W
            tgt[k : k + 1, lo : lo + W] = targets[k, y : y + 1, :].astype(F32)

    def joint_rows(b, carry):
        y = 2 * b
        pre = bias[1:2, :] + dot(c3[rows(y, 2, W), :], wc[0])
        pre = pre + dot(c3[rows(y + 1, 2, W), :], wc[1])
        pre = pre + dot(c3[rows(y + 2, 2, W), :], wc[2])
        for u in range(2):
            value, slope = silu_pair(pre[u * W : (u + 1) * W])
            d_motion[rows(y + u, 1, W), :] = slope
            ok = inside(y + u - 3)
            stack(j3, y + u, jnp.where(ok, value, 0.0), (0, 2 * C, 4 * C))
            patch = xb[pl.ds(pl.multiple_of((y + u) * 16, 16), 112), :]
            f_pre = lax.dot_general(patch, wf[...], TN, preferred_element_type=F32) + bias[2:3, :]
            value, slope = silu_pair(f_pre)
            d_flow[rows(y + u, 1, W), :] = slope
            stack(j3, y + u, jnp.where(ok, value, 0.0), (C, 3 * C, 5 * C))
        return carry

    lax.fori_loop(0, (n_rows + 6) // 2, joint_rows, 0)

    k_row = lax.broadcasted_iota(jnp.int32, (16, 2 * W), 0)
    b_head = jnp.where(k_row == 0, floats[2], jnp.where(k_row == 1, floats[3], 0.0))

    def hidden_rows(b, carry):
        y = 2 * b
        pre = bias[3:4, :] + dot(j3[rows(y, 2, W), :], wj[0])
        pre = pre + dot(j3[rows(y + 1, 2, W), :], wj[1])
        pre = pre + dot(j3[rows(y + 2, 2, W), :], wj[2])
        value, slope = silu_pair(pre)
        hidden = value.astype(BF)
        hid[rows(y, 2, W), :] = hidden
        pred = lax.dot_general(wht[0:16, :], hidden, NT, preferred_element_type=F32)
        error = pred + b_head - tgt[:, rows(y, 2, W)]
        err[:, rows(y, 2, W)] = error
        back = lax.dot_general(split3(error * floats[0]), wht[...], TN, preferred_element_type=F32) * slope
        for u in range(2):
            v = jnp.where(inside(y + u - 2), back[u * W : (u + 1) * W], 0.0)
            stack(s3, y + u, v, bwd)
        return carry

    lax.fori_loop(0, (n_rows + 4) // 2, hidden_rows, 0)

    own = err[:, TARGET_HALO * W : TARGET_HALO * W + body]
    for k in range(2):
        for y in range(n_rows):
            error_out[k, y : y + 1, :] = own[k : k + 1, y * W : (y + 1) * W]
    s = own * floats[0]
    g_b_head = jnp.sum(s, axis=1, keepdims=True)
    loss = jnp.sum(jnp.sum(own * own, axis=1, keepdims=True), axis=0, keepdims=True) * floats[1]

    def joint_slopes(b, carry):
        y = 2 * b
        sj = dot(s3[rows(y + 2, 2, W), :], wjb[0])
        sj = sj + dot(s3[rows(y + 1, 2, W), :], wjb[1])
        sj = sj + dot(s3[rows(y, 2, W), :], wjb[2])
        for u in range(2):
            part = sj[u * W : (u + 1) * W]
            v = part[:, 0:C] * d_motion[rows(y + u + 2, 1, W), :]
            stack(m3, y + u, jnp.where(inside(y + u - 1), v, 0.0), bwd)
            s_flow[rows(y + u, 1, W), :] = (part[:, C:] * d_flow[rows(y + u + 2, 1, W), :]).astype(BF)
        return carry

    lax.fori_loop(0, (n_rows + 2) // 2, joint_slopes, 0)

    def code_slopes(b, carry):
        y = 2 * b
        sc = dot(m3[rows(y + 2, 2, W), :], wcb[0])
        sc = sc + dot(m3[rows(y + 1, 2, W), :], wcb[1])
        sc = sc + dot(m3[rows(y, 2, W), :], wcb[2])
        pre = dot(vol[rows(y, 2, W), :], wv[...]) + bias[0:1, :]
        s_code[rows(y, 2, W), :] = (sc * silu_pair(pre)[1]).astype(BF)
        add_rows(0, s_code[rows(y, 2, W), :].astype(F32))
        add_rows(1, m3[rows(y + 1, 2, W), C : 2 * C].astype(F32))
        add_rows(2, s_flow[rows(y + 1, 2, W), :].astype(F32))
        add_rows(3, s3[rows(y + 2, 2, W), C : 2 * C].astype(F32))
        g_head[...] += dot(split3(err[:, rows(y + 2, 2, W)] * floats[0]), hid[rows(y + 2, 2, W), :])
        jt[:, rows(y, 2, W)] = j3[rows(y + 3, 2, W), 2 * C : 4 * C].T
        return carry

    lax.fori_loop(0, n_rows // 2, code_slopes, 0)

    for i in range(3):
        g = dot(jt[...], s3[(3 - i) * W : (3 - i) * W + body, :])
        for j in range(3):
            at = (i * 3 + j) * 2 * C
            grads[at : at + 2 * C, :] = g[:, j * C : (j + 1) * C]
    code_t = code[...].T
    for i in range(3):
        g = dot(code_t, m3[(2 - i) * W : (2 - i) * W + body, :])
        for j in range(3):
            at = AT_CODE + (i * 3 + j) * C
            grads[at : at + C, :] = g[:, j * C : (j + 1) * C]
    gv = lax.dot_general(vol[...], s_code[...], TN, preferred_element_type=F32)
    grads[AT_VOLUME : AT_VOLUME + 88, :] = gv[0:88]
    grads[AT_VOLUME + 88 : AT_VOLUME + 176, :] = gv[W : W + 88]
    gf = jnp.zeros((112, C), F32)
    for y in range(n_rows):
        gf = gf + dot(xb[(y + 3) * 16 : (y + 3) * 16 + 112, :], s_flow[(y + 1) * W : (y + 2) * W, :])
    grads[AT_FLOW : AT_FLOW + 112, :] = gf
    col = lax.broadcasted_iota(jnp.int32, (1, C), 1)
    tail = jnp.where(col == 0, loss, jnp.where(col == 1, g_b_head[0:1], jnp.where(col == 2, g_b_head[1:2], 0.0)))
    for k in range(4):
        grads[AT_MISC + k : AT_MISC + k + 1, :] = jnp.sum(acc[8 * k : 8 * k + 8, :], axis=0, keepdims=True)
    grads[AT_MISC + 4 : AT_MISC + 6, :] = g_head[0:2, :] + g_head[16:18, :] + g_head[32:34, :]
    grads[AT_MISC + 6 : AT_MISC + 7, :] = tail
    grads[AT_MISC + 7 : GRAD_ROWS, :] = jnp.zeros((GRAD_ROWS - AT_MISC - 7, C), F32)


VMEM = pl.BlockSpec(memory_space=pltpu.VMEM)
SMEM = pl.BlockSpec(memory_space=pltpu.SMEM)
ANY = pl.BlockSpec(memory_space=pl.ANY)


def reduce_all(x):
    steps = []
    for axis in ("tm", "space"):
        bit = 1
        while bit < lax.axis_size(axis):
            steps.append((axis, bit))
            bit *= 2
    for axis, bit in steps:
        upper = (lax.axis_index(axis) // bit) % 2
        half = x.shape[0] // 2
        keep = lax.dynamic_slice_in_dim(x, upper * half, half, 0)
        send = lax.dynamic_slice_in_dim(x, (1 - upper) * half, half, 0)
        route = [(i, i ^ bit) for i in range(lax.axis_size(axis))]
        x = keep + lax.ppermute(send, axis, route)
    for axis, bit in steps[::-1]:
        upper = (lax.axis_index(axis) // bit) % 2
        route = [(i, i ^ bit) for i in range(lax.axis_size(axis))]
        got = lax.ppermute(x, axis, route)
        x = jnp.where(upper == 0, jnp.concatenate([x, got]), jnp.concatenate([got, x]))
    return x


def local(
    features, pair_order, flow_now, targets, w_volume, b_volume, w_code, b_code,
    w_flow, b_flow, w_joint, b_joint, w_head, b_head,
):
    own = features[0]
    n_rows, n_cols, n_chan = own.shape
    n_code = w_code.shape[3]
    body = n_rows * n_cols
    halo = HALO * n_cols
    n_tm, n_space = lax.axis_size("tm"), lax.axis_size("space")
    flat = own.reshape(body, n_chan)

    def route(dt, ds):
        pairs = []
        for t in range(n_tm):
            for s in range(n_space):
                if 0 <= t + dt < n_tm and 0 <= s + ds < n_space:
                    pairs.append((t * n_space + s, (t + dt) * n_space + s + ds))
        return pairs

    both = ("tm", "space")
    first, last = flat[:halo], flat[body - halo :]
    top_n = lax.ppermute(last, both, route(-1, 1))
    bot_n = lax.ppermute(first, both, route(-1, -1))
    top_p = lax.ppermute(last, both, route(1, 1))
    bot_p = lax.ppermute(first, both, route(1, -1))
    mid_n = lax.ppermute(flat, both, route(-1, 0))
    mid_p = lax.ppermute(flat, both, route(1, 0))

    wv = jnp.pad(w_volume.reshape(2, OFF, n_code), ((0, 0), (0, n_cols - OFF), (0, 0))).reshape(2 * n_cols, n_code)
    wc = w_code.reshape(3, 3 * n_code, n_code)
    wcb = w_code.transpose(0, 1, 3, 2).reshape(3, 3 * n_code, n_code)
    wj = w_joint.reshape(3, 6 * n_code, n_code)
    wjb = w_joint.transpose(0, 1, 3, 2).reshape(3, 3 * n_code, 2 * n_code)
    wf = jnp.pad(w_flow.reshape(7, 14, n_code), ((0, 0), (0, 2), (0, 0))).reshape(112, n_code)
    wht = jnp.tile(jnp.pad(w_head.T, ((0, 14), (0, 0))), (3, 1))
    bias = jnp.stack([b_volume, b_code, b_flow, b_joint])
    frame_at = lax.axis_index("tm").astype(F32)
    frame_weight = jnp.power(F32(0.25), (n_tm - 1 - frame_at) / (n_tm - 1))
    height = n_rows * n_space
    count = 2.0 * n_tm * height * n_cols
    floats = jnp.stack([2.0 * frame_weight / count, frame_weight / count, b_head[0], b_head[1]])
    ints = jnp.stack([lax.axis_index("space") * n_rows, jnp.int32(height)]).astype(jnp.int32)
    flow = flow_now[0]
    near_targets = targets[0].astype(BF)
    up_x = jnp.concatenate([flow[:, :FLOW_HALO], near_targets[:, :TARGET_HALO]], axis=1).reshape(16, n_cols)
    dn_x = jnp.concatenate(
        [flow[:, n_rows - FLOW_HALO :], near_targets[:, n_rows - TARGET_HALO :]], axis=1
    ).reshape(16, n_cols)

    vol, code, up, dn = pl.pallas_call(
        functools.partial(correlate_kernel, n_rows, n_cols),
        out_shape=(
            jax.ShapeDtypeStruct((body, 2 * n_cols), BF),
            jax.ShapeDtypeStruct((body, n_code), BF),
            jax.ShapeDtypeStruct((halo + 16, n_code), BF),
            jax.ShapeDtypeStruct((halo + 16, n_code), BF),
        ),
        in_specs=[SMEM] + [ANY] * 7 + [VMEM] * 4,
        out_specs=(VMEM,) * 4,
        scratch_shapes=[
            pltpu.VMEM((body, n_chan), BF),
            pltpu.VMEM((2, body + 2 * halo, n_chan), BF),
            pltpu.SemaphoreType.DMA((7,)),
        ],
        name="correlate",
    )(pair_order, flat, mid_n, top_n, bot_n, mid_p, top_p, bot_p, wv, bias, up_x, dn_x)

    down_route = [(s, s + 1) for s in range(n_space - 1)]
    up_route = [(s + 1, s) for s in range(n_space - 1)]
    top = lax.ppermute(dn, "space", down_route)
    bot = lax.ppermute(up, "space", up_route)

    W, C = n_cols, n_code
    flow_error, grads = pl.pallas_call(
        functools.partial(train_kernel, n_rows, n_cols),
        out_shape=(
            jax.ShapeDtypeStruct((2, n_rows, n_cols), F32),
            jax.ShapeDtypeStruct((GRAD_ROWS, n_code), F32),
        ),
        in_specs=[SMEM, SMEM] + [VMEM] * 14,
        out_specs=(VMEM, VMEM),
        scratch_shapes=[
            pltpu.VMEM(((n_rows + 8) * W, 3 * C), BF),
            pltpu.VMEM(((n_rows + 6) * W, 6 * C), BF),
            pltpu.VMEM(((n_rows + 6) * W, C), F32),
            pltpu.VMEM(((n_rows + 6) * W, C), F32),
            pltpu.VMEM(((n_rows + 4) * W, 3 * C), BF),
            pltpu.VMEM(((n_rows + 2) * W, 3 * C), BF),
            pltpu.VMEM((24, W), F32),
            pltpu.VMEM(((n_rows + 12) * 16, W), F32),
            pltpu.VMEM(((n_rows + 12) * 16, W), BF),
            pltpu.VMEM((16, (n_rows + 4) * W), F32),
            pltpu.VMEM((16, (n_rows + 4) * W), F32),
            pltpu.VMEM(((n_rows + 4) * W, C), BF),
            pltpu.VMEM(((n_rows + 2) * W, C), BF),
            pltpu.VMEM((body, C), BF),
            pltpu.VMEM((2 * C, body), BF),
            pltpu.VMEM((32, C), F32),
            pltpu.VMEM((48, C), F32),
        ],
        name="train",
    )(ints, floats, vol, code, top, bot, flow, targets[0], wv, wc, wcb, wj, wjb, wf, wht, bias)

    grads = reduce_all(grads)
    misc = grads[AT_MISC : AT_MISC + 8]
    return (
        misc[6, 0:1],
        flow_error[None],
        grads[AT_VOLUME:AT_FLOW].reshape(2, 88, n_code)[:, :OFF].reshape(2 * OFF, n_code),
        misc[0],
        grads[AT_CODE:AT_VOLUME].reshape(3, 3, n_code, n_code),
        misc[1],
        grads[AT_FLOW : AT_FLOW + 112].reshape(7, 16, n_code)[:, :14].reshape(7, 7, 2, n_code),
        misc[2],
        grads[:AT_CODE].reshape(3, 3, 2 * n_code, n_code),
        misc[3],
        misc[4:6].T,
        misc[6, 1:3],
    )


def solution(mesh):
    placed = (
        P(("groups", "tm"), "space", None, None),
        P(("groups", "tm")),
        P(("groups", "tm"), None, "space", None),
        P(("groups", "tm"), None, "space", None),
    ) + (P(),) * 10
    return jax.shard_map(
        local,
        mesh=mesh,
        in_specs=placed,
        out_specs=(
            P("groups"),
            P(("groups", "tm"), None, "space", None),
            P("groups", None),
            P("groups"),
            P("groups", None, None, None),
            P("groups"),
            P("groups", None, None, None),
            P("groups"),
            P("groups", None, None, None),
            P("groups"),
            P("groups", None),
            P("groups"),
        ),
        check_vma=False,
    )
```

```python
import functools

import jax
import jax.numpy as jnp
from jax import lax
from jax.experimental import pallas as pl
from jax.experimental.pallas import tpu as pltpu
from jax.sharding import PartitionSpec as P

RADIUS = 4
SIDE = 2 * RADIUS + 1
OFF = SIDE * SIDE
HALO = 4
FLOW_HALO = 6
TARGET_HALO = 2
BF = jnp.bfloat16
F32 = jnp.float32
NT = (((1,), (1,)), ((), ()))
TN = (((0,), (0,)), ((), ()))

AT_CODE = 2304
AT_VOLUME = 3456
AT_FLOW = 3648
AT_END = 3760
HALF = 96
MISC_ROWS = 8


def dot(a, b):
    return jnp.dot(a, b, preferred_element_type=F32)


def dot_nt(a, b):
    return lax.dot_general(a, b, NT, preferred_element_type=F32)


def rows(start, count, unit):
    return pl.ds(pl.multiple_of(start * unit, unit), count * unit)


def split3(s):
    hi = s.astype(BF)
    rest = s - hi.astype(F32)
    mid = rest.astype(BF)
    return jnp.concatenate([hi, mid, (rest - mid.astype(F32)).astype(BF)], axis=0)


def silu_pair(v):
    s = jax.nn.sigmoid(v)
    return v * s, s * (1.0 + v * (1.0 - s))


def correlate_kernel(n_rows, n_cols, own, mid, top, bot, out, near, rows_f):
    n_chan = own.shape[1]
    halo = RADIUS * n_cols
    body = n_rows * n_cols
    near[0:halo, :] = top[...]
    near[halo : halo + body, :] = mid[...]
    near[halo + body :, :] = bot[...]
    W = n_cols
    j_at = lax.broadcasted_iota(jnp.int32, (W, 2 * W), 0)
    x_at = lax.broadcasted_iota(jnp.int32, (W, 2 * W), 1) & (W - 1)
    band = jnp.logical_and(j_at - x_at >= -RADIUS, j_at - x_at < RADIUS)
    edge = j_at - x_at == RADIUS
    turn = lax.broadcasted_iota(jnp.int32, (8, 2 * W), 1) + RADIUS
    scale = n_chan ** (-0.5)

    def fold(v):
        parts = [v[8 * g : 8 * g + 8] for g in range(W // 8)]
        while len(parts) > 1:
            parts = [parts[k] + parts[k + 1] for k in range(0, len(parts), 2)]
        return parts[0]

    def two_rows(b, carry):
        tile = own[rows(2 * b, 2, W), :]
        rows_f[...] = jnp.zeros_like(rows_f)
        for q in range(SIDE + 1):
            scores = lax.dot_general(
                near[rows(2 * b + q, 1, W), :], tile, NT, preferred_element_type=F32
            )
            inner = fold(jnp.where(band, scores, 0.0))
            outer = jnp.sum(fold(jnp.where(edge, scores, 0.0)), axis=0, keepdims=True)
            for bit in (1, 2, 4):
                inner = jnp.where((turn & bit) != 0, pltpu.roll(inner, 8 - bit, 0), inner)
            for u in range(2):
                dy = q - u
                if 0 <= dy < SIDE:
                    rows_f[8 * dy : 8 * dy + 8, u * W : (u + 1) * W] = inner[:, u * W : (u + 1) * W]
                    rows_f[72 + dy : 73 + dy, u * W : (u + 1) * W] = outer[:, u * W : (u + 1) * W]
        out[:, rows(2 * b, 2, W)] = (rows_f[...] * scale).astype(BF)
        return carry

    lax.fori_loop(0, n_rows // 2, two_rows, 0)


def code_kernel(
    n_rows, n_cols,
    order, near_vol, far_vol, w_volume, bias, flow, targets,
    vol, code, up, dn, wv,
    wide, edge,
):
    W = n_cols
    halo = HALO * W
    body = n_rows * W
    wide[...] = jnp.zeros_like(wide)
    weight = w_volume[...].astype(F32)
    for half in range(2):
        for dy in range(SIDE):
            at = half * OFF + dy * SIDE
            wide[half * HALF + 8 * dy : half * HALF + 8 * dy + 8, :] = weight[at : at + 8]
            wide[half * HALF + 72 + dy : half * HALF + 73 + dy, :] = weight[at + 8 : at + 9]
    wv[...] = wide[...].astype(BF)
    near_second = order[0] != lax.axis_index("tm") % 2
    a, b = near_vol[...], far_vol[...]
    vol[0:HALF, :] = jnp.where(near_second, b, a)
    vol[HALF : 2 * HALF, :] = jnp.where(near_second, a, b)

    def one_code(r, carry):
        at = rows(r, 2, W)
        pre = lax.dot_general(vol[:, at], wv[...], TN, preferred_element_type=F32) + bias[0:1, :]
        code[at, :] = (pre * jax.nn.sigmoid(pre)).astype(BF)
        return carry

    lax.fori_loop(0, n_rows // 2, lambda r, c: one_code(2 * r, c), 0)
    for ref, at, flow_at, target_at in (
        (up, 0, 0, 0),
        (dn, body - halo, n_rows - FLOW_HALO, n_rows - TARGET_HALO),
    ):
        ref[0:halo, :] = code[at : at + halo, :]
        for k in range(2):
            edge[8 * k : 8 * k + FLOW_HALO, :] = flow[k].astype(F32)[flow_at : flow_at + FLOW_HALO]
            edge[8 * k + FLOW_HALO : 8 * k + 8, :] = targets[k].astype(F32)[target_at : target_at + TARGET_HALO]
        ref[halo : halo + 16, :] = edge[...].astype(BF)


def frame_scale(n_tm, per):
    frame = lax.axis_index("tm")
    value = jnp.float32(per)
    for t in range(n_tm - 1):
        value = jnp.where(frame == t, jnp.float32(per * 0.25 ** ((n_tm - 1 - t) / (n_tm - 1))), value)
    return value


def inside_frame(n_rows, ext):
    at = lax.axis_index("space") * n_rows + ext
    return jnp.logical_and(at >= 0, at < lax.axis_size("space") * n_rows)


def store_stack(ref, at, v, cols):
    W, C = v.shape
    x_at = lax.broadcasted_iota(jnp.int32, (W, C), 0)
    left = jnp.where(x_at == 0, 0.0, pltpu.roll(v, 1, 0))
    right = jnp.where(x_at == W - 1, 0.0, pltpu.roll(v, W - 1, 0))
    for col, part in zip(cols, (left, v, right)):
        ref[rows(at, 1, W), col * C : (col + 1) * C] = part.astype(BF)


FWD = (0, 1, 2)
BWD = (2, 1, 0)


def flow_kernel(n_rows, n_cols, top, bot, flow, targets, w_flow, bias, jf, d_flow, xb, tgt, xf, xx, wide, wf):
    W = n_cols
    halo = HALO * W
    wide[...] = jnp.zeros_like(wide)
    for i in range(7):
        for j in range(7):
            wide[16 * i + 2 * j : 16 * i + 2 * j + 2, :] = w_flow[i, j].astype(F32)
    wf[...] = wide[...].astype(BF)
    xx[...] = jnp.zeros_like(xx)
    above = top[halo : halo + 16, :].astype(F32)
    below = bot[halo : halo + 16, :].astype(F32)
    n_flow = n_rows + 2 * FLOW_HALO
    lane = lax.broadcasted_iota(jnp.int32, (n_flow, W), 1)
    for k in range(2):
        xf[0:FLOW_HALO, :] = above[8 * k : 8 * k + FLOW_HALO, :]
        xf[FLOW_HALO : FLOW_HALO + n_rows, :] = flow[k].astype(F32)
        xf[FLOW_HALO + n_rows : n_flow, :] = below[8 * k : 8 * k + FLOW_HALO, :]
        own_flow = xf[0:n_flow, :]
        for j in range(7):
            shift = (3 - j) % W
            moved = pltpu.roll(own_flow, shift, 1) if shift else own_flow
            ok = jnp.logical_and(lane + (j - 3) >= 0, lane + (j - 3) < W)
            xx[pl.ds(j * 2 + k, n_flow, stride=16), :] = jnp.where(ok, moved, 0.0)
    xb[...] = xx[...].astype(BF)
    tgt[...] = jnp.zeros_like(tgt)
    for k in range(2):
        for y in range(TARGET_HALO):
            tgt[k : k + 1, y * W : (y + 1) * W] = above[8 * k + 6 + y : 8 * k + 7 + y, :]
            lo = (TARGET_HALO + n_rows + y) * W
            tgt[k : k + 1, lo : lo + W] = below[8 * k + 6 + y : 8 * k + 7 + y, :]
        for y in range(n_rows):
            lo = (TARGET_HALO + y) * W
            tgt[k : k + 1, lo : lo + W] = targets[k, y : y + 1, :].astype(F32)

    def one_row(y, carry):
        patch = xb[pl.ds(pl.multiple_of(y * 16, 16), 112), :]
        pre = lax.dot_general(patch, wf[...], TN, preferred_element_type=F32) + bias[2:3, :]
        value, slope = silu_pair(pre)
        d_flow[rows(y, 1, W), :] = slope
        store_stack(jf, y, jnp.where(inside_frame(n_rows, y - 3), value, 0.0), FWD)
        return carry

    lax.fori_loop(0, n_rows + 6, one_row, 0)


def hidden_kernel(
    n_rows, n_cols, n_tm,
    b_head, code, top, bot, jf, tgt, wc, w_joint, w_head, bias,
    error_out, jt, s3, d_motion, misc,
    c3, jm, err, hid, g_head, acc, wjm, wjf, square, wht,
):
    W = n_cols
    count = 2.0 * n_tm * lax.axis_size("space") * n_rows * n_cols
    slope_scale = frame_scale(n_tm, 2.0 / count)
    for i in range(3):
        for j in range(3):
            wjm[i, j * 128 : (j + 1) * 128, :] = w_joint[i, j, 0:128, :]
            wjf[i, j * 128 : (j + 1) * 128, :] = w_joint[i, j, 128:256, :]
    square[...] = jnp.zeros_like(square)
    square[:, 0:2] = w_head[...].astype(F32)
    head_t = square[...].T[0:16].astype(BF)
    for k in range(3):
        wht[16 * k : 16 * k + 16, :] = head_t
    C = wc.shape[2]
    body = n_rows * W

    def load_halo(y, carry):
        store_stack(c3, y, top[rows(y, 1, W), :].astype(F32), FWD)
        store_stack(c3, y + HALO + n_rows, bot[rows(y, 1, W), :].astype(F32), FWD)
        return carry

    def load_code(y, carry):
        store_stack(c3, y + HALO, code[rows(y, 1, W), :].astype(F32), FWD)
        return carry

    lax.fori_loop(0, HALO, load_halo, 0)
    lax.fori_loop(0, n_rows, load_code, 0)

    def motion_rows(b, carry):
        y = 2 * b
        pre = bias[1:2, :] + dot(c3[rows(y, 2, W), :], wc[0])
        pre = pre + dot(c3[rows(y + 1, 2, W), :], wc[1])
        pre = pre + dot(c3[rows(y + 2, 2, W), :], wc[2])
        for u in range(2):
            value, slope = silu_pair(pre[u * W : (u + 1) * W])
            d_motion[rows(y + u, 1, W), :] = slope
            store_stack(jm, y + u, jnp.where(inside_frame(n_rows, y + u - 3), value, 0.0), FWD)
        return carry

    lax.fori_loop(0, (n_rows + 6) // 2, motion_rows, 0)

    k_row = lax.broadcasted_iota(jnp.int32, (16, 2 * W), 0)
    b_col = jnp.where(k_row == 0, b_head[0], jnp.where(k_row == 1, b_head[1], 0.0))

    def hidden_rows(b, carry):
        y = 2 * b
        pre = bias[3:4, :] + dot(jm[rows(y, 2, W), :], wjm[0])
        pre = pre + dot(jf[rows(y, 2, W), :], wjf[0])
        for i in (1, 2):
            pre = pre + dot(jm[rows(y + i, 2, W), :], wjm[i])
            pre = pre + dot(jf[rows(y + i, 2, W), :], wjf[i])
        value, slope = silu_pair(pre)
        hidden = value.astype(BF)
        hid[rows(y, 2, W), :] = hidden
        pred = lax.dot_general(wht[0:16, :], hidden, NT, preferred_element_type=F32)
        error = pred + b_col - tgt[:, rows(y, 2, W)]
        err[:, rows(y, 2, W)] = error
        back = lax.dot_general(split3(error * slope_scale), wht[...], TN, preferred_element_type=F32) * slope
        for u in range(2):
            v = jnp.where(inside_frame(n_rows, y + u - 2), back[u * W : (u + 1) * W], 0.0)
            store_stack(s3, y + u, v, BWD)
        return carry

    lax.fori_loop(0, (n_rows + 4) // 2, hidden_rows, 0)

    acc[...] = jnp.zeros_like(acc)
    g_head[...] = jnp.zeros_like(g_head)

    def own_rows(b, carry):
        y = 2 * b
        g_head[...] += dot(split3(err[:, rows(y + 2, 2, W)] * slope_scale), hid[rows(y + 2, 2, W), :])
        part = s3[rows(y + 2, 2, W), C : 2 * C].astype(F32)
        acc[...] += jnp.sum(part.reshape(2 * W // 8, 8, C), axis=0)
        jt[0:C, rows(y, 2, W)] = jm[rows(y + 3, 2, W), C : 2 * C].T
        jt[C : 2 * C, rows(y, 2, W)] = jf[rows(y + 3, 2, W), C : 2 * C].T
        return carry

    lax.fori_loop(0, n_rows // 2, own_rows, 0)
    own = err[:, TARGET_HALO * W : TARGET_HALO * W + body]
    for k in range(2):
        for y in range(n_rows):
            error_out[k, y : y + 1, :] = own[k : k + 1, y * W : (y + 1) * W]
    g_b_head = jnp.sum(own * slope_scale, axis=1, keepdims=True)
    loss = jnp.sum(jnp.sum(own * own, axis=1, keepdims=True), axis=0, keepdims=True)
    loss = loss * frame_scale(n_tm, 1.0 / count)
    col = lax.broadcasted_iota(jnp.int32, (1, C), 1)
    tail = jnp.where(col == 0, loss, jnp.where(col == 1, g_b_head[0:1], jnp.where(col == 2, g_b_head[1:2], 0.0)))
    misc[0:3, :] = jnp.zeros((3, C), F32)
    misc[3:4, :] = jnp.sum(acc[...], axis=0, keepdims=True)
    misc[4:6, :] = g_head[0:2, :] + g_head[16:18, :] + g_head[32:34, :]
    misc[6:7, :] = tail
    misc[7:8, :] = jnp.zeros((1, C), F32)


def rest_kernel(
    n_rows, n_cols, at_misc,
    jt, s3, d_motion, d_flow, xb, vol, code, misc, wv, w_code, w_joint, bias,
    keep, send,
    m3, s_flow, s_code, acc, grads, wcb, wjb,
):
    W = n_cols
    C = code.shape[1]
    body = n_rows * W
    for i in range(3):
        for j in range(3):
            wcb[i, :, j * C : (j + 1) * C] = w_code[i, j]
            wjb[i, :, j * C : (j + 1) * C] = w_joint[i, j]

    def joint_slopes(b, carry):
        y = 2 * b
        sj = dot_nt(s3[rows(y + 2, 2, W), :], wjb[0])
        sj = sj + dot_nt(s3[rows(y + 1, 2, W), :], wjb[1])
        sj = sj + dot_nt(s3[rows(y, 2, W), :], wjb[2])
        for u in range(2):
            part = sj[u * W : (u + 1) * W]
            v = part[:, 0:C] * d_motion[rows(y + u + 2, 1, W), :]
            store_stack(m3, y + u, jnp.where(inside_frame(n_rows, y + u - 1), v, 0.0), BWD)
            s_flow[rows(y + u, 1, W), :] = (part[:, C:] * d_flow[rows(y + u + 2, 1, W), :]).astype(BF)
        return carry

    lax.fori_loop(0, (n_rows + 2) // 2, joint_slopes, 0)
    acc[...] = jnp.zeros_like(acc)

    def add_rows(k, v):
        acc[8 * k : 8 * k + 8, :] += jnp.sum(v.reshape(v.shape[0] // 8, 8, C), axis=0)

    def code_slopes(b, carry):
        y = 2 * b
        sc = dot_nt(m3[rows(y + 2, 2, W), :], wcb[0])
        sc = sc + dot_nt(m3[rows(y + 1, 2, W), :], wcb[1])
        sc = sc + dot_nt(m3[rows(y, 2, W), :], wcb[2])
        pre = lax.dot_general(vol[:, rows(y, 2, W)], wv[...], TN, preferred_element_type=F32) + bias[0:1, :]
        s_code[rows(y, 2, W), :] = (sc * silu_pair(pre)[1]).astype(BF)
        add_rows(0, s_code[rows(y, 2, W), :].astype(F32))
        add_rows(1, m3[rows(y + 1, 2, W), C : 2 * C].astype(F32))
        add_rows(2, s_flow[rows(y + 1, 2, W), :].astype(F32))
        return carry

    lax.fori_loop(0, n_rows // 2, code_slopes, 0)

    for i in range(3):
        g = dot(jt[...], s3[(3 - i) * W : (3 - i) * W + body, :])
        for j in range(3):
            at = (i * 3 + j) * 2 * C
            grads[at : at + 2 * C, :] = g[:, j * C : (j + 1) * C]
    code_t = code[...].T
    for i in range(3):
        g = dot(code_t, m3[(2 - i) * W : (2 - i) * W + body, :])
        for j in range(3):
            at = AT_CODE + (i * 3 + j) * C
            grads[at : at + C, :] = g[:, j * C : (j + 1) * C]
    grads[AT_VOLUME:AT_FLOW, :] = dot(vol[...], s_code[...])
    gf = jnp.zeros((112, C), F32)
    for y in range(n_rows):
        gf = gf + dot(xb[(y + 3) * 16 : (y + 3) * 16 + 112, :], s_flow[(y + 1) * W : (y + 2) * W, :])
    grads[AT_FLOW : AT_FLOW + 112, :] = gf
    if at_misc > AT_END:
        grads[AT_END:at_misc, :] = jnp.zeros((at_misc - AT_END, C), F32)
    for k in range(3):
        grads[at_misc + k : at_misc + k + 1, :] = jnp.sum(acc[8 * k : 8 * k + 8, :], axis=0, keepdims=True)
    grads[at_misc + 3 : at_misc + 8, :] = misc[3:8, :]
    grads[at_misc + 8 :, :] = jnp.zeros((grads.shape[0] - at_misc - 8, C), F32)
    half = keep.shape[0]
    core = lax.axis_index("tm") % 2
    keep[...] = pick(grads, core, half)
    send[...] = pick(grads, 1 - core, half)


VMEM = pl.BlockSpec(memory_space=pltpu.VMEM)
SMEM = pl.BlockSpec(memory_space=pltpu.SMEM)
ANY = pl.BlockSpec(memory_space=pl.ANY)


def bits_of(axis):
    bits = []
    bit = 1
    while bit < lax.axis_size(axis):
        bits.append((axis, bit))
        bit *= 2
    return bits


def trade(x, axis, bit):
    return lax.ppermute(x, axis, [(i, i ^ bit) for i in range(lax.axis_size(axis))])


def upper_of(axis, bit):
    return (lax.axis_index(axis) // bit) % 2


def three_terms(x, at, is_last):
    value = x[at : at + MISC_ROWS]
    mid = value - lax.reduce_precision(value, 8, 7)
    low = mid - lax.reduce_precision(mid, 8, 7)
    terms = jnp.concatenate([x[: at + MISC_ROWS], mid, low, x[at + 3 * MISC_ROWS :]])
    return jnp.where(is_last, terms, x).astype(BF)


def halving_reduce(x, steps, is_last):
    for axis, bit in steps:
        upper = upper_of(axis, bit)
        is_last = is_last * upper
        half = x.shape[0] // 2
        mine = lax.dynamic_slice_in_dim(x, upper * half, half, 0)
        other = lax.dynamic_slice_in_dim(x, (1 - upper) * half, half, 0)
        x = mine + trade(other, axis, bit)
    x = three_terms(x, 0, is_last == 1)
    for axis, bit in steps[::-1]:
        got = trade(x, axis, bit)
        x = jnp.where(upper_of(axis, bit) == 0, jnp.concatenate([x, got]), jnp.concatenate([got, x]))
    return x


def pick(ref, which, half):
    return ref[pl.ds(pl.multiple_of(which * half, 8), half), :]


def first_split(bits, keep, got, a_keep, a_send, b_keep, b_send, total):
    quarter = a_keep.shape[0]
    total[...] = keep[...] + got[...]
    for at, (k, s, bit) in enumerate(((a_keep, a_send, bits[1]), (b_keep, b_send, bits[2]))):
        k[...] = total[pl.ds(pl.multiple_of((2 * at + bit) * quarter, 8), quarter), :]
        s[...] = total[pl.ds(pl.multiple_of((2 * at + 1 - bit) * quarter, 8), quarter), :]


def second_split(bits, a_keep, a_got, b_keep, b_got, a_mine, a_send, b_mine, b_send, total):
    half = a_mine.shape[0]
    for keep, got, mine, send, bit in (
        (a_keep, a_got, a_mine, a_send, bits[2]),
        (b_keep, b_got, b_mine, b_send, bits[1]),
    ):
        total[...] = keep[...] + got[...]
        mine[...] = pick(total, bit, half)
        send[...] = pick(total, 1 - bit, half)


def third_split(bits, a_keep, a_got, b_keep, b_got, keep, send, total):
    n = a_keep.shape[0]
    total[0:n, :] = a_keep[...] + a_got[...]
    total[n : 2 * n, :] = b_keep[...] + b_got[...]
    keep[...] = pick(total, bits[3], n)
    send[...] = pick(total, 1 - bits[3], n)


def last_sum(at, bits, keep, got, out, total):
    total[...] = keep[...] + got[...]
    value = total[at : at + MISC_ROWS, :]
    mid = value - value.astype(BF).astype(F32)
    low = mid - mid.astype(BF).astype(F32)
    is_last = bits[0] + bits[1] + bits[2] + bits[3] == 4
    total[at + MISC_ROWS : at + 2 * MISC_ROWS, :] = jnp.where(is_last, mid, total[at + MISC_ROWS : at + 2 * MISC_ROWS, :])
    total[at + 2 * MISC_ROWS : at + 3 * MISC_ROWS, :] = jnp.where(
        is_last, low, total[at + 2 * MISC_ROWS : at + 3 * MISC_ROWS, :]
    )
    out[...] = total[...].astype(BF)


def first_merge(bits, mine, got, a_out, b_out):
    first = bits[3] == 0
    a_out[...] = jnp.where(first, mine[...], got[...])
    b_out[...] = jnp.where(first, got[...], mine[...])


def pair_merge(x_first, bits, a_mine, a_got, b_mine, b_got, a_out, b_out):
    n = a_mine.shape[0]
    a_bit, b_bit = (bits[1], bits[2]) if x_first else (bits[2], bits[1])
    for mine, got, out, bit in ((a_mine, a_got, a_out, a_bit), (b_mine, b_got, b_out, b_bit)):
        out[pl.ds(pl.multiple_of(bit * n, 16), n), :] = mine[...]
        out[pl.ds(pl.multiple_of((1 - bit) * n, 16), n), :] = got[...]


def join_merge(bits, a_mine, a_got, b_mine, b_got, out):
    n = a_mine.shape[0]
    for at, (mine, got, bit) in enumerate(((a_mine, a_got, bits[1]), (b_mine, b_got, bits[2]))):
        out[pl.ds(pl.multiple_of((2 * at + bit) * n, 16), n), :] = mine[...]
        out[pl.ds(pl.multiple_of((2 * at + 1 - bit) * n, 16), n), :] = got[...]


def paired_reduce(bits, keep, got, at_misc, shape):
    half, C = keep.shape
    x, z, far_z = ("tm", 2), ("space", 1), ("space", 2)

    def stage(body, name, n_out, n, dtype, scratch, *args):
        out = (shape(n, C, dtype=dtype),) * n_out
        return call(
            body, name, out, [SMEM] + [VMEM] * len(args),
            [pltpu.VMEM((scratch, C), F32)] if scratch else [], 10_000_000, bits, *args,
        )

    ak, as_, bk, bs = stage(first_split, "split1", 4, half // 4, F32, half, keep, got)
    ag, bg = trade(as_, *x), trade(bs, *z)
    ak, as_, bk, bs = stage(second_split, "split2", 4, half // 8, F32, half // 4, ak, ag, bk, bg)
    ag, bg = trade(as_, *z), trade(bs, *x)
    keep, send = stage(third_split, "split3", 2, half // 8, F32, half // 4, ak, ag, bk, bg)
    got = trade(send, *far_z)
    chunk = half // 8
    (y,) = stage(
        functools.partial(last_sum, at_misc - (2 * half - chunk)), "last", 1, chunk, BF, chunk, keep, got
    )
    a, b = stage(first_merge, "merge1", 2, chunk, BF, 0, y, trade(y, *far_z))
    a, b = stage(
        functools.partial(pair_merge, False), "merge2", 2, half // 4, BF, 0, a, trade(a, *z), b, trade(b, *x)
    )
    (out,) = stage(join_merge, "merge3", 1, half, BF, 0, a, trade(a, *x), b, trade(b, *z))
    return out


def finish_kernel(at_misc, bits, mine, other, joint, code, volume, flow, misc, full):
    half, C = mine.shape
    full[pl.ds(pl.multiple_of(bits[0] * half, 16), half), :] = mine[...]
    full[pl.ds(pl.multiple_of((1 - bits[0]) * half, 16), half), :] = other[...]
    for i in range(3):
        for j in range(3):
            at = (i * 3 + j) * 2 * C
            joint[i, j, :, :] = full[at : at + 2 * C, :].astype(F32)
            at = AT_CODE + (i * 3 + j) * C
            code[i, j, :, :] = full[at : at + C, :].astype(F32)
    parts = full[AT_VOLUME:AT_FLOW, :].astype(F32)
    for half_at in range(2):
        for dy in range(SIDE):
            at, to = half_at * HALF, half_at * OFF + dy * SIDE
            volume[to : to + 8, :] = parts[at + 8 * dy : at + 8 * dy + 8]
            volume[to + 8 : to + 9, :] = parts[at + 72 + dy : at + 73 + dy]
    for i in range(7):
        part = full[AT_FLOW + 16 * i : AT_FLOW + 16 * i + 16, :].astype(F32)
        for j in range(7):
            flow[i, j, :, :] = part[2 * j : 2 * j + 2]
    terms = full[at_misc : at_misc + 32, :].astype(F32)
    misc[...] = terms[0:8] + terms[8:16] + terms[16:24]


def call(body, name, out_shape, in_specs, scratch, flops, *args):
    held = [
        pltpu.with_memory_space_constraint(x, pltpu.VMEM) if spec is VMEM else x
        for x, spec in zip(args, in_specs, strict=True)
    ]
    return pl.pallas_call(
        body,
        out_shape=out_shape,
        in_specs=in_specs,
        out_specs=jax.tree.map(lambda _: VMEM, out_shape),
        scratch_shapes=scratch,
        cost_estimate=pl.CostEstimate(flops=flops, bytes_accessed=flops // 300, transcendentals=0),
        compiler_params=pltpu.CompilerParams(vmem_limit_bytes=16 << 20),
        name=name,
    )(*held)


def local(
    features, pair_order, flow_now, targets, w_volume, b_volume, w_code, b_code,
    w_flow, b_flow, w_joint, b_joint, w_head, b_head,
):
    own = features[0]
    n_rows, n_cols, n_chan = own.shape
    n_code = w_code.shape[3]
    W, C = n_cols, n_code
    body = n_rows * n_cols
    halo = HALO * n_cols
    n_tm, n_space = lax.axis_size("tm"), lax.axis_size("space")
    flat = own.reshape(body, n_chan)
    both = ("tm", "space")

    def route(partner, ds):
        pairs = []
        for t in range(n_tm):
            for s in range(n_space):
                if 0 <= partner(t) < n_tm and 0 <= s + ds < n_space:
                    pairs.append((t * n_space + s, partner(t) * n_space + s + ds))
        return pairs

    def near(t):
        return t + 1 - 2 * (t % 2)

    def far(t):
        return t - 1 + 2 * (t % 2)

    first, last = flat[:halo], flat[body - halo :]
    far_mid = lax.ppermute(flat, both, route(far, 0))
    far_top = lax.ppermute(last, both, route(far, 1))
    far_bot = lax.ppermute(first, both, route(far, -1))
    near_top = lax.ppermute(last, both, route(near, 1))
    near_bot = lax.ppermute(first, both, route(near, -1))
    near_mid = lax.ppermute(flat, both, route(near, 0))

    bias = jnp.stack([b_volume, b_code, b_flow, b_joint])
    flow = flow_now[0]

    def shape(*dims, dtype=BF):
        return pltpu.VMEM(dims, dtype)

    def result(*dims):
        return jax.ShapeDtypeStruct(dims, F32)

    def correlate(mid, top, bot, name):
        return call(
            functools.partial(correlate_kernel, n_rows, n_cols), name,
            shape(HALF, body), [VMEM] * 4,
            [pltpu.VMEM((body + 2 * halo, n_chan), BF), pltpu.VMEM((HALF, 2 * W), F32)],
            4_000_000_000,
            flat, mid, top, bot,
        )

    near_vol = correlate(near_mid, near_top, near_bot, "near")
    far_vol = correlate(far_mid, far_top, far_bot, "far")
    vol, code, up, dn, wv = call(
        functools.partial(code_kernel, n_rows, n_cols), "code",
        (
            shape(2 * HALF, body), shape(body, C), shape(halo + 16, C), shape(halo + 16, C),
            shape(2 * HALF, C),
        ),
        [SMEM] + [VMEM] * 6, [pltpu.VMEM((2 * HALF, C), F32), pltpu.VMEM((16, W), F32)], 500_000_000,
        pair_order, near_vol, far_vol, w_volume, bias, flow, targets[0],
    )
    top = lax.ppermute(dn, "space", [(s, s + 1) for s in range(n_space - 1)])
    bot = lax.ppermute(up, "space", [(s + 1, s) for s in range(n_space - 1)])

    jf, d_flow, xb, tgt = call(
        functools.partial(flow_kernel, n_rows, n_cols), "flow",
        (
            shape((n_rows + 6) * W, 3 * C),
            shape((n_rows + 6) * W, C, dtype=F32),
            shape((n_rows + 12) * 16, W),
            shape(16, (n_rows + 4) * W, dtype=F32),
        ),
        [VMEM] * 6,
        [
            pltpu.VMEM((24, W), F32),
            pltpu.VMEM(((n_rows + 12) * 16, W), F32),
            pltpu.VMEM((112, C), F32),
            pltpu.VMEM((112, C), BF),
        ],
        1_000_000_000,
        top, bot, flow, targets[0], w_flow, bias,
    )
    flow_error, jt, s3, d_motion, misc = call(
        functools.partial(hidden_kernel, n_rows, n_cols, n_tm), "hidden",
        (
            result(2, n_rows, W),
            shape(2 * C, body),
            shape((n_rows + 4) * W, 3 * C),
            shape((n_rows + 6) * W, C, dtype=F32),
            shape(MISC_ROWS, C, dtype=F32),
        ),
        [SMEM] + [VMEM] * 9,
        [
            pltpu.VMEM(((n_rows + 8) * W, 3 * C), BF),
            pltpu.VMEM(((n_rows + 6) * W, 3 * C), BF),
            pltpu.VMEM((16, (n_rows + 4) * W), F32),
            pltpu.VMEM(((n_rows + 4) * W, C), BF),
            pltpu.VMEM((48, C), F32),
            pltpu.VMEM((8, C), F32),
            pltpu.VMEM((3, 3 * C, C), BF),
            pltpu.VMEM((3, 3 * C, C), BF),
            pltpu.VMEM((C, C), F32),
            pltpu.VMEM((48, C), BF),
        ],
        4_000_000_000,
        b_head, code, top, bot, jf, tgt, w_code.reshape(3, 3 * C, C), w_joint, w_head, bias,
    )
    n_dev = n_tm * n_space
    paired = n_tm == 4 and n_space == 4
    if paired:
        grad_rows, at_misc = 3840, AT_END
    else:
        chunk = -(-max(pl.cdiv(AT_END, n_dev - 1), 3 * MISC_ROWS) // 16) * 16
        grad_rows, at_misc = n_dev * chunk, (n_dev - 1) * chunk
    keep, send = call(
        functools.partial(rest_kernel, n_rows, n_cols, at_misc), "rest",
        (shape(grad_rows // 2, C, dtype=F32), shape(grad_rows // 2, C, dtype=F32)),
        [VMEM] * 12,
        [
            pltpu.VMEM(((n_rows + 2) * W, 3 * C), BF),
            pltpu.VMEM(((n_rows + 2) * W, C), BF),
            pltpu.VMEM((body, C), BF),
            pltpu.VMEM((24, C), F32),
            pltpu.VMEM((grad_rows, C), F32),
            pltpu.VMEM((3, C, 3 * C), BF),
            pltpu.VMEM((3, 2 * C, 3 * C), BF),
        ],
        3_000_000_000,
        jt, s3, d_motion, d_flow, xb, vol, code, misc, wv, w_code, w_joint, bias,
    )
    core = ("tm", 1)
    got = trade(send, *core)
    bits = jnp.stack([upper_of("tm", 1), upper_of("tm", 2), upper_of("space", 1), upper_of("space", 2)])
    bits = bits.astype(jnp.int32)
    if paired:
        mine = paired_reduce(bits, keep, got, at_misc, shape)
    else:
        mine = halving_reduce(keep + got, bits_of("tm")[1:] + bits_of("space"), upper_of(*core))
    other = trade(mine, *core)
    outs = call(
        functools.partial(finish_kernel, at_misc), "finish",
        (
            result(3, 3, 2 * C, C),
            result(3, 3, C, C),
            result(2 * OFF, C),
            result(7, 7, 2, C),
            result(MISC_ROWS, C),
        ),
        [SMEM] + [VMEM] * 2, [pltpu.VMEM((grad_rows, C), BF)], 100_000_000,
        bits, mine, other,
    )
    joint, g_code, g_volume, g_flow, misc = outs
    return (
        misc[6, 0:1], flow_error[None], g_volume, misc[0], g_code, misc[1],
        g_flow, misc[2], joint, misc[3], misc[4:6].T, misc[6, 1:3],
    )


def solution(mesh):
    placed = (
        P(("groups", "tm"), "space", None, None),
        P(("groups", "tm")),
        P(("groups", "tm"), None, "space", None),
        P(("groups", "tm"), None, "space", None),
    ) + (P(),) * 10
    return jax.shard_map(
        local,
        mesh=mesh,
        in_specs=placed,
        out_specs=(
            P("groups"),
            P(("groups", "tm"), None, "space", None),
            P("groups", None),
            P("groups"),
            P("groups", None, None, None),
            P("groups"),
            P("groups", None, None, None),
            P("groups"),
            P("groups", None, None, None),
            P("groups"),
            P("groups", None),
            P("groups"),
        ),
        check_vma=False,
    )
```

```python
import functools

import jax
import jax.numpy as jnp
from jax import lax
from jax.experimental import pallas as pl
from jax.experimental.pallas import tpu as pltpu
from jax.sharding import PartitionSpec as P

BF = jnp.bfloat16
F32 = jnp.float32
RADIUS = 4
SIDE = 2 * RADIUS + 1
OFF = SIDE * SIDE
HALO = 4
FLOW_HALO = 6
TARGET_HALO = 2
NT = (((1,), (1,)), ((), ()))
TN = (((0,), (0,)), ((), ()))

AT_CODE = 2304
AT_VOLUME = 3456
AT_FLOW = 3648
AT_END = 3760
HALF = 96
MOTION_BLOCK = 7
HIDDEN_BLOCK = 12
SLOPE_BLOCK = 10
CODE_BLOCK = 4
MISC_ROWS = 8


def dot(a, b):
    return jnp.dot(a, b, preferred_element_type=F32)


def dot_nt(a, b):
    return lax.dot_general(a, b, NT, preferred_element_type=F32)


def rows(start, count, unit):
    return pl.ds(pl.multiple_of(start * unit, unit), count * unit)


def split3(s, padded=False):
    hi = s.astype(BF).astype(F32)
    mid = (s - hi).astype(BF).astype(F32)
    terms = [hi, mid, s - hi - mid] + [jnp.zeros_like(s)] * padded
    return jnp.concatenate(terms, axis=0).astype(BF)


def silu_pair(v):
    s = jax.nn.sigmoid(v)
    return v * s, s * (1.0 + v * (1.0 - s))


def correlate(n_rows, n_cols, own, mid, top, bot, out, out_at, near, rows_f):
    n_chan = own.shape[1]
    halo = RADIUS * n_cols
    body = n_rows * n_cols
    near[0:halo, :] = top[...]
    near[halo : halo + body, :] = mid[...]
    near[halo + body :, :] = bot[...]
    W = n_cols
    j_at = lax.broadcasted_iota(jnp.int32, (W, 2 * W), 0)
    x_at = lax.broadcasted_iota(jnp.int32, (W, 2 * W), 1) & (W - 1)
    band = jnp.logical_and(j_at - x_at >= -RADIUS, j_at - x_at < RADIUS)
    edge = j_at - x_at == RADIUS
    turn = lax.broadcasted_iota(jnp.int32, (8, 2 * W), 1) + RADIUS
    scale = n_chan ** (-0.5)

    def fold(v):
        parts = [v[8 * g : 8 * g + 8] for g in range(W // 8)]
        while len(parts) > 1:
            parts = [parts[k] + parts[k + 1] for k in range(0, len(parts), 2)]
        return parts[0]

    def two_rows(b, carry):
        tile = own[rows(2 * b, 2, W), :]
        rows_f[...] = jnp.zeros_like(rows_f)
        for q in range(SIDE + 1):
            scores = lax.dot_general(
                near[rows(2 * b + q, 1, W), :], tile, NT, preferred_element_type=F32
            )
            inner = fold(jnp.where(band, scores, 0.0))
            outer = jnp.sum(fold(jnp.where(edge, scores, 0.0)), axis=0, keepdims=True)
            for bit in (1, 2, 4):
                inner = jnp.where((turn & bit) != 0, pltpu.roll(inner, 8 - bit, 0), inner)
            for u in range(2):
                dy = q - u
                if 0 <= dy < SIDE:
                    rows_f[8 * dy : 8 * dy + 8, u * W : (u + 1) * W] = inner[:, u * W : (u + 1) * W]
                    rows_f[72 + dy : 73 + dy, u * W : (u + 1) * W] = outer[:, u * W : (u + 1) * W]
        out[out_at, rows(2 * b, 2, W)] = (rows_f[...] * scale).astype(BF)
        return carry

    lax.fori_loop(0, n_rows // 2, two_rows, 0)


def near_kernel(
    n_rows, n_cols,
    own_hbm, flow_hbm, targets_hbm, volume_hbm, code_hbm, joint_hbm, w_flow_hbm, bv_hbm, bc_hbm, bf_hbm, bj_hbm,
    mid, top, bot, head,
    out, own, flow, targets, w_code, bias, wv, wcb, wj, wjb, wf, wht,
    near, rows_f, wide, w_volume, w_joint, w_flow, sems,
):
    loads = (
        (own_hbm, own), (flow_hbm, flow), (targets_hbm, targets), (volume_hbm, w_volume), (code_hbm, w_code),
        (joint_hbm, w_joint), (w_flow_hbm, w_flow), (bv_hbm, bias.at[0]), (bc_hbm, bias.at[1]),
        (bf_hbm, bias.at[2]), (bj_hbm, bias.at[3]),
    )
    copies = [pltpu.make_async_copy(src, dst, sems.at[k]) for k, (src, dst) in enumerate(loads)]
    for copy in copies:
        copy.start()
    copies[0].wait()
    correlate(n_rows, n_cols, own, mid, top, bot, out, slice(None), near, rows_f)
    for copy in copies[1:]:
        copy.wait()
    C = w_code.shape[3]
    wide[...] = jnp.zeros_like(wide)
    weight = w_volume[...].astype(F32)
    for half in range(2):
        for dy in range(SIDE):
            at = half * OFF + dy * SIDE
            wide[half * HALF + 8 * dy : half * HALF + 8 * dy + 8, :] = weight[at : at + 8]
            wide[half * HALF + 72 + dy : half * HALF + 73 + dy, :] = weight[at + 8 : at + 9]
    wv[...] = wide[...].astype(BF)
    wide[...] = jnp.zeros_like(wide)
    for i in range(7):
        for j in range(7):
            wide[16 * i + 2 * j : 16 * i + 2 * j + 2, :] = w_flow[i, j].astype(F32)
    wf[...] = wide[0:112, :].astype(BF)
    for i in range(3):
        for j in range(3):
            at = (3 * i + j) * C
            wcb[:, at : at + C] = w_code[i, j]
            wjb[:, at : at + C] = w_joint[i, j]
            for part in range(2):
                at = (2 * i + part) * 3 * C + j * C
                wj[at : at + C, :] = w_joint[i, j, part * C : (part + 1) * C, :]
    wide[...] = jnp.zeros_like(wide)
    for k in range(3):
        wide[16 * k : 16 * k + 2, :] = head[...].astype(F32)
    wht[...] = wide[0:48, :].astype(BF)


def code_kernel(
    n_rows, n_cols,
    order, own, mid, top, bot, near_vol, wv, bias, flow, targets,
    vol, code, up, dn,
    near, rows_f, edge,
):
    W = n_cols
    halo = HALO * W
    body = n_rows * W
    near_second = (order[0] != lax.axis_index("tm") % 2).astype(jnp.int32)
    near_at = pl.multiple_of(near_second * HALF, HALF)
    far_at = pl.multiple_of((1 - near_second) * HALF, HALF)
    vol[pl.ds(near_at, HALF), :] = near_vol[...]
    correlate(n_rows, n_cols, own, mid, top, bot, vol, pl.ds(far_at, HALF), near, rows_f)

    def one_code(r, carry):
        at = rows(r, CODE_BLOCK, W)
        pre = lax.dot_general(vol[:, at], wv[...], TN, preferred_element_type=F32) + bias[0:1, :]
        code[at, :] = (pre * jax.nn.sigmoid(pre)).astype(BF)
        return carry

    lax.fori_loop(0, n_rows // CODE_BLOCK, lambda r, c: one_code(CODE_BLOCK * r, c), 0)
    for ref, at, flow_at, target_at in (
        (up, 0, 0, 0),
        (dn, body - halo, n_rows - FLOW_HALO, n_rows - TARGET_HALO),
    ):
        ref[0:halo, :] = code[at : at + halo, :]
        for k in range(2):
            edge[8 * k : 8 * k + FLOW_HALO, :] = flow[k].astype(F32)[flow_at : flow_at + FLOW_HALO]
            edge[8 * k + FLOW_HALO : 8 * k + 8, :] = targets[k].astype(F32)[target_at : target_at + TARGET_HALO]
        ref[halo : halo + 16, :] = edge[...].astype(BF)


def frame_scale(n_tm, per):
    frame = lax.axis_index("tm")
    value = jnp.float32(per)
    for t in range(n_tm - 1):
        value = jnp.where(frame == t, jnp.float32(per * 0.25 ** ((n_tm - 1 - t) / (n_tm - 1))), value)
    return value


def inside_frame(n_rows, ext):
    at = lax.axis_index("space") * n_rows + ext
    return jnp.logical_and(at >= 0, at < lax.axis_size("space") * n_rows)


def store_stack(ref, at, v, cols):
    W, C = v.shape
    x_at = lax.broadcasted_iota(jnp.int32, (W, C), 0)
    left = jnp.where(x_at == 0, 0.0, pltpu.roll(v, 1, 0))
    right = jnp.where(x_at == W - 1, 0.0, pltpu.roll(v, W - 1, 0))
    for col, part in zip(cols, (left, v, right)):
        ref[rows(at, 1, W), col * C : (col + 1) * C] = part.astype(BF)


FWD = (0, 1, 2)
BWD = (2, 1, 0)


def flow_kernel(n_rows, n_cols, top, bot, flow, targets, wf, bias, jf, d_flow, xb, tgt, xf, xx):
    W = n_cols
    halo = HALO * W
    xx[...] = jnp.zeros_like(xx)
    above = top[halo : halo + 16, :].astype(F32)
    below = bot[halo : halo + 16, :].astype(F32)
    n_flow = n_rows + 2 * FLOW_HALO
    lane = lax.broadcasted_iota(jnp.int32, (n_flow, W), 1)
    for k in range(2):
        xf[0:FLOW_HALO, :] = above[8 * k : 8 * k + FLOW_HALO, :]
        xf[FLOW_HALO : FLOW_HALO + n_rows, :] = flow[k].astype(F32)
        xf[FLOW_HALO + n_rows : n_flow, :] = below[8 * k : 8 * k + FLOW_HALO, :]
        own_flow = xf[0:n_flow, :]
        for j in range(7):
            shift = (3 - j) % W
            moved = pltpu.roll(own_flow, shift, 1) if shift else own_flow
            ok = jnp.logical_and(lane + (j - 3) >= 0, lane + (j - 3) < W)
            xx[pl.ds(j * 2 + k, n_flow, stride=16), :] = jnp.where(ok, moved, 0.0)
    xb[...] = xx[...].astype(BF)
    tgt[...] = jnp.zeros_like(tgt)
    for k in range(2):
        for y in range(TARGET_HALO):
            tgt[k : k + 1, y * W : (y + 1) * W] = above[8 * k + 6 + y : 8 * k + 7 + y, :]
            lo = (TARGET_HALO + n_rows + y) * W
            tgt[k : k + 1, lo : lo + W] = below[8 * k + 6 + y : 8 * k + 7 + y, :]
        for y in range(n_rows):
            lo = (TARGET_HALO + y) * W
            tgt[k : k + 1, lo : lo + W] = targets[k, y : y + 1, :].astype(F32)

    def flow_rows(b, carry):
        y = b * MOTION_BLOCK
        patches = [xb[pl.ds(pl.multiple_of((y + u) * 16, 16), 112), :] for u in range(MOTION_BLOCK)]
        pre = lax.dot_general(jnp.concatenate(patches, axis=1), wf[...], TN, preferred_element_type=F32)
        for u in range(MOTION_BLOCK):
            value, slope = silu_pair(pre[u * W : (u + 1) * W] + bias[2:3, :])
            d_flow[rows(y + u, 1, W), :] = slope
            store_stack(jf, y + u, jnp.where(inside_frame(n_rows, y + u - 3), value, 0.0), FWD)
        return carry

    lax.fori_loop(0, (n_rows + 6) // MOTION_BLOCK, flow_rows, 0)


def hidden_kernel(
    n_rows, n_cols, n_tm,
    b_head, code, top, bot, jf, tgt, wc, wj, wht, bias,
    error_out, jt, s3, d_motion, misc,
    c3, jm, err, hid, g_head, acc,
):
    W = n_cols
    count = 2.0 * n_tm * lax.axis_size("space") * n_rows * n_cols
    slope_scale = frame_scale(n_tm, 2.0 / count)
    C = wc.shape[1]
    body = n_rows * W

    def load_halo(y, carry):
        store_stack(c3, y, top[rows(y, 1, W), :].astype(F32), FWD)
        store_stack(c3, y + HALO + n_rows, bot[rows(y, 1, W), :].astype(F32), FWD)
        return carry

    def load_code(y, carry):
        store_stack(c3, y + HALO, code[rows(y, 1, W), :].astype(F32), FWD)
        return carry

    lax.fori_loop(0, HALO, load_halo, 0)
    lax.fori_loop(0, n_rows, load_code, 0)

    def motion_rows(b, carry):
        y = b * MOTION_BLOCK
        taps = jnp.concatenate([c3[rows(y + i, MOTION_BLOCK, W), :] for i in range(3)], axis=1)
        pre = dot(taps, wc[...]) + bias[1:2, :]
        for u in range(MOTION_BLOCK):
            value, slope = silu_pair(pre[u * W : (u + 1) * W])
            d_motion[rows(y + u, 1, W), :] = slope
            store_stack(jm, y + u, jnp.where(inside_frame(n_rows, y + u - 3), value, 0.0), FWD)
        return carry

    lax.fori_loop(0, (n_rows + 6) // MOTION_BLOCK, motion_rows, 0)

    block = HIDDEN_BLOCK
    k_row = lax.broadcasted_iota(jnp.int32, (16, block * W), 0)
    b_col = jnp.where(k_row == 0, b_head[0], jnp.where(k_row == 1, b_head[1], 0.0))

    def hidden_rows(b, carry):
        y = b * block
        taps = [ref[rows(y + i, block, W), :] for i in range(3) for ref in (jm, jf)]
        pre = dot(jnp.concatenate(taps, axis=1), wj[...]) + bias[3:4, :]
        value, slope = silu_pair(pre)
        hidden = value.astype(BF)
        hid[rows(y, block, W), :] = hidden
        pred = lax.dot_general(wht[0:16, :], hidden, NT, preferred_element_type=F32)
        error = pred + b_col - tgt[:, rows(y, block, W)]
        err[:, rows(y, block, W)] = error
        back = lax.dot_general(split3(error * slope_scale), wht[...], TN, preferred_element_type=F32) * slope
        for u in range(block):
            v = jnp.where(inside_frame(n_rows, y + u - 2), back[u * W : (u + 1) * W], 0.0)
            store_stack(s3, y + u, v, BWD)
        return carry

    lax.fori_loop(0, (n_rows + 4) // block, hidden_rows, 0)

    acc[...] = jnp.zeros_like(acc)
    g_head[...] = jnp.zeros_like(g_head)

    def own_rows(b, carry):
        y = 2 * b
        g_head[...] += dot(split3(err[:, rows(y + 2, 2, W)] * slope_scale), hid[rows(y + 2, 2, W), :])
        part = s3[rows(y + 2, 2, W), C : 2 * C].astype(F32)
        acc[...] += jnp.sum(part.reshape(2 * W // 8, 8, C), axis=0)
        jt[0:C, rows(y, 2, W)] = jm[rows(y + 3, 2, W), C : 2 * C].T
        jt[C : 2 * C, rows(y, 2, W)] = jf[rows(y + 3, 2, W), C : 2 * C].T
        return carry

    lax.fori_loop(0, n_rows // 2, own_rows, 0)
    own = err[:, TARGET_HALO * W : TARGET_HALO * W + body]
    for k in range(2):
        for y in range(n_rows):
            error_out[k, y : y + 1, :] = own[k : k + 1, y * W : (y + 1) * W]
    g_b_head = jnp.sum(own * slope_scale, axis=1, keepdims=True)
    loss = jnp.sum(jnp.sum(own * own, axis=1, keepdims=True), axis=0, keepdims=True)
    loss = loss * frame_scale(n_tm, 1.0 / count)
    col = lax.broadcasted_iota(jnp.int32, (1, C), 1)
    tail = jnp.where(col == 0, loss, jnp.where(col == 1, g_b_head[0:1], jnp.where(col == 2, g_b_head[1:2], 0.0)))
    misc[0:3, :] = jnp.zeros((3, C), F32)
    misc[3:4, :] = jnp.sum(acc[...], axis=0, keepdims=True)
    misc[4:6, :] = g_head[0:2, :] + g_head[16:18, :] + g_head[32:34, :]
    misc[6:7, :] = tail
    misc[7:8, :] = jnp.zeros((1, C), F32)


def rest_kernel(
    n_rows, n_cols, at_misc,
    jt, s3, d_motion, d_flow, xb, vol, code, misc, wv, wcb, wjb, bias,
    keep, send,
    m3, s_flow, s_code, acc, grads,
):
    W = n_cols
    C = code.shape[1]
    body = n_rows * W

    def joint_slopes(b, carry):
        y = b * SLOPE_BLOCK
        taps = jnp.concatenate([s3[rows(y + 2 - i, SLOPE_BLOCK, W), :] for i in range(3)], axis=1)
        sj = dot_nt(taps, wjb[...])
        for u in range(SLOPE_BLOCK):
            part = sj[u * W : (u + 1) * W]
            v = part[:, 0:C] * d_motion[rows(y + u + 2, 1, W), :]
            store_stack(m3, y + u, jnp.where(inside_frame(n_rows, y + u - 1), v, 0.0), BWD)
            s_flow[rows(y + u, 1, W), :] = (part[:, C:] * d_flow[rows(y + u + 2, 1, W), :]).astype(BF)
        return carry

    lax.fori_loop(0, (n_rows + 2) // SLOPE_BLOCK, joint_slopes, 0)
    acc[...] = jnp.zeros_like(acc)

    def add_rows(k, v):
        acc[8 * k : 8 * k + 8, :] += jnp.sum(v.reshape(v.shape[0] // 8, 8, C), axis=0)

    def code_slopes(b, carry):
        y = b * CODE_BLOCK
        at = rows(y, CODE_BLOCK, W)
        taps = jnp.concatenate([m3[rows(y + 2 - i, CODE_BLOCK, W), :] for i in range(3)], axis=1)
        sc = dot_nt(taps, wcb[...])
        pre = lax.dot_general(vol[:, at], wv[...], TN, preferred_element_type=F32) + bias[0:1, :]
        slope = (sc * silu_pair(pre)[1]).astype(BF)
        s_code[at, :] = slope
        add_rows(0, slope.astype(F32))
        add_rows(1, m3[rows(y + 1, CODE_BLOCK, W), C : 2 * C].astype(F32))
        add_rows(2, s_flow[rows(y + 1, CODE_BLOCK, W), :].astype(F32))
        return carry

    lax.fori_loop(0, n_rows // CODE_BLOCK, code_slopes, 0)

    for i in range(3):
        g = dot(jt[...], s3[(3 - i) * W : (3 - i) * W + body, :])
        for j in range(3):
            at = (i * 3 + j) * 2 * C
            grads[at : at + 2 * C, :] = g[:, j * C : (j + 1) * C]
    code_t = code[...].T
    for i in range(3):
        g = dot(code_t, m3[(2 - i) * W : (2 - i) * W + body, :])
        for j in range(3):
            at = AT_CODE + (i * 3 + j) * C
            grads[at : at + C, :] = g[:, j * C : (j + 1) * C]
    grads[AT_VOLUME:AT_FLOW, :] = dot(vol[...], s_code[...])
    gf = jnp.zeros((112, C), F32)
    for y in range(n_rows):
        gf = gf + dot(xb[(y + 3) * 16 : (y + 3) * 16 + 112, :], s_flow[(y + 1) * W : (y + 2) * W, :])
    grads[AT_FLOW : AT_FLOW + 112, :] = gf
    if at_misc > AT_END:
        grads[AT_END:at_misc, :] = jnp.zeros((at_misc - AT_END, C), F32)
    for k in range(3):
        grads[at_misc + k : at_misc + k + 1, :] = jnp.sum(acc[8 * k : 8 * k + 8, :], axis=0, keepdims=True)
    grads[at_misc + 3 : at_misc + 8, :] = misc[3:8, :]
    grads[at_misc + 8 :, :] = jnp.zeros((grads.shape[0] - at_misc - 8, C), F32)
    half = keep.shape[0]
    core = lax.axis_index("tm") % 2
    keep[...] = pick(grads, core, half)
    send[...] = pick(grads, 1 - core, half)


VMEM = pl.BlockSpec(memory_space=pltpu.VMEM)
SMEM = pl.BlockSpec(memory_space=pltpu.SMEM)
HBM = pl.BlockSpec(memory_space=pltpu.HBM)


def bits_of(axis):
    bits = []
    bit = 1
    while bit < lax.axis_size(axis):
        bits.append((axis, bit))
        bit *= 2
    return bits


def trade(x, axis, bit):
    return lax.ppermute(x, axis, [(i, i ^ bit) for i in range(lax.axis_size(axis))])


def upper_of(axis, bit):
    return (lax.axis_index(axis) // bit) % 2


def three_terms(x, at, is_last):
    value = x[at : at + MISC_ROWS]
    mid = value - lax.reduce_precision(value, 8, 7)
    low = mid - lax.reduce_precision(mid, 8, 7)
    terms = jnp.concatenate([x[: at + MISC_ROWS], mid, low, x[at + 3 * MISC_ROWS :]])
    return jnp.where(is_last, terms, x).astype(BF)


def halving_reduce(x, steps, is_last):
    for axis, bit in steps:
        upper = upper_of(axis, bit)
        is_last = is_last * upper
        half = x.shape[0] // 2
        mine = lax.dynamic_slice_in_dim(x, upper * half, half, 0)
        other = lax.dynamic_slice_in_dim(x, (1 - upper) * half, half, 0)
        x = mine + trade(other, axis, bit)
    x = three_terms(x, 0, is_last == 1)
    for axis, bit in steps[::-1]:
        got = trade(x, axis, bit)
        x = jnp.where(upper_of(axis, bit) == 0, jnp.concatenate([x, got]), jnp.concatenate([got, x]))
    return x


def pick(ref, which, half):
    return ref[pl.ds(pl.multiple_of(which * half, 8), half), :]


def first_split(at, bits, keep, got, a_keep, a_send, b_keep, b_send, total):
    quarter = a_keep.shape[0]
    total[...] = keep[...] + got[...]
    for part, (k, s, bit) in enumerate(((a_keep, a_send, bits[1]), (b_keep, b_send, bits[2]))):
        k[...] = total[pl.ds(pl.multiple_of((2 * part + bit) * quarter, 8), quarter), :]
        s[...] = total[pl.ds(pl.multiple_of((2 * part + 1 - bit) * quarter, 8), quarter), :].astype(s.dtype)
    @pl.when(jnp.logical_and(bits[0] == 1, bits[2] == 0))
    def _():
        value = total[3 * quarter + at : 3 * quarter + at + MISC_ROWS, :]
        b_send[at : at + 4 * MISC_ROWS, :] = split3(value, True)


def second_split(at, bits, a_keep, a_got, b_keep, b_got, a_mine, a_send, b_mine, b_send, total):
    half = a_mine.shape[0]
    for is_b, (keep, got, mine, send, bit) in enumerate((
        (a_keep, a_got, a_mine, a_send, bits[2]),
        (b_keep, b_got, b_mine, b_send, bits[1]),
    )):
        total[...] = keep[...] + got[...].astype(F32)
        if is_b:

            @pl.when(jnp.logical_and(bits[0] == 1, bits[2] == 1))
            def _():
                terms = got[at : at + 4 * MISC_ROWS, :].astype(F32)
                value = keep[at : at + MISC_ROWS, :]
                for k in range(3):
                    value = value + terms[k * MISC_ROWS : (k + 1) * MISC_ROWS]
                total[at : at + MISC_ROWS, :] = value
                total[at + MISC_ROWS : at + 4 * MISC_ROWS, :] = jnp.zeros((3 * MISC_ROWS, value.shape[1]), F32)

        mine[...] = pick(total, bit, half)
        send[...] = pick(total, 1 - bit, half)


def third_split(bits, a_keep, a_got, b_keep, b_got, keep, send, total):
    n = a_keep.shape[0]
    total[0:n, :] = a_keep[...] + a_got[...]
    total[n : 2 * n, :] = b_keep[...] + b_got[...]
    keep[...] = pick(total, bits[3], n)
    send[...] = pick(total, 1 - bits[3], n)


def last_sum(at, bits, keep, got, out, total):
    total[...] = keep[...] + got[...]
    value = total[at : at + MISC_ROWS, :]
    mid = value - value.astype(BF).astype(F32)
    low = mid - mid.astype(BF).astype(F32)
    is_last = bits[0] + bits[1] + bits[2] + bits[3] == 4
    total[at + MISC_ROWS : at + 2 * MISC_ROWS, :] = jnp.where(is_last, mid, total[at + MISC_ROWS : at + 2 * MISC_ROWS, :])
    total[at + 2 * MISC_ROWS : at + 3 * MISC_ROWS, :] = jnp.where(
        is_last, low, total[at + 2 * MISC_ROWS : at + 3 * MISC_ROWS, :]
    )
    out[...] = total[...].astype(BF)


def first_merge(bits, mine, got, a_out, b_out):
    first = bits[3] == 0
    a_out[...] = jnp.where(first, mine[...], got[...])
    b_out[...] = jnp.where(first, got[...], mine[...])


def pair_merge(x_first, bits, a_mine, a_got, b_mine, b_got, a_out, b_out):
    n = a_mine.shape[0]
    a_bit, b_bit = (bits[1], bits[2]) if x_first else (bits[2], bits[1])
    for mine, got, out, bit in ((a_mine, a_got, a_out, a_bit), (b_mine, b_got, b_out, b_bit)):
        out[pl.ds(pl.multiple_of(bit * n, 16), n), :] = mine[...]
        out[pl.ds(pl.multiple_of((1 - bit) * n, 16), n), :] = got[...]


def join_merge(bits, a_mine, a_got, b_mine, b_got, out):
    n = a_mine.shape[0]
    for at, (mine, got, bit) in enumerate(((a_mine, a_got, bits[1]), (b_mine, b_got, bits[2]))):
        out[pl.ds(pl.multiple_of((2 * at + bit) * n, 16), n), :] = mine[...]
        out[pl.ds(pl.multiple_of((2 * at + 1 - bit) * n, 16), n), :] = got[...]


def paired_reduce(bits, keep, got, at_misc, shape):
    half, C = keep.shape
    x, z, far_z = ("tm", 2), ("space", 1), ("space", 2)

    def stage(body, name, dtypes, n, scratch, *args):
        out = tuple(shape(n, C, dtype=dtype) for dtype in dtypes)
        return call(
            body, name, out, [SMEM] + [VMEM] * len(args),
            [pltpu.VMEM((scratch, C), F32)] if scratch else [], 10_000_000, bits, *args,
        )

    first_at = at_misc - 2 * half + half // 4
    ak, as_, bk, bs = stage(functools.partial(first_split, first_at), "split1", (F32, BF, F32, BF), half // 4, half, keep, got)
    ag, bg = trade(as_, *x), trade(bs, *z)
    ak, as_, bk, bs = stage(functools.partial(second_split, first_at), "split2", (F32,) * 4, half // 8, half // 4, ak, ag, bk, bg)
    ag, bg = trade(as_, *z), trade(bs, *x)
    keep, send = stage(third_split, "split3", (F32, F32), half // 8, half // 4, ak, ag, bk, bg)
    got = trade(send, *far_z)
    chunk = half // 8
    (y,) = stage(
        functools.partial(last_sum, at_misc - (2 * half - chunk)), "last", (BF,), chunk, chunk, keep, got
    )
    a, b = stage(first_merge, "merge1", (BF, BF), chunk, 0, y, trade(y, *far_z))
    a, b = stage(
        functools.partial(pair_merge, False), "merge2", (BF, BF), half // 4, 0, a, trade(a, *z), b, trade(b, *x)
    )
    (out,) = stage(join_merge, "merge3", (BF,), half, 0, a, trade(a, *x), b, trade(b, *z))
    return out


def finish_kernel(
    at_misc,
    bits, mine, other,
    joint, code, volume, flow, b_volume, b_code, b_flow, b_joint, head, loss, b_head,
    full,
):
    half, C = mine.shape
    full[pl.ds(pl.multiple_of(bits[0] * half, 16), half), :] = mine[...]
    full[pl.ds(pl.multiple_of((1 - bits[0]) * half, 16), half), :] = other[...]
    for i in range(3):
        for j in range(3):
            at = (i * 3 + j) * 2 * C
            joint[i, j, :, :] = full[at : at + 2 * C, :].astype(F32)
            at = AT_CODE + (i * 3 + j) * C
            code[i, j, :, :] = full[at : at + C, :].astype(F32)
    parts = full[AT_VOLUME:AT_FLOW, :].astype(F32)
    for half_at in range(2):
        for dy in range(SIDE):
            at, to = half_at * HALF, half_at * OFF + dy * SIDE
            volume[to : to + 8, :] = parts[at + 8 * dy : at + 8 * dy + 8]
            volume[to + 8 : to + 9, :] = parts[at + 72 + dy : at + 73 + dy]
    for i in range(7):
        part = full[AT_FLOW + 16 * i : AT_FLOW + 16 * i + 16, :].astype(F32)
        for j in range(7):
            flow[i, j, :, :] = part[2 * j : 2 * j + 2]
    terms = full[at_misc : at_misc + 32, :].astype(F32)
    misc = terms[0:8] + terms[8:16] + terms[16:24]
    for k, ref in enumerate((b_volume, b_code, b_flow, b_joint)):
        ref[...] = misc[k]
    head[...] = misc[4:6]
    lane = lax.broadcasted_iota(jnp.int32, (1, C), 1)
    loss[0] = jnp.sum(jnp.where(lane == 0, misc[6:7], 0.0))
    b_head[0] = jnp.sum(jnp.where(lane == 1, misc[6:7], 0.0))
    b_head[1] = jnp.sum(jnp.where(lane == 2, misc[6:7], 0.0))


def call(body, name, out_shape, in_specs, scratch, flops, *args, out_specs=None):
    held = [
        x if spec is SMEM else pltpu.with_memory_space_constraint(x, spec.memory_space)
        for x, spec in zip(args, in_specs, strict=True)
    ]
    return pl.pallas_call(
        body,
        out_shape=out_shape,
        in_specs=in_specs,
        out_specs=out_specs or jax.tree.map(lambda _: VMEM, out_shape),
        scratch_shapes=scratch,
        cost_estimate=pl.CostEstimate(flops=flops, bytes_accessed=flops // 300, transcendentals=0),
        compiler_params=pltpu.CompilerParams(vmem_limit_bytes=16 << 20),
        name=name,
    )(*held)


def local(
    features, pair_order, flow_now, targets, w_volume, b_volume, w_code, b_code,
    w_flow, b_flow, w_joint, b_joint, w_head, b_head,
):
    own = features[0]
    n_rows, n_cols, n_chan = own.shape
    n_code = w_code.shape[3]
    W, C = n_cols, n_code
    body = n_rows * n_cols
    halo = HALO * n_cols
    n_tm, n_space = lax.axis_size("tm"), lax.axis_size("space")
    flat = own.reshape(body, n_chan)
    both = ("tm", "space")

    def route(partner, ds):
        pairs = []
        for t in range(n_tm):
            for s in range(n_space):
                if 0 <= partner(t) < n_tm and 0 <= s + ds < n_space:
                    pairs.append((t * n_space + s, partner(t) * n_space + s + ds))
        return pairs

    def near(t):
        return t + 1 - 2 * (t % 2)

    def far(t):
        return t - 1 + 2 * (t % 2)

    first, last = flat[:halo], flat[body - halo :]
    near_top = lax.ppermute(last, both, route(near, 1))
    near_bot = lax.ppermute(first, both, route(near, -1))
    near_mid = lax.ppermute(flat, both, route(near, 0))
    far_top = lax.ppermute(last, both, route(far, 1))
    far_bot = lax.ppermute(first, both, route(far, -1))
    far_mid = lax.ppermute(flat, both, route(far, 0))

    def shape(*dims, dtype=BF):
        return pltpu.VMEM(dims, dtype)

    def result(*dims):
        return jax.ShapeDtypeStruct(dims, F32)

    near_vol, held, flow, held_targets, wc, bias, wv, wcb, wj, wjb, wf, wht = call(
        functools.partial(near_kernel, n_rows, n_cols), "near",
        (
            shape(HALF, body), shape(body, n_chan), shape(*flow_now.shape[1:]),
            shape(*targets.shape[1:], dtype=jnp.int32), shape(3, 3, C, C), shape(4, C, dtype=F32),
            shape(2 * HALF, C), shape(C, 9 * C), shape(18 * C, C),
            shape(2 * C, 9 * C), shape(112, C), shape(48, C),
        ),
        [HBM] * 11 + [VMEM] * 4,
        [
            pltpu.VMEM((body + 2 * halo, n_chan), BF),
            pltpu.VMEM((HALF, 2 * W), F32),
            pltpu.VMEM((2 * HALF, C), F32),
            pltpu.VMEM(w_volume.shape, BF),
            pltpu.VMEM(w_joint.shape, BF),
            pltpu.VMEM(w_flow.shape, BF),
            pltpu.SemaphoreType.DMA((11,)),
        ],
        4_000_000_000,
        flat, flow_now[0], targets[0], w_volume, w_code, w_joint, w_flow, b_volume, b_code, b_flow, b_joint,
        near_mid, near_top, near_bot, w_head.T,
    )
    vol, code, up, dn = call(
        functools.partial(code_kernel, n_rows, n_cols), "code",
        (shape(2 * HALF, body), shape(body, C), shape(halo + 16, C), shape(halo + 16, C)),
        [SMEM] + [VMEM] * 9,
        [
            pltpu.VMEM((body + 2 * halo, n_chan), BF),
            pltpu.VMEM((HALF, 2 * W), F32),
            pltpu.VMEM((16, W), F32),
        ],
        4_000_000_000,
        pair_order, held, far_mid, far_top, far_bot, near_vol, wv, bias, flow, held_targets,
    )
    top = lax.ppermute(dn, "space", [(s, s + 1) for s in range(n_space - 1)])
    bot = lax.ppermute(up, "space", [(s + 1, s) for s in range(n_space - 1)])

    jf, d_flow, xb, tgt = call(
        functools.partial(flow_kernel, n_rows, n_cols), "flow",
        (
            shape((n_rows + 6) * W, 3 * C),
            shape((n_rows + 6) * W, C, dtype=F32),
            shape((n_rows + 12) * 16, W),
            shape(16, (n_rows + 4) * W, dtype=F32),
        ),
        [VMEM] * 6,
        [
            pltpu.VMEM((24, W), F32),
            pltpu.VMEM(((n_rows + 12) * 16, W), F32),
        ],
        1_000_000_000,
        top, bot, flow, held_targets, wf, bias,
    )
    flow_error, jt, s3, d_motion, misc = call(
        functools.partial(hidden_kernel, n_rows, n_cols, n_tm), "hidden",
        (
            result(2, n_rows, W),
            shape(2 * C, body),
            shape((n_rows + 4) * W, 3 * C),
            shape((n_rows + 6) * W, C, dtype=F32),
            shape(MISC_ROWS, C, dtype=F32),
        ),
        [SMEM] + [VMEM] * 9,
        [
            pltpu.VMEM(((n_rows + 8) * W, 3 * C), BF),
            pltpu.VMEM(((n_rows + 6) * W, 3 * C), BF),
            pltpu.VMEM((16, (n_rows + 4) * W), F32),
            pltpu.VMEM(((n_rows + 4) * W, C), BF),
            pltpu.VMEM((48, C), F32),
            pltpu.VMEM((8, C), F32),
        ],
        4_000_000_000,
        b_head, code, top, bot, jf, tgt, wc.reshape(9 * C, C), wj, wht, bias,
    )
    n_dev = n_tm * n_space
    paired = n_tm == 4 and n_space == 4
    if paired:
        grad_rows, at_misc = 3840, AT_END
    else:
        chunk = -(-max(pl.cdiv(AT_END, n_dev - 1), 3 * MISC_ROWS) // 16) * 16
        grad_rows, at_misc = n_dev * chunk, (n_dev - 1) * chunk
    keep, send = call(
        functools.partial(rest_kernel, n_rows, n_cols, at_misc), "rest",
        (shape(grad_rows // 2, C, dtype=F32), shape(grad_rows // 2, C, dtype=F32)),
        [VMEM] * 12,
        [
            pltpu.VMEM(((n_rows + 2) * W, 3 * C), BF),
            pltpu.VMEM(((n_rows + 2) * W, C), BF),
            pltpu.VMEM((body, C), BF),
            pltpu.VMEM((24, C), F32),
            pltpu.VMEM((grad_rows, C), F32),
        ],
        3_000_000_000,
        jt, s3, d_motion, d_flow, xb, vol, code, misc, wv, wcb, wjb, bias,
    )
    core = ("tm", 1)
    got = trade(send, *core)
    bits = jnp.stack([upper_of("tm", 1), upper_of("tm", 2), upper_of("space", 1), upper_of("space", 2)])
    bits = bits.astype(jnp.int32)
    if paired:
        mine = paired_reduce(bits, keep, got, at_misc, shape)
    else:
        mine = halving_reduce(keep + got, bits_of("tm")[1:] + bits_of("space"), upper_of(*core))
    other = trade(mine, *core)
    outs = call(
        functools.partial(finish_kernel, at_misc), "finish",
        (
            result(3, 3, 2 * C, C),
            result(3, 3, C, C),
            result(2 * OFF, C),
            result(7, 7, 2, C),
            result(C), result(C), result(C), result(C),
            result(2, C), result(1), result(2),
        ),
        [SMEM] + [VMEM] * 2, [pltpu.VMEM((grad_rows, C), BF)], 100_000_000,
        bits, mine, other,
        out_specs=(VMEM,) * 9 + (SMEM,) * 2,
    )
    joint, g_code, g_volume, g_flow, g_bv, g_bc, g_bf, g_bj, head, loss, g_b_head = outs
    return loss, flow_error[None], g_volume, g_bv, g_code, g_bc, g_flow, g_bf, joint, g_bj, head.T, g_b_head


def solution(mesh):
    placed = (
        P(("groups", "tm"), "space", None, None),
        P(("groups", "tm")),
        P(("groups", "tm"), None, "space", None),
        P(("groups", "tm"), None, "space", None),
    ) + (P(),) * 10
    return jax.shard_map(
        local,
        mesh=mesh,
        in_specs=placed,
        out_specs=(
            P("groups"),
            P(("groups", "tm"), None, "space", None),
            P("groups", None),
            P("groups"),
            P("groups", None, None, None),
            P("groups"),
            P("groups", None, None, None),
            P("groups"),
            P("groups", None, None, None),
            P("groups"),
            P("groups", None),
            P("groups"),
        ),
        check_vma=False,
    )
```

```python
import functools

import jax
import jax.numpy as jnp
from jax import lax
from jax.experimental import pallas as pl
from jax.experimental.pallas import tpu as pltpu
from jax.sharding import PartitionSpec as P

BF = jnp.bfloat16
F32 = jnp.float32
RADIUS = 4
SIDE = 2 * RADIUS + 1
OFF = SIDE * SIDE
HALO = 4
FLOW_HALO = 6
TARGET_HALO = 2
NT = (((1,), (1,)), ((), ()))
TN = (((0,), (0,)), ((), ()))

AT_CODE = 2304
AT_VOLUME = 3456
AT_FLOW = 3648
AT_END = 3760
HALF = 96
MOTION_BLOCK = 7
HIDDEN_BLOCK = 12
SLOPE_BLOCK = 10
CODE_BLOCK = 4
MISC_ROWS = 8


def dot(a, b):
    return jnp.dot(a, b, preferred_element_type=F32)


def dot_nt(a, b):
    return lax.dot_general(a, b, NT, preferred_element_type=F32)


def rows(start, count, unit):
    return pl.ds(pl.multiple_of(start * unit, unit), count * unit)


def split3(s, padded=False):
    hi = s.astype(BF).astype(F32)
    mid = (s - hi).astype(BF).astype(F32)
    terms = [hi, mid, s - hi - mid] + [jnp.zeros_like(s)] * padded
    return jnp.concatenate(terms, axis=0).astype(BF)


def silu_pair(v):
    s = jax.nn.sigmoid(v)
    return v * s, s * (1.0 + v * (1.0 - s))


def correlate(n_rows, n_cols, own, mid, top, bot, out, out_at, near, rows_f):
    n_chan = own.shape[1]
    halo = RADIUS * n_cols
    body = n_rows * n_cols
    near[0:halo, :] = top[...]
    near[halo : halo + body, :] = mid[...]
    near[halo + body :, :] = bot[...]
    W = n_cols
    j_at = lax.broadcasted_iota(jnp.int32, (W, 2 * W), 0)
    x_at = lax.broadcasted_iota(jnp.int32, (W, 2 * W), 1) & (W - 1)
    band = jnp.logical_and(j_at - x_at >= -RADIUS, j_at - x_at < RADIUS)
    edge = j_at - x_at == RADIUS
    turn = lax.broadcasted_iota(jnp.int32, (8, 2 * W), 1) + RADIUS
    scale = n_chan ** (-0.5)

    def fold(v):
        parts = [v[8 * g : 8 * g + 8] for g in range(W // 8)]
        while len(parts) > 1:
            parts = [parts[k] + parts[k + 1] for k in range(0, len(parts), 2)]
        return parts[0]

    def two_rows(b, carry):
        tile = own[rows(2 * b, 2, W), :]
        rows_f[...] = jnp.zeros_like(rows_f)
        for q in range(SIDE + 1):
            scores = lax.dot_general(
                near[rows(2 * b + q, 1, W), :], tile, NT, preferred_element_type=F32
            )
            inner = fold(jnp.where(band, scores, 0.0))
            outer = jnp.sum(fold(jnp.where(edge, scores, 0.0)), axis=0, keepdims=True)
            for bit in (1, 2, 4):
                inner = jnp.where((turn & bit) != 0, pltpu.roll(inner, 8 - bit, 0), inner)
            for u in range(2):
                dy = q - u
                if 0 <= dy < SIDE:
                    rows_f[8 * dy : 8 * dy + 8, u * W : (u + 1) * W] = inner[:, u * W : (u + 1) * W]
                    rows_f[72 + dy : 73 + dy, u * W : (u + 1) * W] = outer[:, u * W : (u + 1) * W]
        out[out_at, rows(2 * b, 2, W)] = (rows_f[...] * scale).astype(BF)
        return carry

    lax.fori_loop(0, n_rows // 2, two_rows, 0)


def near_kernel(
    n_rows, n_cols,
    own_hbm, flow_hbm, targets_hbm, volume_hbm, code_hbm, joint_hbm, w_flow_hbm, bv_hbm, bc_hbm, bf_hbm, bj_hbm,
    mid, top, bot, head,
    out, own, flow, targets, w_code, bias, wv, wcb, wj, wjb, wf, wht,
    near, rows_f, wide, w_volume, w_joint, w_flow, sems,
):
    loads = (
        (own_hbm, own), (flow_hbm, flow), (targets_hbm, targets), (volume_hbm, w_volume), (code_hbm, w_code),
        (joint_hbm, w_joint), (w_flow_hbm, w_flow), (bv_hbm, bias.at[0]), (bc_hbm, bias.at[1]),
        (bf_hbm, bias.at[2]), (bj_hbm, bias.at[3]),
    )
    copies = [pltpu.make_async_copy(src, dst, sems.at[k]) for k, (src, dst) in enumerate(loads)]
    for copy in copies:
        copy.start()
    copies[0].wait()
    correlate(n_rows, n_cols, own, mid, top, bot, out, slice(None), near, rows_f)
    for copy in copies[1:]:
        copy.wait()
    C = w_code.shape[3]
    wide[...] = jnp.zeros_like(wide)
    weight = w_volume[...].astype(F32)
    for half in range(2):
        for dy in range(SIDE):
            at = half * OFF + dy * SIDE
            wide[half * HALF + 8 * dy : half * HALF + 8 * dy + 8, :] = weight[at : at + 8]
            wide[half * HALF + 72 + dy : half * HALF + 73 + dy, :] = weight[at + 8 : at + 9]
    wv[...] = wide[...].astype(BF)
    wide[...] = jnp.zeros_like(wide)
    for i in range(7):
        for j in range(7):
            wide[16 * i + 2 * j : 16 * i + 2 * j + 2, :] = w_flow[i, j].astype(F32)
    wf[...] = wide[0:112, :].astype(BF)
    for i in range(3):
        for j in range(3):
            at = (3 * i + j) * C
            wcb[:, at : at + C] = w_code[i, j]
            wjb[:, at : at + C] = w_joint[i, j]
            for part in range(2):
                at = (2 * i + part) * 3 * C + j * C
                wj[at : at + C, :] = w_joint[i, j, part * C : (part + 1) * C, :]
    wide[...] = jnp.zeros_like(wide)
    for k in range(3):
        wide[16 * k : 16 * k + 2, :] = head[...].astype(F32)
    wht[...] = wide[0:48, :].astype(BF)


def code_kernel(
    n_rows, n_cols,
    order, own, mid, top, bot, near_vol, wv, bias, flow, targets,
    vol, code, up, dn,
    near, rows_f, edge,
):
    W = n_cols
    halo = HALO * W
    body = n_rows * W
    near_second = (order[0] != lax.axis_index("tm") % 2).astype(jnp.int32)
    near_at = pl.multiple_of(near_second * HALF, HALF)
    far_at = pl.multiple_of((1 - near_second) * HALF, HALF)
    vol[pl.ds(near_at, HALF), :] = near_vol[...]
    correlate(n_rows, n_cols, own, mid, top, bot, vol, pl.ds(far_at, HALF), near, rows_f)

    def one_code(r, carry):
        at = rows(r, CODE_BLOCK, W)
        pre = lax.dot_general(vol[:, at], wv[...], TN, preferred_element_type=F32) + bias[0:1, :]
        code[at, :] = (pre * jax.nn.sigmoid(pre)).astype(BF)
        return carry

    lax.fori_loop(0, n_rows // CODE_BLOCK, lambda r, c: one_code(CODE_BLOCK * r, c), 0)
    for ref, at, flow_at, target_at in (
        (up, 0, 0, 0),
        (dn, body - halo, n_rows - FLOW_HALO, n_rows - TARGET_HALO),
    ):
        ref[0:halo, :] = code[at : at + halo, :]
        for k in range(2):
            edge[8 * k : 8 * k + FLOW_HALO, :] = flow[k].astype(F32)[flow_at : flow_at + FLOW_HALO]
            edge[8 * k + FLOW_HALO : 8 * k + 8, :] = targets[k].astype(F32)[target_at : target_at + TARGET_HALO]
        ref[halo : halo + 16, :] = edge[...].astype(BF)


def frame_scale(n_tm, per):
    frame = lax.axis_index("tm")
    value = jnp.float32(per)
    for t in range(n_tm - 1):
        value = jnp.where(frame == t, jnp.float32(per * 0.25 ** ((n_tm - 1 - t) / (n_tm - 1))), value)
    return value


def inside_frame(n_rows, ext):
    at = lax.axis_index("space") * n_rows + ext
    return jnp.logical_and(at >= 0, at < lax.axis_size("space") * n_rows)


def store_stack(ref, at, v, cols):
    W, C = v.shape
    x_at = lax.broadcasted_iota(jnp.int32, (W, C), 0)
    left = jnp.where(x_at == 0, 0.0, pltpu.roll(v, 1, 0))
    right = jnp.where(x_at == W - 1, 0.0, pltpu.roll(v, W - 1, 0))
    for col, part in zip(cols, (left, v, right)):
        ref[rows(at, 1, W), col * C : (col + 1) * C] = part.astype(BF)


FWD = (0, 1, 2)
BWD = (2, 1, 0)


def flow_kernel(n_rows, n_cols, top, bot, flow, targets, wf, bias, jf, d_flow, xb, tgt, xf, xx):
    W = n_cols
    halo = HALO * W
    xx[...] = jnp.zeros_like(xx)
    above = top[halo : halo + 16, :].astype(F32)
    below = bot[halo : halo + 16, :].astype(F32)
    n_flow = n_rows + 2 * FLOW_HALO
    lane = lax.broadcasted_iota(jnp.int32, (n_flow, W), 1)
    for k in range(2):
        xf[0:FLOW_HALO, :] = above[8 * k : 8 * k + FLOW_HALO, :]
        xf[FLOW_HALO : FLOW_HALO + n_rows, :] = flow[k].astype(F32)
        xf[FLOW_HALO + n_rows : n_flow, :] = below[8 * k : 8 * k + FLOW_HALO, :]
        own_flow = xf[0:n_flow, :]
        for j in range(7):
            shift = (3 - j) % W
            moved = pltpu.roll(own_flow, shift, 1) if shift else own_flow
            ok = jnp.logical_and(lane + (j - 3) >= 0, lane + (j - 3) < W)
            xx[pl.ds(j * 2 + k, n_flow, stride=16), :] = jnp.where(ok, moved, 0.0)
    xb[...] = xx[...].astype(BF)
    tgt[...] = jnp.zeros_like(tgt)
    for k in range(2):
        for y in range(TARGET_HALO):
            tgt[k : k + 1, y * W : (y + 1) * W] = above[8 * k + 6 + y : 8 * k + 7 + y, :]
            lo = (TARGET_HALO + n_rows + y) * W
            tgt[k : k + 1, lo : lo + W] = below[8 * k + 6 + y : 8 * k + 7 + y, :]
        for y in range(n_rows):
            lo = (TARGET_HALO + y) * W
            tgt[k : k + 1, lo : lo + W] = targets[k, y : y + 1, :].astype(F32)

    def flow_rows(b, carry):
        y = b * MOTION_BLOCK
        patches = [xb[pl.ds(pl.multiple_of((y + u) * 16, 16), 112), :] for u in range(MOTION_BLOCK)]
        pre = lax.dot_general(jnp.concatenate(patches, axis=1), wf[...], TN, preferred_element_type=F32)
        for u in range(MOTION_BLOCK):
            value, slope = silu_pair(pre[u * W : (u + 1) * W] + bias[2:3, :])
            d_flow[rows(y + u, 1, W), :] = slope
            store_stack(jf, y + u, jnp.where(inside_frame(n_rows, y + u - 3), value, 0.0), FWD)
        return carry

    lax.fori_loop(0, (n_rows + 6) // MOTION_BLOCK, flow_rows, 0)


def hidden_kernel(
    n_rows, n_cols, n_tm,
    b_head, code, top, bot, jf, tgt, wc, wj, wht, bias,
    error_out, jt, s3, d_motion, misc,
    c3, jm, err, hid, g_head, acc,
):
    W = n_cols
    count = 2.0 * n_tm * lax.axis_size("space") * n_rows * n_cols
    slope_scale = frame_scale(n_tm, 2.0 / count)
    C = wc.shape[1]
    body = n_rows * W

    def load_halo(y, carry):
        store_stack(c3, y, top[rows(y, 1, W), :].astype(F32), FWD)
        store_stack(c3, y + HALO + n_rows, bot[rows(y, 1, W), :].astype(F32), FWD)
        return carry

    def load_code(y, carry):
        store_stack(c3, y + HALO, code[rows(y, 1, W), :].astype(F32), FWD)
        return carry

    lax.fori_loop(0, HALO, load_halo, 0)
    lax.fori_loop(0, n_rows, load_code, 0)

    def motion_rows(b, carry):
        y = b * MOTION_BLOCK
        taps = jnp.concatenate([c3[rows(y + i, MOTION_BLOCK, W), :] for i in range(3)], axis=1)
        pre = dot(taps, wc[...]) + bias[1:2, :]
        for u in range(MOTION_BLOCK):
            value, slope = silu_pair(pre[u * W : (u + 1) * W])
            d_motion[rows(y + u, 1, W), :] = slope
            store_stack(jm, y + u, jnp.where(inside_frame(n_rows, y + u - 3), value, 0.0), FWD)
        return carry

    lax.fori_loop(0, (n_rows + 6) // MOTION_BLOCK, motion_rows, 0)

    block = HIDDEN_BLOCK
    k_row = lax.broadcasted_iota(jnp.int32, (16, block * W), 0)
    b_col = jnp.where(k_row == 0, b_head[0], jnp.where(k_row == 1, b_head[1], 0.0))

    def hidden_rows(b, carry):
        y = b * block
        taps = [ref[rows(y + i, block, W), :] for i in range(3) for ref in (jm, jf)]
        pre = dot(jnp.concatenate(taps, axis=1), wj[...]) + bias[3:4, :]
        value, slope = silu_pair(pre)
        hidden = value.astype(BF)
        hid[rows(y, block, W), :] = hidden
        pred = lax.dot_general(wht[0:16, :], hidden, NT, preferred_element_type=F32)
        error = pred + b_col - tgt[:, rows(y, block, W)]
        err[:, rows(y, block, W)] = error
        back = lax.dot_general(split3(error * slope_scale), wht[...], TN, preferred_element_type=F32) * slope
        for u in range(block):
            v = jnp.where(inside_frame(n_rows, y + u - 2), back[u * W : (u + 1) * W], 0.0)
            store_stack(s3, y + u, v, BWD)
        return carry

    lax.fori_loop(0, (n_rows + 4) // block, hidden_rows, 0)

    acc[...] = jnp.zeros_like(acc)
    g_head[...] = jnp.zeros_like(g_head)

    def own_rows(b, carry):
        y = 2 * b
        g_head[...] += dot(split3(err[:, rows(y + 2, 2, W)] * slope_scale), hid[rows(y + 2, 2, W), :])
        part = s3[rows(y + 2, 2, W), C : 2 * C].astype(F32)
        acc[...] += jnp.sum(part.reshape(2 * W // 8, 8, C), axis=0)
        jt[0:C, rows(y, 2, W)] = jm[rows(y + 3, 2, W), C : 2 * C].T
        jt[C : 2 * C, rows(y, 2, W)] = jf[rows(y + 3, 2, W), C : 2 * C].T
        return carry

    lax.fori_loop(0, n_rows // 2, own_rows, 0)
    own = err[:, TARGET_HALO * W : TARGET_HALO * W + body]
    for k in range(2):
        for y in range(n_rows):
            error_out[k, y : y + 1, :] = own[k : k + 1, y * W : (y + 1) * W]
    g_b_head = jnp.sum(own * slope_scale, axis=1, keepdims=True)
    loss = jnp.sum(jnp.sum(own * own, axis=1, keepdims=True), axis=0, keepdims=True)
    loss = loss * frame_scale(n_tm, 1.0 / count)
    col = lax.broadcasted_iota(jnp.int32, (1, C), 1)
    tail = jnp.where(col == 0, loss, jnp.where(col == 1, g_b_head[0:1], jnp.where(col == 2, g_b_head[1:2], 0.0)))
    misc[0:3, :] = jnp.zeros((3, C), F32)
    misc[3:4, :] = jnp.sum(acc[...], axis=0, keepdims=True)
    misc[4:6, :] = g_head[0:2, :] + g_head[16:18, :] + g_head[32:34, :]
    misc[6:7, :] = tail
    misc[7:8, :] = jnp.zeros((1, C), F32)


def rest_kernel(
    n_rows, n_cols, at_misc,
    jt, s3, d_motion, d_flow, xb, vol, code, misc, wv, wcb, wjb, bias,
    keep, send,
    m3, s_flow, s_code, acc, grads,
):
    W = n_cols
    C = code.shape[1]
    body = n_rows * W

    def joint_slopes(b, carry):
        y = b * SLOPE_BLOCK
        taps = jnp.concatenate([s3[rows(y + 2 - i, SLOPE_BLOCK, W), :] for i in range(3)], axis=1)
        sj = dot_nt(taps, wjb[...])
        for u in range(SLOPE_BLOCK):
            part = sj[u * W : (u + 1) * W]
            v = part[:, 0:C] * d_motion[rows(y + u + 2, 1, W), :]
            store_stack(m3, y + u, jnp.where(inside_frame(n_rows, y + u - 1), v, 0.0), BWD)
            s_flow[rows(y + u, 1, W), :] = (part[:, C:] * d_flow[rows(y + u + 2, 1, W), :]).astype(BF)
        return carry

    lax.fori_loop(0, (n_rows + 2) // SLOPE_BLOCK, joint_slopes, 0)
    acc[...] = jnp.zeros_like(acc)

    def add_rows(k, v):
        acc[8 * k : 8 * k + 8, :] += jnp.sum(v.reshape(v.shape[0] // 8, 8, C), axis=0)

    def code_slopes(b, carry):
        y = b * CODE_BLOCK
        at = rows(y, CODE_BLOCK, W)
        taps = jnp.concatenate([m3[rows(y + 2 - i, CODE_BLOCK, W), :] for i in range(3)], axis=1)
        sc = dot_nt(taps, wcb[...])
        pre = lax.dot_general(vol[:, at], wv[...], TN, preferred_element_type=F32) + bias[0:1, :]
        slope = (sc * silu_pair(pre)[1]).astype(BF)
        s_code[at, :] = slope
        add_rows(0, slope.astype(F32))
        add_rows(1, m3[rows(y + 1, CODE_BLOCK, W), C : 2 * C].astype(F32))
        add_rows(2, s_flow[rows(y + 1, CODE_BLOCK, W), :].astype(F32))
        return carry

    lax.fori_loop(0, n_rows // CODE_BLOCK, code_slopes, 0)

    for i in range(3):
        g = dot(jt[...], s3[(3 - i) * W : (3 - i) * W + body, :])
        for j in range(3):
            at = (i * 3 + j) * 2 * C
            grads[at : at + 2 * C, :] = g[:, j * C : (j + 1) * C]
    code_t = code[...].T
    for i in range(3):
        g = dot(code_t, m3[(2 - i) * W : (2 - i) * W + body, :])
        for j in range(3):
            at = AT_CODE + (i * 3 + j) * C
            grads[at : at + C, :] = g[:, j * C : (j + 1) * C]
    grads[AT_VOLUME:AT_FLOW, :] = dot(vol[...], s_code[...])
    gf = jnp.zeros((112, C), F32)
    for y in range(n_rows):
        gf = gf + dot(xb[(y + 3) * 16 : (y + 3) * 16 + 112, :], s_flow[(y + 1) * W : (y + 2) * W, :])
    grads[AT_FLOW : AT_FLOW + 112, :] = gf
    if at_misc > AT_END:
        grads[AT_END:at_misc, :] = jnp.zeros((at_misc - AT_END, C), F32)
    for k in range(3):
        grads[at_misc + k : at_misc + k + 1, :] = jnp.sum(acc[8 * k : 8 * k + 8, :], axis=0, keepdims=True)
    grads[at_misc + 3 : at_misc + 8, :] = misc[3:8, :]
    grads[at_misc + 8 :, :] = jnp.zeros((grads.shape[0] - at_misc - 8, C), F32)
    half = keep.shape[0]
    core = lax.axis_index("tm") % 2
    keep[...] = pick(grads, core, half)
    send[...] = pick(grads, 1 - core, half)


VMEM = pl.BlockSpec(memory_space=pltpu.VMEM)
SMEM = pl.BlockSpec(memory_space=pltpu.SMEM)
HBM = pl.BlockSpec(memory_space=pltpu.HBM)


def bits_of(axis):
    bits = []
    bit = 1
    while bit < lax.axis_size(axis):
        bits.append((axis, bit))
        bit *= 2
    return bits


def trade(x, axis, bit):
    return lax.ppermute(x, axis, [(i, i ^ bit) for i in range(lax.axis_size(axis))])


def upper_of(axis, bit):
    return (lax.axis_index(axis) // bit) % 2


def three_terms(x, at, is_last):
    value = x[at : at + MISC_ROWS]
    mid = value - lax.reduce_precision(value, 8, 7)
    low = mid - lax.reduce_precision(mid, 8, 7)
    terms = jnp.concatenate([x[: at + MISC_ROWS], mid, low, x[at + 3 * MISC_ROWS :]])
    return jnp.where(is_last, terms, x).astype(BF)


def halving_reduce(x, steps, is_last):
    for axis, bit in steps:
        upper = upper_of(axis, bit)
        is_last = is_last * upper
        half = x.shape[0] // 2
        mine = lax.dynamic_slice_in_dim(x, upper * half, half, 0)
        other = lax.dynamic_slice_in_dim(x, (1 - upper) * half, half, 0)
        x = mine + trade(other, axis, bit)
    x = three_terms(x, 0, is_last == 1)
    for axis, bit in steps[::-1]:
        got = trade(x, axis, bit)
        x = jnp.where(upper_of(axis, bit) == 0, jnp.concatenate([x, got]), jnp.concatenate([got, x]))
    return x


def pick(ref, which, half):
    return ref[pl.ds(pl.multiple_of(which * half, 8), half), :]


def cut(x, which, n):
    return lax.dynamic_slice_in_dim(x, which * n, n, 0)


def ordered(mine, got, axis, bit):
    return jnp.where(upper_of(axis, bit) == 0, jnp.concatenate([mine, got]), jnp.concatenate([got, mine]))


def paired_reduce(x_sum, at_misc):
    half = x_sum.shape[0]
    x, z, far_z = ("tm", 2), ("space", 1), ("space", 2)
    upper_x, upper_z, upper_far, core = upper_of(*x), upper_of(*z), upper_of(*far_z), upper_of("tm", 1)
    a, b = x_sum[: half // 2], x_sum[half // 2 :]
    n = half // 4
    at = at_misc - 2 * half + n
    sends = jnp.logical_and(core == 1, upper_z == 0)
    holds = jnp.logical_and(core == 1, upper_z == 1)
    a_got = trade(cut(a, 1 - upper_x, n).astype(BF), *x)
    b_got = trade(three_terms(cut(b, 1 - upper_z, n), at, sends), *z)
    a = cut(a, upper_x, n) + a_got.astype(F32)
    b = cut(b, upper_z, n)
    got = b_got.astype(F32)
    misc = b[at : at + MISC_ROWS] + sum(got[at + k * MISC_ROWS : at + (k + 1) * MISC_ROWS] for k in range(3))
    fixed = jnp.concatenate([misc, jnp.zeros((2 * MISC_ROWS, misc.shape[1]), F32)])
    b = b + got
    b = jnp.concatenate([b[:at], jnp.where(holds, fixed, b[at : at + 3 * MISC_ROWS]), b[at + 3 * MISC_ROWS :]])
    n = half // 8
    a_got, b_got = trade(cut(a, 1 - upper_z, n), *z), trade(cut(b, 1 - upper_x, n), *x)
    a, b = cut(a, upper_z, n) + a_got, cut(b, upper_x, n) + b_got
    is_far = upper_far == 1
    y = jnp.where(is_far, b, a) + trade(jnp.where(is_far, a, b), *far_z)
    y = three_terms(y, at_misc - (2 * half - n), core + upper_x + upper_z + upper_far == 4)
    got = trade(y, *far_z)
    a, b = jnp.where(is_far, got, y), jnp.where(is_far, y, got)
    a, b = ordered(a, trade(a, *z), *z), ordered(b, trade(b, *x), *x)
    a, b = ordered(a, trade(a, *x), *x), ordered(b, trade(b, *z), *z)
    return jnp.concatenate([a, b])


def finish_kernel(
    at_misc,
    bits, mine, other,
    joint, code, volume, flow, b_volume, b_code, b_flow, b_joint, head, loss, b_head,
    full,
):
    half, C = mine.shape
    full[pl.ds(pl.multiple_of(bits[0] * half, 16), half), :] = mine[...]
    full[pl.ds(pl.multiple_of((1 - bits[0]) * half, 16), half), :] = other[...]
    for i in range(3):
        for j in range(3):
            at = (i * 3 + j) * 2 * C
            joint[i, j, :, :] = full[at : at + 2 * C, :].astype(F32)
            at = AT_CODE + (i * 3 + j) * C
            code[i, j, :, :] = full[at : at + C, :].astype(F32)
    parts = full[AT_VOLUME:AT_FLOW, :].astype(F32)
    for half_at in range(2):
        for dy in range(SIDE):
            at, to = half_at * HALF, half_at * OFF + dy * SIDE
            volume[to : to + 8, :] = parts[at + 8 * dy : at + 8 * dy + 8]
            volume[to + 8 : to + 9, :] = parts[at + 72 + dy : at + 73 + dy]
    for i in range(7):
        part = full[AT_FLOW + 16 * i : AT_FLOW + 16 * i + 16, :].astype(F32)
        for j in range(7):
            flow[i, j, :, :] = part[2 * j : 2 * j + 2]
    terms = full[at_misc : at_misc + 32, :].astype(F32)
    misc = terms[0:8] + terms[8:16] + terms[16:24]
    for k, ref in enumerate((b_volume, b_code, b_flow, b_joint)):
        ref[...] = misc[k]
    head[...] = misc[4:6]
    lane = lax.broadcasted_iota(jnp.int32, (1, C), 1)
    loss[0] = jnp.sum(jnp.where(lane == 0, misc[6:7], 0.0))
    b_head[0] = jnp.sum(jnp.where(lane == 1, misc[6:7], 0.0))
    b_head[1] = jnp.sum(jnp.where(lane == 2, misc[6:7], 0.0))


def call(body, name, out_shape, in_specs, scratch, flops, *args, out_specs=None):
    held = [
        x if spec is SMEM else pltpu.with_memory_space_constraint(x, spec.memory_space)
        for x, spec in zip(args, in_specs, strict=True)
    ]
    return pl.pallas_call(
        body,
        out_shape=out_shape,
        in_specs=in_specs,
        out_specs=out_specs or jax.tree.map(lambda _: VMEM, out_shape),
        scratch_shapes=scratch,
        cost_estimate=pl.CostEstimate(flops=flops, bytes_accessed=flops // 300, transcendentals=0),
        compiler_params=pltpu.CompilerParams(vmem_limit_bytes=16 << 20),
        name=name,
    )(*held)


def local(
    features, pair_order, flow_now, targets, w_volume, b_volume, w_code, b_code,
    w_flow, b_flow, w_joint, b_joint, w_head, b_head,
):
    own = features[0]
    n_rows, n_cols, n_chan = own.shape
    n_code = w_code.shape[3]
    W, C = n_cols, n_code
    body = n_rows * n_cols
    halo = HALO * n_cols
    n_tm, n_space = lax.axis_size("tm"), lax.axis_size("space")
    flat = own.reshape(body, n_chan)
    both = ("tm", "space")

    def route(partner, ds):
        pairs = []
        for t in range(n_tm):
            for s in range(n_space):
                if 0 <= partner(t) < n_tm and 0 <= s + ds < n_space:
                    pairs.append((t * n_space + s, partner(t) * n_space + s + ds))
        return pairs

    def near(t):
        return t + 1 - 2 * (t % 2)

    def far(t):
        return t - 1 + 2 * (t % 2)

    first, last = flat[:halo], flat[body - halo :]
    near_top = lax.ppermute(last, both, route(near, 1))
    near_bot = lax.ppermute(first, both, route(near, -1))
    near_mid = lax.ppermute(flat, both, route(near, 0))
    far_top = lax.ppermute(last, both, route(far, 1))
    far_bot = lax.ppermute(first, both, route(far, -1))
    far_mid = lax.ppermute(flat, both, route(far, 0))

    def shape(*dims, dtype=BF):
        return pltpu.VMEM(dims, dtype)

    def result(*dims):
        return jax.ShapeDtypeStruct(dims, F32)

    near_vol, held, flow, held_targets, wc, bias, wv, wcb, wj, wjb, wf, wht = call(
        functools.partial(near_kernel, n_rows, n_cols), "near",
        (
            shape(HALF, body), shape(body, n_chan), shape(*flow_now.shape[1:]),
            shape(*targets.shape[1:], dtype=jnp.int32), shape(3, 3, C, C), shape(4, C, dtype=F32),
            shape(2 * HALF, C), shape(C, 9 * C), shape(18 * C, C),
            shape(2 * C, 9 * C), shape(112, C), shape(48, C),
        ),
        [HBM] * 11 + [VMEM] * 4,
        [
            pltpu.VMEM((body + 2 * halo, n_chan), BF),
            pltpu.VMEM((HALF, 2 * W), F32),
            pltpu.VMEM((2 * HALF, C), F32),
            pltpu.VMEM(w_volume.shape, BF),
            pltpu.VMEM(w_joint.shape, BF),
            pltpu.VMEM(w_flow.shape, BF),
            pltpu.SemaphoreType.DMA((11,)),
        ],
        4_000_000_000,
        flat, flow_now[0], targets[0], w_volume, w_code, w_joint, w_flow, b_volume, b_code, b_flow, b_joint,
        near_mid, near_top, near_bot, w_head.T,
    )
    vol, code, up, dn = call(
        functools.partial(code_kernel, n_rows, n_cols), "code",
        (shape(2 * HALF, body), shape(body, C), shape(halo + 16, C), shape(halo + 16, C)),
        [SMEM] + [VMEM] * 9,
        [
            pltpu.VMEM((body + 2 * halo, n_chan), BF),
            pltpu.VMEM((HALF, 2 * W), F32),
            pltpu.VMEM((16, W), F32),
        ],
        4_000_000_000,
        pair_order, held, far_mid, far_top, far_bot, near_vol, wv, bias, flow, held_targets,
    )
    top = lax.ppermute(dn, "space", [(s, s + 1) for s in range(n_space - 1)])
    bot = lax.ppermute(up, "space", [(s + 1, s) for s in range(n_space - 1)])

    jf, d_flow, xb, tgt = call(
        functools.partial(flow_kernel, n_rows, n_cols), "flow",
        (
            shape((n_rows + 6) * W, 3 * C),
            shape((n_rows + 6) * W, C, dtype=F32),
            shape((n_rows + 12) * 16, W),
            shape(16, (n_rows + 4) * W, dtype=F32),
        ),
        [VMEM] * 6,
        [
            pltpu.VMEM((24, W), F32),
            pltpu.VMEM(((n_rows + 12) * 16, W), F32),
        ],
        1_000_000_000,
        top, bot, flow, held_targets, wf, bias,
    )
    flow_error, jt, s3, d_motion, misc = call(
        functools.partial(hidden_kernel, n_rows, n_cols, n_tm), "hidden",
        (
            result(2, n_rows, W),
            shape(2 * C, body),
            shape((n_rows + 4) * W, 3 * C),
            shape((n_rows + 6) * W, C, dtype=F32),
            shape(MISC_ROWS, C, dtype=F32),
        ),
        [SMEM] + [VMEM] * 9,
        [
            pltpu.VMEM(((n_rows + 8) * W, 3 * C), BF),
            pltpu.VMEM(((n_rows + 6) * W, 3 * C), BF),
            pltpu.VMEM((16, (n_rows + 4) * W), F32),
            pltpu.VMEM(((n_rows + 4) * W, C), BF),
            pltpu.VMEM((48, C), F32),
            pltpu.VMEM((8, C), F32),
        ],
        4_000_000_000,
        b_head, code, top, bot, jf, tgt, wc.reshape(9 * C, C), wj, wht, bias,
    )
    n_dev = n_tm * n_space
    paired = n_tm == 4 and n_space == 4
    if paired:
        grad_rows, at_misc = 3840, AT_END
    else:
        chunk = -(-max(pl.cdiv(AT_END, n_dev - 1), 3 * MISC_ROWS) // 16) * 16
        grad_rows, at_misc = n_dev * chunk, (n_dev - 1) * chunk
    keep, send = call(
        functools.partial(rest_kernel, n_rows, n_cols, at_misc), "rest",
        (shape(grad_rows // 2, C, dtype=F32), shape(grad_rows // 2, C, dtype=F32)),
        [VMEM] * 12,
        [
            pltpu.VMEM(((n_rows + 2) * W, 3 * C), BF),
            pltpu.VMEM(((n_rows + 2) * W, C), BF),
            pltpu.VMEM((body, C), BF),
            pltpu.VMEM((24, C), F32),
            pltpu.VMEM((grad_rows, C), F32),
        ],
        3_000_000_000,
        jt, s3, d_motion, d_flow, xb, vol, code, misc, wv, wcb, wjb, bias,
    )
    core = ("tm", 1)
    got = trade(send, *core)
    bits = jnp.stack([upper_of("tm", 1), upper_of("tm", 2), upper_of("space", 1), upper_of("space", 2)])
    bits = bits.astype(jnp.int32)
    if paired:
        mine = paired_reduce(keep + got, at_misc)
    else:
        mine = halving_reduce(keep + got, bits_of("tm")[1:] + bits_of("space"), upper_of(*core))
    other = trade(mine, *core)
    outs = call(
        functools.partial(finish_kernel, at_misc), "finish",
        (
            result(3, 3, 2 * C, C),
            result(3, 3, C, C),
            result(2 * OFF, C),
            result(7, 7, 2, C),
            result(C), result(C), result(C), result(C),
            result(2, C), result(1), result(2),
        ),
        [SMEM] + [VMEM] * 2, [pltpu.VMEM((grad_rows, C), BF)], 100_000_000,
        bits, mine, other,
        out_specs=(VMEM,) * 9 + (SMEM,) * 2,
    )
    joint, g_code, g_volume, g_flow, g_bv, g_bc, g_bf, g_bj, head, loss, g_b_head = outs
    return loss, flow_error[None], g_volume, g_bv, g_code, g_bc, g_flow, g_bf, joint, g_bj, head.T, g_b_head


def solution(mesh):
    placed = (
        P(("groups", "tm"), "space", None, None),
        P(("groups", "tm")),
        P(("groups", "tm"), None, "space", None),
        P(("groups", "tm"), None, "space", None),
    ) + (P(),) * 10
    return jax.shard_map(
        local,
        mesh=mesh,
        in_specs=placed,
        out_specs=(
            P("groups"),
            P(("groups", "tm"), None, "space", None),
            P("groups", None),
            P("groups"),
            P("groups", None, None, None),
            P("groups"),
            P("groups", None, None, None),
            P("groups"),
            P("groups", None, None, None),
            P("groups"),
            P("groups", None),
            P("groups"),
        ),
        check_vma=False,
    )
```

```python
import functools

import jax
import jax.numpy as jnp
from jax import lax
from jax.experimental import pallas as pl
from jax.experimental.pallas import tpu as pltpu
from jax.sharding import PartitionSpec as P

BF = jnp.bfloat16
F32 = jnp.float32
RADIUS = 4
SIDE = 2 * RADIUS + 1
OFF = SIDE * SIDE
HALO = 4
FLOW_HALO = 6
TARGET_HALO = 2
NT = (((1,), (1,)), ((), ()))
TN = (((0,), (0,)), ((), ()))

AT_CODE = 2304
AT_VOLUME = 3456
AT_FLOW = 3648
AT_END = 3760
HALF = 96
MOTION_BLOCK = 7
HIDDEN_BLOCK = 12
SLOPE_BLOCK = 10
CODE_BLOCK = 4
MISC_ROWS = 8


def dot(a, b):
    return jnp.dot(a, b, preferred_element_type=F32)


def dot_nt(a, b):
    return lax.dot_general(a, b, NT, preferred_element_type=F32)


def rows(start, count, unit):
    return pl.ds(pl.multiple_of(start * unit, unit), count * unit)


def split3(s, padded=False):
    hi = s.astype(BF).astype(F32)
    mid = (s - hi).astype(BF).astype(F32)
    terms = [hi, mid, s - hi - mid] + [jnp.zeros_like(s)] * padded
    return jnp.concatenate(terms, axis=0).astype(BF)


def silu_pair(v):
    s = jax.nn.sigmoid(v)
    return v * s, s * (1.0 + v * (1.0 - s))


def correlate(n_rows, n_cols, own, mid, top, bot, out, out_at, near, rows_f):
    n_chan = own.shape[1]
    halo = RADIUS * n_cols
    body = n_rows * n_cols
    near[0:halo, :] = top[...]
    near[halo : halo + body, :] = mid[...]
    near[halo + body :, :] = bot[...]
    W = n_cols
    j_at = lax.broadcasted_iota(jnp.int32, (W, 2 * W), 0)
    x_at = lax.broadcasted_iota(jnp.int32, (W, 2 * W), 1) & (W - 1)
    band = jnp.logical_and(j_at - x_at >= -RADIUS, j_at - x_at < RADIUS)
    edge = j_at - x_at == RADIUS
    turn = lax.broadcasted_iota(jnp.int32, (8, 2 * W), 1) + RADIUS
    scale = n_chan ** (-0.5)

    def fold(v):
        parts = [v[8 * g : 8 * g + 8] for g in range(W // 8)]
        while len(parts) > 1:
            parts = [parts[k] + parts[k + 1] for k in range(0, len(parts), 2)]
        return parts[0]

    def two_rows(b, carry):
        tile = own[rows(2 * b, 2, W), :]
        rows_f[...] = jnp.zeros_like(rows_f)
        for q in range(SIDE + 1):
            scores = lax.dot_general(
                near[rows(2 * b + q, 1, W), :], tile, NT, preferred_element_type=F32
            )
            inner = fold(jnp.where(band, scores, 0.0))
            outer = jnp.sum(fold(jnp.where(edge, scores, 0.0)), axis=0, keepdims=True)
            for bit in (1, 2, 4):
                inner = jnp.where((turn & bit) != 0, pltpu.roll(inner, 8 - bit, 0), inner)
            for u in range(2):
                dy = q - u
                if 0 <= dy < SIDE:
                    rows_f[8 * dy : 8 * dy + 8, u * W : (u + 1) * W] = inner[:, u * W : (u + 1) * W]
                    rows_f[72 + dy : 73 + dy, u * W : (u + 1) * W] = outer[:, u * W : (u + 1) * W]
        out[out_at, rows(2 * b, 2, W)] = (rows_f[...] * scale).astype(BF)
        return carry

    lax.fori_loop(0, n_rows // 2, two_rows, 0)


def near_kernel(
    n_rows, n_cols,
    own_hbm, flow_hbm, targets_hbm, volume_hbm, code_hbm, joint_hbm, w_flow_hbm, bv_hbm, bc_hbm, bf_hbm, bj_hbm,
    mid, top, bot, head,
    out, own, flow, targets, w_code, bias, wv, wcb, wj, wjb, wf, wht,
    near, rows_f, wide, w_volume, w_joint, w_flow, sems,
):
    loads = (
        (own_hbm, own), (flow_hbm, flow), (targets_hbm, targets), (volume_hbm, w_volume), (code_hbm, w_code),
        (joint_hbm, w_joint), (w_flow_hbm, w_flow), (bv_hbm, bias.at[0]), (bc_hbm, bias.at[1]),
        (bf_hbm, bias.at[2]), (bj_hbm, bias.at[3]),
    )
    copies = [pltpu.make_async_copy(src, dst, sems.at[k]) for k, (src, dst) in enumerate(loads)]
    for copy in copies:
        copy.start()
    copies[0].wait()
    correlate(n_rows, n_cols, own, mid, top, bot, out, slice(None), near, rows_f)
    for copy in copies[1:]:
        copy.wait()
    C = w_code.shape[3]
    wide[...] = jnp.zeros_like(wide)
    weight = w_volume[...].astype(F32)
    for half in range(2):
        for dy in range(SIDE):
            at = half * OFF + dy * SIDE
            wide[half * HALF + 8 * dy : half * HALF + 8 * dy + 8, :] = weight[at : at + 8]
            wide[half * HALF + 72 + dy : half * HALF + 73 + dy, :] = weight[at + 8 : at + 9]
    wv[...] = wide[...].astype(BF)
    wide[...] = jnp.zeros_like(wide)
    for i in range(7):
        for j in range(7):
            wide[16 * i + 2 * j : 16 * i + 2 * j + 2, :] = w_flow[i, j].astype(F32)
    wf[...] = wide[0:112, :].astype(BF)
    for i in range(3):
        for j in range(3):
            at = (3 * i + j) * C
            wcb[:, at : at + C] = w_code[i, j]
            wjb[:, at : at + C] = w_joint[i, j]
            for part in range(2):
                at = (2 * i + part) * 3 * C + j * C
                wj[at : at + C, :] = w_joint[i, j, part * C : (part + 1) * C, :]
    wide[...] = jnp.zeros_like(wide)
    for k in range(3):
        wide[16 * k : 16 * k + 2, :] = head[...].astype(F32)
    wht[...] = wide[0:48, :].astype(BF)


def code_kernel(
    n_rows, n_cols,
    order, own, mid, top, bot, near_vol, wv, bias, flow, targets,
    vol, code, up, dn,
    near, rows_f, edge,
):
    W = n_cols
    halo = HALO * W
    body = n_rows * W
    near_second = (order[0] != lax.axis_index("tm") % 2).astype(jnp.int32)
    near_at = pl.multiple_of(near_second * HALF, HALF)
    far_at = pl.multiple_of((1 - near_second) * HALF, HALF)
    vol[pl.ds(near_at, HALF), :] = near_vol[...]
    correlate(n_rows, n_cols, own, mid, top, bot, vol, pl.ds(far_at, HALF), near, rows_f)

    def one_code(r, carry):
        at = rows(r, CODE_BLOCK, W)
        pre = lax.dot_general(vol[:, at], wv[...], TN, preferred_element_type=F32) + bias[0:1, :]
        code[at, :] = (pre * jax.nn.sigmoid(pre)).astype(BF)
        return carry

    lax.fori_loop(0, n_rows // CODE_BLOCK, lambda r, c: one_code(CODE_BLOCK * r, c), 0)
    for ref, at, flow_at, target_at in (
        (up, 0, 0, 0),
        (dn, body - halo, n_rows - FLOW_HALO, n_rows - TARGET_HALO),
    ):
        ref[0:halo, :] = code[at : at + halo, :]
        for k in range(2):
            edge[8 * k : 8 * k + FLOW_HALO, :] = flow[k].astype(F32)[flow_at : flow_at + FLOW_HALO]
            edge[8 * k + FLOW_HALO : 8 * k + 8, :] = targets[k].astype(F32)[target_at : target_at + TARGET_HALO]
        ref[halo : halo + 16, :] = edge[...].astype(BF)


def frame_scale(n_tm, per):
    frame = lax.axis_index("tm")
    value = jnp.float32(per)
    for t in range(n_tm - 1):
        value = jnp.where(frame == t, jnp.float32(per * 0.25 ** ((n_tm - 1 - t) / (n_tm - 1))), value)
    return value


def code_slope_kernel(vol, wv, bias, code, d_code, code_t):
    pre = lax.dot_general(vol[...], wv[...], TN, preferred_element_type=F32) + bias[0:1, :]
    d_code[...] = silu_pair(pre)[1]
    code_t[...] = code[...].T


def inside_frame(n_rows, ext):
    at = lax.axis_index("space") * n_rows + ext
    return jnp.logical_and(at >= 0, at < lax.axis_size("space") * n_rows)


def store_stack(ref, at, v, cols):
    W, C = v.shape
    x_at = lax.broadcasted_iota(jnp.int32, (W, C), 0)
    left = jnp.where(x_at == 0, 0.0, pltpu.roll(v, 1, 0))
    right = jnp.where(x_at == W - 1, 0.0, pltpu.roll(v, W - 1, 0))
    for col, part in zip(cols, (left, v, right)):
        ref[rows(at, 1, W), col * C : (col + 1) * C] = part.astype(BF)


FWD = (0, 1, 2)
BWD = (2, 1, 0)


def flow_kernel(n_rows, n_cols, top, bot, flow, targets, wf, bias, jf, d_flow, xb, tgt, xf, xx):
    W = n_cols
    halo = HALO * W
    xx[...] = jnp.zeros_like(xx)
    above = top[halo : halo + 16, :].astype(F32)
    below = bot[halo : halo + 16, :].astype(F32)
    n_flow = n_rows + 2 * FLOW_HALO
    lane = lax.broadcasted_iota(jnp.int32, (n_flow, W), 1)
    for k in range(2):
        xf[0:FLOW_HALO, :] = above[8 * k : 8 * k + FLOW_HALO, :]
        xf[FLOW_HALO : FLOW_HALO + n_rows, :] = flow[k].astype(F32)
        xf[FLOW_HALO + n_rows : n_flow, :] = below[8 * k : 8 * k + FLOW_HALO, :]
        own_flow = xf[0:n_flow, :]
        for j in range(7):
            shift = (3 - j) % W
            moved = pltpu.roll(own_flow, shift, 1) if shift else own_flow
            ok = jnp.logical_and(lane + (j - 3) >= 0, lane + (j - 3) < W)
            xx[pl.ds(j * 2 + k, n_flow, stride=16), :] = jnp.where(ok, moved, 0.0)
    xb[...] = xx[...].astype(BF)
    tgt[...] = jnp.zeros_like(tgt)
    for k in range(2):
        for y in range(TARGET_HALO):
            tgt[k : k + 1, y * W : (y + 1) * W] = above[8 * k + 6 + y : 8 * k + 7 + y, :]
            lo = (TARGET_HALO + n_rows + y) * W
            tgt[k : k + 1, lo : lo + W] = below[8 * k + 6 + y : 8 * k + 7 + y, :]
        for y in range(n_rows):
            lo = (TARGET_HALO + y) * W
            tgt[k : k + 1, lo : lo + W] = targets[k, y : y + 1, :].astype(F32)

    def flow_rows(b, carry):
        y = b * MOTION_BLOCK
        patches = [xb[pl.ds(pl.multiple_of((y + u) * 16, 16), 112), :] for u in range(MOTION_BLOCK)]
        pre = lax.dot_general(jnp.concatenate(patches, axis=1), wf[...], TN, preferred_element_type=F32)
        for u in range(MOTION_BLOCK):
            value, slope = silu_pair(pre[u * W : (u + 1) * W] + bias[2:3, :])
            d_flow[rows(y + u, 1, W), :] = slope
            store_stack(jf, y + u, jnp.where(inside_frame(n_rows, y + u - 3), value, 0.0), FWD)
        return carry

    lax.fori_loop(0, (n_rows + 6) // MOTION_BLOCK, flow_rows, 0)


def hidden_kernel(
    n_rows, n_cols, n_tm,
    b_head, code, top, bot, jf, tgt, wc, wj, wht, bias,
    error_out, jt, s3, d_motion, misc,
    c3, jm, err, hid, g_head, acc,
):
    W = n_cols
    count = 2.0 * n_tm * lax.axis_size("space") * n_rows * n_cols
    slope_scale = frame_scale(n_tm, 2.0 / count)
    C = wc.shape[1]
    body = n_rows * W

    def load_halo(y, carry):
        store_stack(c3, y, top[rows(y, 1, W), :].astype(F32), FWD)
        store_stack(c3, y + HALO + n_rows, bot[rows(y, 1, W), :].astype(F32), FWD)
        return carry

    def load_code(y, carry):
        store_stack(c3, y + HALO, code[rows(y, 1, W), :].astype(F32), FWD)
        return carry

    lax.fori_loop(0, HALO, load_halo, 0)
    lax.fori_loop(0, n_rows, load_code, 0)

    def motion_rows(b, carry):
        y = b * MOTION_BLOCK
        taps = jnp.concatenate([c3[rows(y + i, MOTION_BLOCK, W), :] for i in range(3)], axis=1)
        pre = dot(taps, wc[...]) + bias[1:2, :]
        for u in range(MOTION_BLOCK):
            value, slope = silu_pair(pre[u * W : (u + 1) * W])
            d_motion[rows(y + u, 1, W), :] = slope
            store_stack(jm, y + u, jnp.where(inside_frame(n_rows, y + u - 3), value, 0.0), FWD)
        return carry

    lax.fori_loop(0, (n_rows + 6) // MOTION_BLOCK, motion_rows, 0)

    block = HIDDEN_BLOCK
    k_row = lax.broadcasted_iota(jnp.int32, (16, block * W), 0)
    b_col = jnp.where(k_row == 0, b_head[0], jnp.where(k_row == 1, b_head[1], 0.0))

    def hidden_rows(b, carry):
        y = b * block
        taps = [ref[rows(y + i, block, W), :] for i in range(3) for ref in (jm, jf)]
        pre = dot(jnp.concatenate(taps, axis=1), wj[...]) + bias[3:4, :]
        value, slope = silu_pair(pre)
        hidden = value.astype(BF)
        hid[rows(y, block, W), :] = hidden
        pred = lax.dot_general(wht[0:16, :], hidden, NT, preferred_element_type=F32)
        error = pred + b_col - tgt[:, rows(y, block, W)]
        err[:, rows(y, block, W)] = error
        back = lax.dot_general(split3(error * slope_scale), wht[...], TN, preferred_element_type=F32) * slope
        for u in range(block):
            v = jnp.where(inside_frame(n_rows, y + u - 2), back[u * W : (u + 1) * W], 0.0)
            store_stack(s3, y + u, v, BWD)
        return carry

    lax.fori_loop(0, (n_rows + 4) // block, hidden_rows, 0)

    acc[...] = jnp.zeros_like(acc)
    g_head[...] = jnp.zeros_like(g_head)

    def own_rows(b, carry):
        y = 2 * b
        g_head[...] += dot(split3(err[:, rows(y + 2, 2, W)] * slope_scale), hid[rows(y + 2, 2, W), :])
        part = s3[rows(y + 2, 2, W), C : 2 * C].astype(F32)
        acc[...] += jnp.sum(part.reshape(2 * W // 8, 8, C), axis=0)
        jt[0:C, rows(y, 2, W)] = jm[rows(y + 3, 2, W), C : 2 * C].T
        jt[C : 2 * C, rows(y, 2, W)] = jf[rows(y + 3, 2, W), C : 2 * C].T
        return carry

    lax.fori_loop(0, n_rows // 2, own_rows, 0)
    own = err[:, TARGET_HALO * W : TARGET_HALO * W + body]
    for k in range(2):
        for y in range(n_rows):
            error_out[k, y : y + 1, :] = own[k : k + 1, y * W : (y + 1) * W]
    g_b_head = jnp.sum(own * slope_scale, axis=1, keepdims=True)
    loss = jnp.sum(jnp.sum(own * own, axis=1, keepdims=True), axis=0, keepdims=True)
    loss = loss * frame_scale(n_tm, 1.0 / count)
    col = lax.broadcasted_iota(jnp.int32, (1, C), 1)
    tail = jnp.where(col == 0, loss, jnp.where(col == 1, g_b_head[0:1], jnp.where(col == 2, g_b_head[1:2], 0.0)))
    misc[0:3, :] = jnp.zeros((3, C), F32)
    misc[3:4, :] = jnp.sum(acc[...], axis=0, keepdims=True)
    misc[4:6, :] = g_head[0:2, :] + g_head[16:18, :] + g_head[32:34, :]
    misc[6:7, :] = tail
    misc[7:8, :] = jnp.zeros((1, C), F32)


def rest_kernel(
    n_rows, n_cols, at_misc,
    jt, s3, d_motion, d_flow, xb, vol, d_code, code_t, misc, wcb, wjb,
    keep, send,
    m3, s_flow, s_code, acc, grads,
):
    W = n_cols
    C = d_code.shape[1]
    body = n_rows * W

    def joint_slopes(b, carry):
        y = b * SLOPE_BLOCK
        taps = jnp.concatenate([s3[rows(y + 2 - i, SLOPE_BLOCK, W), :] for i in range(3)], axis=1)
        sj = dot_nt(taps, wjb[...])
        for u in range(SLOPE_BLOCK):
            part = sj[u * W : (u + 1) * W]
            v = part[:, 0:C] * d_motion[rows(y + u + 2, 1, W), :]
            store_stack(m3, y + u, jnp.where(inside_frame(n_rows, y + u - 1), v, 0.0), BWD)
            s_flow[rows(y + u, 1, W), :] = (part[:, C:] * d_flow[rows(y + u + 2, 1, W), :]).astype(BF)
        return carry

    lax.fori_loop(0, (n_rows + 2) // SLOPE_BLOCK, joint_slopes, 0)
    acc[...] = jnp.zeros_like(acc)

    def add_rows(k, v):
        acc[8 * k : 8 * k + 8, :] += jnp.sum(v.reshape(v.shape[0] // 8, 8, C), axis=0)

    def code_slopes(b, carry):
        y = b * CODE_BLOCK
        at = rows(y, CODE_BLOCK, W)
        taps = jnp.concatenate([m3[rows(y + 2 - i, CODE_BLOCK, W), :] for i in range(3)], axis=1)
        sc = dot_nt(taps, wcb[...])
        slope = (sc * d_code[at, :]).astype(BF)
        s_code[at, :] = slope
        add_rows(0, slope.astype(F32))
        add_rows(1, m3[rows(y + 1, CODE_BLOCK, W), C : 2 * C].astype(F32))
        add_rows(2, s_flow[rows(y + 1, CODE_BLOCK, W), :].astype(F32))
        return carry

    lax.fori_loop(0, n_rows // CODE_BLOCK, code_slopes, 0)

    for i in range(3):
        g = dot(jt[...], s3[(3 - i) * W : (3 - i) * W + body, :])
        for j in range(3):
            at = (i * 3 + j) * 2 * C
            grads[at : at + 2 * C, :] = g[:, j * C : (j + 1) * C]
    for i in range(3):
        g = dot(code_t[...], m3[(2 - i) * W : (2 - i) * W + body, :])
        for j in range(3):
            at = AT_CODE + (i * 3 + j) * C
            grads[at : at + C, :] = g[:, j * C : (j + 1) * C]
    grads[AT_VOLUME:AT_FLOW, :] = dot(vol[...], s_code[...])
    gf = jnp.zeros((112, C), F32)
    for y in range(n_rows):
        gf = gf + dot(xb[(y + 3) * 16 : (y + 3) * 16 + 112, :], s_flow[(y + 1) * W : (y + 2) * W, :])
    grads[AT_FLOW : AT_FLOW + 112, :] = gf
    if at_misc > AT_END:
        grads[AT_END:at_misc, :] = jnp.zeros((at_misc - AT_END, C), F32)
    for k in range(3):
        grads[at_misc + k : at_misc + k + 1, :] = jnp.sum(acc[8 * k : 8 * k + 8, :], axis=0, keepdims=True)
    grads[at_misc + 3 : at_misc + 8, :] = misc[3:8, :]
    grads[at_misc + 8 :, :] = jnp.zeros((grads.shape[0] - at_misc - 8, C), F32)
    half = keep.shape[0]
    core = lax.axis_index("tm") % 2
    keep[...] = pick(grads, core, half)
    send[...] = pick(grads, 1 - core, half)


VMEM = pl.BlockSpec(memory_space=pltpu.VMEM)
SMEM = pl.BlockSpec(memory_space=pltpu.SMEM)
HBM = pl.BlockSpec(memory_space=pltpu.HBM)


def bits_of(axis):
    bits = []
    bit = 1
    while bit < lax.axis_size(axis):
        bits.append((axis, bit))
        bit *= 2
    return bits


def trade(x, axis, bit):
    return lax.ppermute(x, axis, [(i, i ^ bit) for i in range(lax.axis_size(axis))])


def upper_of(axis, bit):
    return (lax.axis_index(axis) // bit) % 2


def three_terms(x, at, is_last):
    value = x[at : at + MISC_ROWS]
    mid = value - lax.reduce_precision(value, 8, 7)
    low = mid - lax.reduce_precision(mid, 8, 7)
    terms = jnp.concatenate([x[: at + MISC_ROWS], mid, low, x[at + 3 * MISC_ROWS :]])
    return jnp.where(is_last, terms, x).astype(BF)


def halving_reduce(x, steps, is_last):
    for axis, bit in steps:
        upper = upper_of(axis, bit)
        is_last = is_last * upper
        half = x.shape[0] // 2
        mine = lax.dynamic_slice_in_dim(x, upper * half, half, 0)
        other = lax.dynamic_slice_in_dim(x, (1 - upper) * half, half, 0)
        x = mine + trade(other, axis, bit)
    x = three_terms(x, 0, is_last == 1)
    for axis, bit in steps[::-1]:
        got = trade(x, axis, bit)
        x = jnp.where(upper_of(axis, bit) == 0, jnp.concatenate([x, got]), jnp.concatenate([got, x]))
    return x


def pick(ref, which, half):
    return ref[pl.ds(pl.multiple_of(which * half, 8), half), :]


def cut(x, which, n):
    return lax.dynamic_slice_in_dim(x, which * n, n, 0)


def ordered(mine, got, axis, bit):
    return jnp.where(upper_of(axis, bit) == 0, jnp.concatenate([mine, got]), jnp.concatenate([got, mine]))


def paired_reduce(x_sum, at_misc):
    half = x_sum.shape[0]
    x, z, far_z = ("tm", 2), ("space", 1), ("space", 2)
    upper_x, upper_z, upper_far, core = upper_of(*x), upper_of(*z), upper_of(*far_z), upper_of("tm", 1)
    a, b = x_sum[: half // 2], x_sum[half // 2 :]
    n = half // 4
    at = at_misc - 2 * half + n
    sends = jnp.logical_and(core == 1, upper_z == 0)
    holds = jnp.logical_and(core == 1, upper_z == 1)
    a_got = trade(cut(a, 1 - upper_x, n).astype(BF), *x)
    b_got = trade(three_terms(cut(b, 1 - upper_z, n), at, sends), *z)
    a = cut(a, upper_x, n) + a_got.astype(F32)
    b = cut(b, upper_z, n)
    got = b_got.astype(F32)
    misc = b[at : at + MISC_ROWS] + sum(got[at + k * MISC_ROWS : at + (k + 1) * MISC_ROWS] for k in range(3))
    fixed = jnp.concatenate([misc, jnp.zeros((2 * MISC_ROWS, misc.shape[1]), F32)])
    b = b + got
    b = jnp.concatenate([b[:at], jnp.where(holds, fixed, b[at : at + 3 * MISC_ROWS]), b[at + 3 * MISC_ROWS :]])
    n = half // 8
    a_got, b_got = trade(cut(a, 1 - upper_z, n), *z), trade(cut(b, 1 - upper_x, n), *x)
    a, b = cut(a, upper_z, n) + a_got, cut(b, upper_x, n) + b_got
    is_far = upper_far == 1
    y = jnp.where(is_far, b, a) + trade(jnp.where(is_far, a, b), *far_z)
    y = three_terms(y, at_misc - (2 * half - n), core + upper_x + upper_z + upper_far == 4)
    got = trade(y, *far_z)
    a, b = jnp.where(is_far, got, y), jnp.where(is_far, y, got)
    a, b = ordered(a, trade(a, *z), *z), ordered(b, trade(b, *x), *x)
    a, b = ordered(a, trade(a, *x), *x), ordered(b, trade(b, *z), *z)
    return jnp.concatenate([a, b])


def finish_kernel(
    at_misc,
    bits, mine, other,
    joint, code, volume, flow, b_volume, b_code, b_flow, b_joint, head, loss, b_head,
    full,
):
    half, C = mine.shape
    full[pl.ds(pl.multiple_of(bits[0] * half, 16), half), :] = mine[...]
    full[pl.ds(pl.multiple_of((1 - bits[0]) * half, 16), half), :] = other[...]
    for i in range(3):
        for j in range(3):
            at = (i * 3 + j) * 2 * C
            joint[i, j, :, :] = full[at : at + 2 * C, :].astype(F32)
            at = AT_CODE + (i * 3 + j) * C
            code[i, j, :, :] = full[at : at + C, :].astype(F32)
    parts = full[AT_VOLUME:AT_FLOW, :].astype(F32)
    for half_at in range(2):
        for dy in range(SIDE):
            at, to = half_at * HALF, half_at * OFF + dy * SIDE
            volume[to : to + 8, :] = parts[at + 8 * dy : at + 8 * dy + 8]
            volume[to + 8 : to + 9, :] = parts[at + 72 + dy : at + 73 + dy]
    for i in range(7):
        part = full[AT_FLOW + 16 * i : AT_FLOW + 16 * i + 16, :].astype(F32)
        for j in range(7):
            flow[i, j, :, :] = part[2 * j : 2 * j + 2]
    terms = full[at_misc : at_misc + 32, :].astype(F32)
    misc = terms[0:8] + terms[8:16] + terms[16:24]
    for k, ref in enumerate((b_volume, b_code, b_flow, b_joint)):
        ref[...] = misc[k]
    head[...] = misc[4:6]
    lane = lax.broadcasted_iota(jnp.int32, (1, C), 1)
    loss[0] = jnp.sum(jnp.where(lane == 0, misc[6:7], 0.0))
    b_head[0] = jnp.sum(jnp.where(lane == 1, misc[6:7], 0.0))
    b_head[1] = jnp.sum(jnp.where(lane == 2, misc[6:7], 0.0))


def call(body, name, out_shape, in_specs, scratch, flops, *args, out_specs=None):
    held = [
        x if spec is SMEM else pltpu.with_memory_space_constraint(x, spec.memory_space)
        for x, spec in zip(args, in_specs, strict=True)
    ]
    return pl.pallas_call(
        body,
        out_shape=out_shape,
        in_specs=in_specs,
        out_specs=out_specs or jax.tree.map(lambda _: VMEM, out_shape),
        scratch_shapes=scratch,
        cost_estimate=pl.CostEstimate(flops=flops, bytes_accessed=flops // 300, transcendentals=0),
        compiler_params=pltpu.CompilerParams(vmem_limit_bytes=16 << 20),
        name=name,
    )(*held)


def local(
    features, pair_order, flow_now, targets, w_volume, b_volume, w_code, b_code,
    w_flow, b_flow, w_joint, b_joint, w_head, b_head,
):
    own = features[0]
    n_rows, n_cols, n_chan = own.shape
    n_code = w_code.shape[3]
    W, C = n_cols, n_code
    body = n_rows * n_cols
    halo = HALO * n_cols
    n_tm, n_space = lax.axis_size("tm"), lax.axis_size("space")
    flat = own.reshape(body, n_chan)
    both = ("tm", "space")

    def route(partner, ds):
        pairs = []
        for t in range(n_tm):
            for s in range(n_space):
                if 0 <= partner(t) < n_tm and 0 <= s + ds < n_space:
                    pairs.append((t * n_space + s, partner(t) * n_space + s + ds))
        return pairs

    def near(t):
        return t + 1 - 2 * (t % 2)

    def far(t):
        return t - 1 + 2 * (t % 2)

    first, last = flat[:halo], flat[body - halo :]
    near_mid = lax.ppermute(flat, both, route(near, 0))
    far_mid = lax.ppermute(flat, both, route(far, 0))
    near_top = lax.ppermute(last, both, route(near, 1))
    near_bot = lax.ppermute(first, both, route(near, -1))

    def down_column(ds):
        return [(a, b + ds) for a, b in route(lambda t: t, 0) if 0 <= far(a // n_space) < n_tm and 0 <= b % n_space + ds < n_space]

    far_top = lax.ppermute(far_mid[body - halo :], both, down_column(1))
    far_bot = lax.ppermute(far_mid[:halo], both, down_column(-1))

    def shape(*dims, dtype=BF):
        return pltpu.VMEM(dims, dtype)

    def result(*dims):
        return jax.ShapeDtypeStruct(dims, F32)

    near_vol, held, flow, held_targets, wc, bias, wv, wcb, wj, wjb, wf, wht = call(
        functools.partial(near_kernel, n_rows, n_cols), "near",
        (
            shape(HALF, body), shape(body, n_chan), shape(*flow_now.shape[1:]),
            shape(*targets.shape[1:], dtype=jnp.int32), shape(3, 3, C, C), shape(4, C, dtype=F32),
            shape(2 * HALF, C), shape(C, 9 * C), shape(18 * C, C),
            shape(2 * C, 9 * C), shape(112, C), shape(48, C),
        ),
        [HBM] * 11 + [VMEM] * 4,
        [
            pltpu.VMEM((body + 2 * halo, n_chan), BF),
            pltpu.VMEM((HALF, 2 * W), F32),
            pltpu.VMEM((2 * HALF, C), F32),
            pltpu.VMEM(w_volume.shape, BF),
            pltpu.VMEM(w_joint.shape, BF),
            pltpu.VMEM(w_flow.shape, BF),
            pltpu.SemaphoreType.DMA((11,)),
        ],
        4_000_000_000,
        flat, flow_now[0], targets[0], w_volume, w_code, w_joint, w_flow, b_volume, b_code, b_flow, b_joint,
        near_mid, near_top, near_bot, w_head.T,
    )
    vol, code, up, dn = call(
        functools.partial(code_kernel, n_rows, n_cols), "code",
        (shape(2 * HALF, body), shape(body, C), shape(halo + 16, C), shape(halo + 16, C)),
        [SMEM] + [VMEM] * 9,
        [
            pltpu.VMEM((body + 2 * halo, n_chan), BF),
            pltpu.VMEM((HALF, 2 * W), F32),
            pltpu.VMEM((16, W), F32),
        ],
        4_000_000_000,
        pair_order, held, far_mid, far_top, far_bot, near_vol, wv, bias, flow, held_targets,
    )
    top = lax.ppermute(dn, "space", [(s, s + 1) for s in range(n_space - 1)])
    bot = lax.ppermute(up, "space", [(s + 1, s) for s in range(n_space - 1)])

    d_code, code_t = call(
        code_slope_kernel, "slope", (shape(body, C, dtype=F32), shape(C, body)), [VMEM] * 4, [], 500_000_000,
        vol, wv, bias, code,
    )
    jf, d_flow, xb, tgt = call(
        functools.partial(flow_kernel, n_rows, n_cols), "flow",
        (
            shape((n_rows + 6) * W, 3 * C),
            shape((n_rows + 6) * W, C, dtype=F32),
            shape((n_rows + 12) * 16, W),
            shape(16, (n_rows + 4) * W, dtype=F32),
        ),
        [VMEM] * 6,
        [
            pltpu.VMEM((24, W), F32),
            pltpu.VMEM(((n_rows + 12) * 16, W), F32),
        ],
        1_000_000_000,
        top, bot, flow, held_targets, wf, bias,
    )
    flow_error, jt, s3, d_motion, misc = call(
        functools.partial(hidden_kernel, n_rows, n_cols, n_tm), "hidden",
        (
            result(2, n_rows, W),
            shape(2 * C, body),
            shape((n_rows + 4) * W, 3 * C),
            shape((n_rows + 6) * W, C, dtype=F32),
            shape(MISC_ROWS, C, dtype=F32),
        ),
        [SMEM] + [VMEM] * 9,
        [
            pltpu.VMEM(((n_rows + 8) * W, 3 * C), BF),
            pltpu.VMEM(((n_rows + 6) * W, 3 * C), BF),
            pltpu.VMEM((16, (n_rows + 4) * W), F32),
            pltpu.VMEM(((n_rows + 4) * W, C), BF),
            pltpu.VMEM((48, C), F32),
            pltpu.VMEM((8, C), F32),
        ],
        4_000_000_000,
        b_head, code, top, bot, jf, tgt, wc.reshape(9 * C, C), wj, wht, bias,
    )
    n_dev = n_tm * n_space
    paired = n_tm == 4 and n_space == 4
    if paired:
        grad_rows, at_misc = 3840, AT_END
    else:
        chunk = -(-max(pl.cdiv(AT_END, n_dev - 1), 3 * MISC_ROWS) // 16) * 16
        grad_rows, at_misc = n_dev * chunk, (n_dev - 1) * chunk
    keep, send = call(
        functools.partial(rest_kernel, n_rows, n_cols, at_misc), "rest",
        (shape(grad_rows // 2, C, dtype=F32), shape(grad_rows // 2, C, dtype=F32)),
        [VMEM] * 11,
        [
            pltpu.VMEM(((n_rows + 2) * W, 3 * C), BF),
            pltpu.VMEM(((n_rows + 2) * W, C), BF),
            pltpu.VMEM((body, C), BF),
            pltpu.VMEM((24, C), F32),
            pltpu.VMEM((grad_rows, C), F32),
        ],
        3_000_000_000,
        jt, s3, d_motion, d_flow, xb, vol, d_code, code_t, misc, wcb, wjb,
    )
    core = ("tm", 1)
    got = trade(send, *core)
    bits = jnp.stack([upper_of("tm", 1), upper_of("tm", 2), upper_of("space", 1), upper_of("space", 2)])
    bits = bits.astype(jnp.int32)
    if paired:
        mine = paired_reduce(keep + got, at_misc)
    else:
        mine = halving_reduce(keep + got, bits_of("tm")[1:] + bits_of("space"), upper_of(*core))
    other = trade(mine, *core)
    outs = call(
        functools.partial(finish_kernel, at_misc), "finish",
        (
            result(3, 3, 2 * C, C),
            result(3, 3, C, C),
            result(2 * OFF, C),
            result(7, 7, 2, C),
            result(C), result(C), result(C), result(C),
            result(2, C), result(1), result(2),
        ),
        [SMEM] + [VMEM] * 2, [pltpu.VMEM((grad_rows, C), BF)], 100_000_000,
        bits, mine, other,
        out_specs=(VMEM,) * 9 + (SMEM,) * 2,
    )
    joint, g_code, g_volume, g_flow, g_bv, g_bc, g_bf, g_bj, head, loss, g_b_head = outs
    return loss, flow_error[None], g_volume, g_bv, g_code, g_bc, g_flow, g_bf, joint, g_bj, head.T, g_b_head


def solution(mesh):
    placed = (
        P(("groups", "tm"), "space", None, None),
        P(("groups", "tm")),
        P(("groups", "tm"), None, "space", None),
        P(("groups", "tm"), None, "space", None),
    ) + (P(),) * 10
    return jax.shard_map(
        local,
        mesh=mesh,
        in_specs=placed,
        out_specs=(
            P("groups"),
            P(("groups", "tm"), None, "space", None),
            P("groups", None),
            P("groups"),
            P("groups", None, None, None),
            P("groups"),
            P("groups", None, None, None),
            P("groups"),
            P("groups", None, None, None),
            P("groups"),
            P("groups", None),
            P("groups"),
        ),
        check_vma=False,
    )
```

```python
import functools

import jax
import jax.numpy as jnp
from jax import lax
from jax.experimental import pallas as pl
from jax.experimental.pallas import tpu as pltpu
from jax.sharding import PartitionSpec as P

BF = jnp.bfloat16
F32 = jnp.float32
RADIUS = 4
SIDE = 2 * RADIUS + 1
OFF = SIDE * SIDE
HALO = 4
FLOW_HALO = 6
TARGET_HALO = 2
NT = (((1,), (1,)), ((), ()))
TN = (((0,), (0,)), ((), ()))

AT_CODE = 2304
AT_VOLUME = 3456
AT_FLOW = 3648
AT_END = 3760
HALF = 96
MOTION_BLOCK = 7
HIDDEN_BLOCK = 12
SLOPE_BLOCK = 10
CODE_BLOCK = 4
MISC_ROWS = 8


def dot(a, b):
    return jnp.dot(a, b, preferred_element_type=F32)


def dot_nt(a, b):
    return lax.dot_general(a, b, NT, preferred_element_type=F32)


def rows(start, count, unit):
    return pl.ds(pl.multiple_of(start * unit, unit), count * unit)


def split3(s, padded=False):
    hi = s.astype(BF).astype(F32)
    mid = (s - hi).astype(BF).astype(F32)
    terms = [hi, mid, s - hi - mid] + [jnp.zeros_like(s)] * padded
    return jnp.concatenate(terms, axis=0).astype(BF)


def silu_pair(v):
    s = jax.nn.sigmoid(v)
    return v * s, s * (1.0 + v * (1.0 - s))


def correlate(n_rows, n_cols, own, mid, top, bot, out, out_at, near, rows_f):
    n_chan = own.shape[1]
    halo = RADIUS * n_cols
    body = n_rows * n_cols
    near[0:halo, :] = top[...]
    near[halo : halo + body, :] = mid[...]
    near[halo + body :, :] = bot[...]
    W = n_cols
    j_at = lax.broadcasted_iota(jnp.int32, (W, 2 * W), 0)
    x_at = lax.broadcasted_iota(jnp.int32, (W, 2 * W), 1) & (W - 1)
    band = jnp.logical_and(j_at - x_at >= -RADIUS, j_at - x_at < RADIUS)
    edge = j_at - x_at == RADIUS
    turn = lax.broadcasted_iota(jnp.int32, (8, 2 * W), 1) + RADIUS
    scale = n_chan ** (-0.5)

    def fold(v):
        parts = [v[8 * g : 8 * g + 8] for g in range(W // 8)]
        while len(parts) > 1:
            parts = [parts[k] + parts[k + 1] for k in range(0, len(parts), 2)]
        return parts[0]

    def two_rows(b, carry):
        tile = own[rows(2 * b, 2, W), :]
        rows_f[...] = jnp.zeros_like(rows_f)
        for q in range(SIDE + 1):
            scores = lax.dot_general(
                near[rows(2 * b + q, 1, W), :], tile, NT, preferred_element_type=F32
            )
            inner = fold(jnp.where(band, scores, 0.0))
            outer = jnp.sum(fold(jnp.where(edge, scores, 0.0)), axis=0, keepdims=True)
            for bit in (1, 2, 4):
                inner = jnp.where((turn & bit) != 0, pltpu.roll(inner, 8 - bit, 0), inner)
            for u in range(2):
                dy = q - u
                if 0 <= dy < SIDE:
                    rows_f[8 * dy : 8 * dy + 8, u * W : (u + 1) * W] = inner[:, u * W : (u + 1) * W]
                    rows_f[72 + dy : 73 + dy, u * W : (u + 1) * W] = outer[:, u * W : (u + 1) * W]
        out[out_at, rows(2 * b, 2, W)] = (rows_f[...] * scale).astype(BF)
        return carry

    lax.fori_loop(0, n_rows // 2, two_rows, 0)


def near_kernel(
    n_rows, n_cols,
    own_hbm, flow_hbm, targets_hbm, volume_hbm, code_hbm, joint_hbm, w_flow_hbm, bv_hbm, bc_hbm, bf_hbm, bj_hbm,
    mid, top, bot, head,
    out, own, flow, targets, w_code, bias, wv, wcb, wj, wjb, wf, wht,
    near, rows_f, wide, w_volume, w_joint, w_flow, sems,
):
    loads = (
        (own_hbm, own), (flow_hbm, flow), (targets_hbm, targets), (volume_hbm, w_volume), (code_hbm, w_code),
        (joint_hbm, w_joint), (w_flow_hbm, w_flow), (bv_hbm, bias.at[0]), (bc_hbm, bias.at[1]),
        (bf_hbm, bias.at[2]), (bj_hbm, bias.at[3]),
    )
    copies = [pltpu.make_async_copy(src, dst, sems.at[k]) for k, (src, dst) in enumerate(loads)]
    for copy in copies:
        copy.start()
    copies[0].wait()
    correlate(n_rows, n_cols, own, mid, top, bot, out, slice(None), near, rows_f)
    for copy in copies[1:]:
        copy.wait()
    C = w_code.shape[3]
    wide[...] = jnp.zeros_like(wide)
    weight = w_volume[...].astype(F32)
    for half in range(2):
        for dy in range(SIDE):
            at = half * OFF + dy * SIDE
            wide[half * HALF + 8 * dy : half * HALF + 8 * dy + 8, :] = weight[at : at + 8]
            wide[half * HALF + 72 + dy : half * HALF + 73 + dy, :] = weight[at + 8 : at + 9]
    wv[...] = wide[...].astype(BF)
    wide[...] = jnp.zeros_like(wide)
    for i in range(7):
        for j in range(7):
            wide[16 * i + 2 * j : 16 * i + 2 * j + 2, :] = w_flow[i, j].astype(F32)
    wf[...] = wide[0:112, :].astype(BF)
    for i in range(3):
        for j in range(3):
            at = (3 * i + j) * C
            wcb[:, at : at + C] = w_code[i, j]
            wjb[:, at : at + C] = w_joint[i, j]
            for part in range(2):
                at = (2 * i + part) * 3 * C + j * C
                wj[at : at + C, :] = w_joint[i, j, part * C : (part + 1) * C, :]
    wide[...] = jnp.zeros_like(wide)
    for k in range(3):
        wide[16 * k : 16 * k + 2, :] = head[...].astype(F32)
    wht[...] = wide[0:48, :].astype(BF)


def code_kernel(
    n_rows, n_cols,
    order, own, mid, top, bot, near_vol, wv, bias, flow, targets,
    vol, code, up, dn,
    near, rows_f, edge,
):
    W = n_cols
    halo = HALO * W
    body = n_rows * W
    near_second = (order[0] != lax.axis_index("tm") % 2).astype(jnp.int32)
    near_at = pl.multiple_of(near_second * HALF, HALF)
    far_at = pl.multiple_of((1 - near_second) * HALF, HALF)
    vol[pl.ds(near_at, HALF), :] = near_vol[...]
    correlate(n_rows, n_cols, own, mid, top, bot, vol, pl.ds(far_at, HALF), near, rows_f)

    def one_code(r, carry):
        at = rows(r, CODE_BLOCK, W)
        pre = lax.dot_general(vol[:, at], wv[...], TN, preferred_element_type=F32) + bias[0:1, :]
        code[at, :] = (pre * jax.nn.sigmoid(pre)).astype(BF)
        return carry

    lax.fori_loop(0, n_rows // CODE_BLOCK, lambda r, c: one_code(CODE_BLOCK * r, c), 0)
    for ref, at, flow_at, target_at in (
        (up, 0, 0, 0),
        (dn, body - halo, n_rows - FLOW_HALO, n_rows - TARGET_HALO),
    ):
        ref[0:halo, :] = code[at : at + halo, :]
        for k in range(2):
            edge[8 * k : 8 * k + FLOW_HALO, :] = flow[k].astype(F32)[flow_at : flow_at + FLOW_HALO]
            edge[8 * k + FLOW_HALO : 8 * k + 8, :] = targets[k].astype(F32)[target_at : target_at + TARGET_HALO]
        ref[halo : halo + 16, :] = edge[...].astype(BF)


def frame_scale(n_tm, per):
    frame = lax.axis_index("tm")
    value = jnp.float32(per)
    for t in range(n_tm - 1):
        value = jnp.where(frame == t, jnp.float32(per * 0.25 ** ((n_tm - 1 - t) / (n_tm - 1))), value)
    return value


def code_slope_kernel(vol, wv, bias, code, d_code, code_t):
    pre = lax.dot_general(vol[...], wv[...], TN, preferred_element_type=F32) + bias[0:1, :]
    d_code[...] = silu_pair(pre)[1]
    code_t[...] = code[...].T


def inside_frame(n_rows, ext):
    at = lax.axis_index("space") * n_rows + ext
    return jnp.logical_and(at >= 0, at < lax.axis_size("space") * n_rows)


def store_stack(ref, at, v, cols):
    W, C = v.shape
    x_at = lax.broadcasted_iota(jnp.int32, (W, C), 0)
    left = jnp.where(x_at == 0, 0.0, pltpu.roll(v, 1, 0))
    right = jnp.where(x_at == W - 1, 0.0, pltpu.roll(v, W - 1, 0))
    for col, part in zip(cols, (left, v, right)):
        ref[rows(at, 1, W), col * C : (col + 1) * C] = part.astype(BF)


FWD = (0, 1, 2)
BWD = (2, 1, 0)


def flow_kernel(n_rows, n_cols, top, bot, flow, targets, wf, bias, jf, d_flow, xb, tgt, xf, xx):
    W = n_cols
    halo = HALO * W
    xx[...] = jnp.zeros_like(xx)
    above = top[halo : halo + 16, :].astype(F32)
    below = bot[halo : halo + 16, :].astype(F32)
    n_flow = n_rows + 2 * FLOW_HALO
    lane = lax.broadcasted_iota(jnp.int32, (n_flow, W), 1)
    for k in range(2):
        xf[0:FLOW_HALO, :] = above[8 * k : 8 * k + FLOW_HALO, :]
        xf[FLOW_HALO : FLOW_HALO + n_rows, :] = flow[k].astype(F32)
        xf[FLOW_HALO + n_rows : n_flow, :] = below[8 * k : 8 * k + FLOW_HALO, :]
        own_flow = xf[0:n_flow, :]
        for j in range(7):
            shift = (3 - j) % W
            moved = pltpu.roll(own_flow, shift, 1) if shift else own_flow
            ok = jnp.logical_and(lane + (j - 3) >= 0, lane + (j - 3) < W)
            xx[pl.ds(j * 2 + k, n_flow, stride=16), :] = jnp.where(ok, moved, 0.0)
    xb[...] = xx[...].astype(BF)
    tgt[...] = jnp.zeros_like(tgt)
    for k in range(2):
        for y in range(TARGET_HALO):
            tgt[k : k + 1, y * W : (y + 1) * W] = above[8 * k + 6 + y : 8 * k + 7 + y, :]
            lo = (TARGET_HALO + n_rows + y) * W
            tgt[k : k + 1, lo : lo + W] = below[8 * k + 6 + y : 8 * k + 7 + y, :]
        for y in range(n_rows):
            lo = (TARGET_HALO + y) * W
            tgt[k : k + 1, lo : lo + W] = targets[k, y : y + 1, :].astype(F32)

    def flow_rows(b, carry):
        y = b * MOTION_BLOCK
        patches = [xb[pl.ds(pl.multiple_of((y + u) * 16, 16), 112), :] for u in range(MOTION_BLOCK)]
        pre = lax.dot_general(jnp.concatenate(patches, axis=1), wf[...], TN, preferred_element_type=F32)
        for u in range(MOTION_BLOCK):
            value, slope = silu_pair(pre[u * W : (u + 1) * W] + bias[2:3, :])
            d_flow[rows(y + u, 1, W), :] = slope
            store_stack(jf, y + u, jnp.where(inside_frame(n_rows, y + u - 3), value, 0.0), FWD)
        return carry

    lax.fori_loop(0, (n_rows + 6) // MOTION_BLOCK, flow_rows, 0)


def hidden_kernel(
    n_rows, n_cols, n_tm,
    b_head, code, top, bot, jf, tgt, wc, wj, wht, bias,
    error_out, jt, s3, d_motion, misc,
    c3, jm, err, hid, g_head, acc,
):
    W = n_cols
    count = 2.0 * n_tm * lax.axis_size("space") * n_rows * n_cols
    slope_scale = frame_scale(n_tm, 2.0 / count)
    C = wc.shape[1]
    body = n_rows * W

    def load_halo(y, carry):
        store_stack(c3, y, top[rows(y, 1, W), :].astype(F32), FWD)
        store_stack(c3, y + HALO + n_rows, bot[rows(y, 1, W), :].astype(F32), FWD)
        return carry

    def load_code(y, carry):
        store_stack(c3, y + HALO, code[rows(y, 1, W), :].astype(F32), FWD)
        return carry

    lax.fori_loop(0, HALO, load_halo, 0)
    lax.fori_loop(0, n_rows, load_code, 0)

    def motion_rows(b, carry):
        y = b * MOTION_BLOCK
        taps = jnp.concatenate([c3[rows(y + i, MOTION_BLOCK, W), :] for i in range(3)], axis=1)
        pre = dot(taps, wc[...]) + bias[1:2, :]
        for u in range(MOTION_BLOCK):
            value, slope = silu_pair(pre[u * W : (u + 1) * W])
            d_motion[rows(y + u, 1, W), :] = slope
            store_stack(jm, y + u, jnp.where(inside_frame(n_rows, y + u - 3), value, 0.0), FWD)
        return carry

    lax.fori_loop(0, (n_rows + 6) // MOTION_BLOCK, motion_rows, 0)

    block = HIDDEN_BLOCK
    k_row = lax.broadcasted_iota(jnp.int32, (16, block * W), 0)
    b_col = jnp.where(k_row == 0, b_head[0], jnp.where(k_row == 1, b_head[1], 0.0))

    def hidden_rows(b, carry):
        y = b * block
        taps = [ref[rows(y + i, block, W), :] for i in range(3) for ref in (jm, jf)]
        pre = dot(jnp.concatenate(taps, axis=1), wj[...]) + bias[3:4, :]
        value, slope = silu_pair(pre)
        hidden = value.astype(BF)
        hid[rows(y, block, W), :] = hidden
        pred = lax.dot_general(wht[0:16, :], hidden, NT, preferred_element_type=F32)
        error = pred + b_col - tgt[:, rows(y, block, W)]
        err[:, rows(y, block, W)] = error
        back = lax.dot_general(split3(error * slope_scale), wht[...], TN, preferred_element_type=F32) * slope
        for u in range(block):
            v = jnp.where(inside_frame(n_rows, y + u - 2), back[u * W : (u + 1) * W], 0.0)
            store_stack(s3, y + u, v, BWD)
        return carry

    lax.fori_loop(0, (n_rows + 4) // block, hidden_rows, 0)

    acc[...] = jnp.zeros_like(acc)
    g_head[...] = jnp.zeros_like(g_head)

    def own_rows(b, carry):
        y = 2 * b
        g_head[...] += dot(split3(err[:, rows(y + 2, 2, W)] * slope_scale), hid[rows(y + 2, 2, W), :])
        part = s3[rows(y + 2, 2, W), C : 2 * C].astype(F32)
        acc[...] += jnp.sum(part.reshape(2 * W // 8, 8, C), axis=0)
        jt[0:C, rows(y, 2, W)] = jm[rows(y + 3, 2, W), C : 2 * C].T
        jt[C : 2 * C, rows(y, 2, W)] = jf[rows(y + 3, 2, W), C : 2 * C].T
        return carry

    lax.fori_loop(0, n_rows // 2, own_rows, 0)
    own = err[:, TARGET_HALO * W : TARGET_HALO * W + body]
    for k in range(2):
        for y in range(n_rows):
            error_out[k, y : y + 1, :] = own[k : k + 1, y * W : (y + 1) * W]
    g_b_head = jnp.sum(own * slope_scale, axis=1, keepdims=True)
    loss = jnp.sum(jnp.sum(own * own, axis=1, keepdims=True), axis=0, keepdims=True)
    loss = loss * frame_scale(n_tm, 1.0 / count)
    col = lax.broadcasted_iota(jnp.int32, (1, C), 1)
    tail = jnp.where(col == 0, loss, jnp.where(col == 1, g_b_head[0:1], jnp.where(col == 2, g_b_head[1:2], 0.0)))
    misc[0:3, :] = jnp.zeros((3, C), F32)
    misc[3:4, :] = jnp.sum(acc[...], axis=0, keepdims=True)
    misc[4:6, :] = g_head[0:2, :] + g_head[16:18, :] + g_head[32:34, :]
    misc[6:7, :] = tail
    misc[7:8, :] = jnp.zeros((1, C), F32)


def rest_kernel(
    n_rows, n_cols, at_misc,
    jt, s3, d_motion, d_flow, xb, vol, d_code, code_t, misc, wcb, wjb,
    keep, send,
    m3, s_flow, s_code, acc, grads,
):
    W = n_cols
    C = d_code.shape[1]
    body = n_rows * W

    def joint_slopes(b, carry):
        y = b * SLOPE_BLOCK
        taps = jnp.concatenate([s3[rows(y + 2 - i, SLOPE_BLOCK, W), :] for i in range(3)], axis=1)
        sj = dot_nt(taps, wjb[...])
        for u in range(SLOPE_BLOCK):
            part = sj[u * W : (u + 1) * W]
            v = part[:, 0:C] * d_motion[rows(y + u + 2, 1, W), :]
            store_stack(m3, y + u, jnp.where(inside_frame(n_rows, y + u - 1), v, 0.0), BWD)
            s_flow[rows(y + u, 1, W), :] = (part[:, C:] * d_flow[rows(y + u + 2, 1, W), :]).astype(BF)
        return carry

    lax.fori_loop(0, (n_rows + 2) // SLOPE_BLOCK, joint_slopes, 0)
    acc[...] = jnp.zeros_like(acc)

    def add_rows(k, v):
        acc[8 * k : 8 * k + 8, :] += jnp.sum(v.reshape(v.shape[0] // 8, 8, C), axis=0)

    def code_slopes(b, carry):
        y = b * CODE_BLOCK
        at = rows(y, CODE_BLOCK, W)
        taps = jnp.concatenate([m3[rows(y + 2 - i, CODE_BLOCK, W), :] for i in range(3)], axis=1)
        sc = dot_nt(taps, wcb[...])
        slope = (sc * d_code[at, :]).astype(BF)
        s_code[at, :] = slope
        add_rows(0, slope.astype(F32))
        add_rows(1, m3[rows(y + 1, CODE_BLOCK, W), C : 2 * C].astype(F32))
        add_rows(2, s_flow[rows(y + 1, CODE_BLOCK, W), :].astype(F32))
        return carry

    lax.fori_loop(0, n_rows // CODE_BLOCK, code_slopes, 0)

    for i in range(3):
        g = dot(jt[...], s3[(3 - i) * W : (3 - i) * W + body, :])
        for j in range(3):
            at = (i * 3 + j) * 2 * C
            grads[at : at + 2 * C, :] = g[:, j * C : (j + 1) * C]
    for i in range(3):
        g = dot(code_t[...], m3[(2 - i) * W : (2 - i) * W + body, :])
        for j in range(3):
            at = AT_CODE + (i * 3 + j) * C
            grads[at : at + C, :] = g[:, j * C : (j + 1) * C]
    grads[AT_VOLUME:AT_FLOW, :] = dot(vol[...], s_code[...])
    gf = jnp.zeros((112, C), F32)
    for y in range(n_rows):
        gf = gf + dot(xb[(y + 3) * 16 : (y + 3) * 16 + 112, :], s_flow[(y + 1) * W : (y + 2) * W, :])
    grads[AT_FLOW : AT_FLOW + 112, :] = gf
    if at_misc > AT_END:
        grads[AT_END:at_misc, :] = jnp.zeros((at_misc - AT_END, C), F32)
    for k in range(3):
        grads[at_misc + k : at_misc + k + 1, :] = jnp.sum(acc[8 * k : 8 * k + 8, :], axis=0, keepdims=True)
    grads[at_misc + 3 : at_misc + 8, :] = misc[3:8, :]
    grads[at_misc + 8 :, :] = jnp.zeros((grads.shape[0] - at_misc - 8, C), F32)
    half = keep.shape[0]
    core = lax.axis_index("tm") % 2
    keep[...] = pick(grads, core, half)
    send[...] = pick(grads, 1 - core, half)


VMEM = pl.BlockSpec(memory_space=pltpu.VMEM)
SMEM = pl.BlockSpec(memory_space=pltpu.SMEM)
HBM = pl.BlockSpec(memory_space=pltpu.HBM)


def bits_of(axis):
    bits = []
    bit = 1
    while bit < lax.axis_size(axis):
        bits.append((axis, bit))
        bit *= 2
    return bits


def trade(x, axis, bit):
    return lax.ppermute(x, axis, [(i, i ^ bit) for i in range(lax.axis_size(axis))])


def upper_of(axis, bit):
    return (lax.axis_index(axis) // bit) % 2


def three_terms(x, at, is_last):
    value = x[at : at + MISC_ROWS]
    mid = value - lax.reduce_precision(value, 8, 7)
    low = mid - lax.reduce_precision(mid, 8, 7)
    terms = jnp.concatenate([x[: at + MISC_ROWS], mid, low, x[at + 3 * MISC_ROWS :]])
    return jnp.where(is_last, terms, x).astype(BF)


def halving_reduce(x, steps, is_last):
    for axis, bit in steps:
        upper = upper_of(axis, bit)
        is_last = is_last * upper
        half = x.shape[0] // 2
        mine = lax.dynamic_slice_in_dim(x, upper * half, half, 0)
        other = lax.dynamic_slice_in_dim(x, (1 - upper) * half, half, 0)
        x = mine + trade(other, axis, bit)
    x = three_terms(x, 0, is_last == 1)
    for axis, bit in steps[::-1]:
        got = trade(x, axis, bit)
        x = jnp.where(upper_of(axis, bit) == 0, jnp.concatenate([x, got]), jnp.concatenate([got, x]))
    return x


def pick(ref, which, half):
    return ref[pl.ds(pl.multiple_of(which * half, 8), half), :]


def cut(x, which, n):
    return lax.dynamic_slice_in_dim(x, which * n, n, 0)


def ordered(mine, got, axis, bit):
    return jnp.where(upper_of(axis, bit) == 0, jnp.concatenate([mine, got]), jnp.concatenate([got, mine]))


def add_terms(x, got, at, holds):
    misc = x[at : at + MISC_ROWS] + sum(got[at + k * MISC_ROWS : at + (k + 1) * MISC_ROWS] for k in range(3))
    fixed = jnp.concatenate([misc, jnp.zeros((2 * MISC_ROWS, misc.shape[1]), F32)])
    x = x + got
    return jnp.concatenate([x[:at], jnp.where(holds, fixed, x[at : at + 3 * MISC_ROWS]), x[at + 3 * MISC_ROWS :]])


def paired_reduce(x_sum, at_misc):
    half = x_sum.shape[0]
    x, z, far_z = ("tm", 2), ("space", 1), ("space", 2)
    upper_x, upper_z, upper_far, core = upper_of(*x), upper_of(*z), upper_of(*far_z), upper_of("tm", 1)
    a, b = x_sum[: half // 2], x_sum[half // 2 :]
    n = half // 4
    at = at_misc - 2 * half + n
    sends = jnp.logical_and(core == 1, upper_z == 0)
    holds = jnp.logical_and(core == 1, upper_z == 1)
    a_got = trade(cut(a, 1 - upper_x, n).astype(BF), *x)
    b_got = trade(three_terms(cut(b, 1 - upper_z, n), at, sends), *z)
    a = cut(a, upper_x, n) + a_got.astype(F32)
    b = add_terms(cut(b, upper_z, n), b_got.astype(F32), at, holds)
    n = half // 8
    a_got, b_got = trade(cut(a, 1 - upper_z, n), *z), trade(cut(b, 1 - upper_x, n), *x)
    a, b = cut(a, upper_z, n) + a_got, cut(b, upper_x, n) + b_got
    is_far = upper_far == 1
    at = at_misc - (2 * half - n)
    corner = core + upper_x + upper_z
    sent = three_terms(jnp.where(is_far, a, b), at, corner - upper_far == 3)
    y = add_terms(jnp.where(is_far, b, a), trade(sent, *far_z).astype(F32), at, corner + upper_far == 4)
    y = three_terms(y, at, corner + upper_far == 4)
    got = trade(y, *far_z)
    a, b = jnp.where(is_far, got, y), jnp.where(is_far, y, got)
    a, b = ordered(a, trade(a, *z), *z), ordered(b, trade(b, *x), *x)
    a, b = ordered(a, trade(a, *x), *x), ordered(b, trade(b, *z), *z)
    return jnp.concatenate([a, b])


def finish_kernel(
    at_misc,
    bits, mine, other,
    joint, code, volume, flow, b_volume, b_code, b_flow, b_joint, head, loss, b_head,
    full,
):
    half, C = mine.shape
    full[pl.ds(pl.multiple_of(bits[0] * half, 16), half), :] = mine[...]
    full[pl.ds(pl.multiple_of((1 - bits[0]) * half, 16), half), :] = other[...]
    for i in range(3):
        for j in range(3):
            at = (i * 3 + j) * 2 * C
            joint[i, j, :, :] = full[at : at + 2 * C, :].astype(F32)
            at = AT_CODE + (i * 3 + j) * C
            code[i, j, :, :] = full[at : at + C, :].astype(F32)
    parts = full[AT_VOLUME:AT_FLOW, :].astype(F32)
    for half_at in range(2):
        for dy in range(SIDE):
            at, to = half_at * HALF, half_at * OFF + dy * SIDE
            volume[to : to + 8, :] = parts[at + 8 * dy : at + 8 * dy + 8]
            volume[to + 8 : to + 9, :] = parts[at + 72 + dy : at + 73 + dy]
    for i in range(7):
        part = full[AT_FLOW + 16 * i : AT_FLOW + 16 * i + 16, :].astype(F32)
        for j in range(7):
            flow[i, j, :, :] = part[2 * j : 2 * j + 2]
    terms = full[at_misc : at_misc + 32, :].astype(F32)
    misc = terms[0:8] + terms[8:16] + terms[16:24]
    for k, ref in enumerate((b_volume, b_code, b_flow, b_joint)):
        ref[...] = misc[k]
    head[...] = misc[4:6]
    lane = lax.broadcasted_iota(jnp.int32, (1, C), 1)
    loss[0] = jnp.sum(jnp.where(lane == 0, misc[6:7], 0.0))
    b_head[0] = jnp.sum(jnp.where(lane == 1, misc[6:7], 0.0))
    b_head[1] = jnp.sum(jnp.where(lane == 2, misc[6:7], 0.0))


def call(body, name, out_shape, in_specs, scratch, flops, *args, out_specs=None):
    held = [
        x if spec is SMEM else pltpu.with_memory_space_constraint(x, spec.memory_space)
        for x, spec in zip(args, in_specs, strict=True)
    ]
    return pl.pallas_call(
        body,
        out_shape=out_shape,
        in_specs=in_specs,
        out_specs=out_specs or jax.tree.map(lambda _: VMEM, out_shape),
        scratch_shapes=scratch,
        cost_estimate=pl.CostEstimate(flops=flops, bytes_accessed=flops // 300, transcendentals=0),
        compiler_params=pltpu.CompilerParams(vmem_limit_bytes=16 << 20),
        name=name,
    )(*held)


def local(
    features, pair_order, flow_now, targets, w_volume, b_volume, w_code, b_code,
    w_flow, b_flow, w_joint, b_joint, w_head, b_head,
):
    own = features[0]
    n_rows, n_cols, n_chan = own.shape
    n_code = w_code.shape[3]
    W, C = n_cols, n_code
    body = n_rows * n_cols
    halo = HALO * n_cols
    n_tm, n_space = lax.axis_size("tm"), lax.axis_size("space")
    flat = own.reshape(body, n_chan)
    both = ("tm", "space")

    def route(partner, ds):
        pairs = []
        for t in range(n_tm):
            for s in range(n_space):
                if 0 <= partner(t) < n_tm and 0 <= s + ds < n_space:
                    pairs.append((t * n_space + s, partner(t) * n_space + s + ds))
        return pairs

    def near(t):
        return t + 1 - 2 * (t % 2)

    def far(t):
        return t - 1 + 2 * (t % 2)

    first, last = flat[:halo], flat[body - halo :]
    near_mid = lax.ppermute(flat, both, route(near, 0))
    far_mid = lax.ppermute(flat, both, route(far, 0))
    near_top = lax.ppermute(last, both, route(near, 1))
    near_bot = lax.ppermute(first, both, route(near, -1))

    def down_column(ds):
        return [(a, b + ds) for a, b in route(lambda t: t, 0) if 0 <= far(a // n_space) < n_tm and 0 <= b % n_space + ds < n_space]

    far_top = lax.ppermute(far_mid[body - halo :], both, down_column(1))
    far_bot = lax.ppermute(far_mid[:halo], both, down_column(-1))

    def shape(*dims, dtype=BF):
        return pltpu.VMEM(dims, dtype)

    def result(*dims):
        return jax.ShapeDtypeStruct(dims, F32)

    near_vol, held, flow, held_targets, wc, bias, wv, wcb, wj, wjb, wf, wht = call(
        functools.partial(near_kernel, n_rows, n_cols), "near",
        (
            shape(HALF, body), shape(body, n_chan), shape(*flow_now.shape[1:]),
            shape(*targets.shape[1:], dtype=jnp.int32), shape(3, 3, C, C), shape(4, C, dtype=F32),
            shape(2 * HALF, C), shape(C, 9 * C), shape(18 * C, C),
            shape(2 * C, 9 * C), shape(112, C), shape(48, C),
        ),
        [HBM] * 11 + [VMEM] * 4,
        [
            pltpu.VMEM((body + 2 * halo, n_chan), BF),
            pltpu.VMEM((HALF, 2 * W), F32),
            pltpu.VMEM((2 * HALF, C), F32),
            pltpu.VMEM(w_volume.shape, BF),
            pltpu.VMEM(w_joint.shape, BF),
            pltpu.VMEM(w_flow.shape, BF),
            pltpu.SemaphoreType.DMA((11,)),
        ],
        4_000_000_000,
        flat, flow_now[0], targets[0], w_volume, w_code, w_joint, w_flow, b_volume, b_code, b_flow, b_joint,
        near_mid, near_top, near_bot, w_head.T,
    )
    vol, code, up, dn = call(
        functools.partial(code_kernel, n_rows, n_cols), "code",
        (shape(2 * HALF, body), shape(body, C), shape(halo + 16, C), shape(halo + 16, C)),
        [SMEM] + [VMEM] * 9,
        [
            pltpu.VMEM((body + 2 * halo, n_chan), BF),
            pltpu.VMEM((HALF, 2 * W), F32),
            pltpu.VMEM((16, W), F32),
        ],
        4_000_000_000,
        pair_order, held, far_mid, far_top, far_bot, near_vol, wv, bias, flow, held_targets,
    )
    top = lax.ppermute(dn, "space", [(s, s + 1) for s in range(n_space - 1)])
    bot = lax.ppermute(up, "space", [(s + 1, s) for s in range(n_space - 1)])

    d_code, code_t = call(
        code_slope_kernel, "slope", (shape(body, C, dtype=F32), shape(C, body)), [VMEM] * 4, [], 500_000_000,
        vol, wv, bias, code,
    )
    jf, d_flow, xb, tgt = call(
        functools.partial(flow_kernel, n_rows, n_cols), "flow",
        (
            shape((n_rows + 6) * W, 3 * C),
            shape((n_rows + 6) * W, C, dtype=F32),
            shape((n_rows + 12) * 16, W),
            shape(16, (n_rows + 4) * W, dtype=F32),
        ),
        [VMEM] * 6,
        [
            pltpu.VMEM((24, W), F32),
            pltpu.VMEM(((n_rows + 12) * 16, W), F32),
        ],
        1_000_000_000,
        top, bot, flow, held_targets, wf, bias,
    )
    flow_error, jt, s3, d_motion, misc = call(
        functools.partial(hidden_kernel, n_rows, n_cols, n_tm), "hidden",
        (
            result(2, n_rows, W),
            shape(2 * C, body),
            shape((n_rows + 4) * W, 3 * C),
            shape((n_rows + 6) * W, C, dtype=F32),
            shape(MISC_ROWS, C, dtype=F32),
        ),
        [SMEM] + [VMEM] * 9,
        [
            pltpu.VMEM(((n_rows + 8) * W, 3 * C), BF),
            pltpu.VMEM(((n_rows + 6) * W, 3 * C), BF),
            pltpu.VMEM((16, (n_rows + 4) * W), F32),
            pltpu.VMEM(((n_rows + 4) * W, C), BF),
            pltpu.VMEM((48, C), F32),
            pltpu.VMEM((8, C), F32),
        ],
        4_000_000_000,
        b_head, code, top, bot, jf, tgt, wc.reshape(9 * C, C), wj, wht, bias,
    )
    n_dev = n_tm * n_space
    paired = n_tm == 4 and n_space == 4
    if paired:
        grad_rows, at_misc = 3840, AT_END
    else:
        chunk = -(-max(pl.cdiv(AT_END, n_dev - 1), 3 * MISC_ROWS) // 16) * 16
        grad_rows, at_misc = n_dev * chunk, (n_dev - 1) * chunk
    keep, send = call(
        functools.partial(rest_kernel, n_rows, n_cols, at_misc), "rest",
        (shape(grad_rows // 2, C, dtype=F32), shape(grad_rows // 2, C, dtype=F32)),
        [VMEM] * 11,
        [
            pltpu.VMEM(((n_rows + 2) * W, 3 * C), BF),
            pltpu.VMEM(((n_rows + 2) * W, C), BF),
            pltpu.VMEM((body, C), BF),
            pltpu.VMEM((24, C), F32),
            pltpu.VMEM((grad_rows, C), F32),
        ],
        3_000_000_000,
        jt, s3, d_motion, d_flow, xb, vol, d_code, code_t, misc, wcb, wjb,
    )
    core = ("tm", 1)
    got = trade(send, *core)
    bits = jnp.stack([upper_of("tm", 1), upper_of("tm", 2), upper_of("space", 1), upper_of("space", 2)])
    bits = bits.astype(jnp.int32)
    if paired:
        mine = paired_reduce(keep + got, at_misc)
    else:
        mine = halving_reduce(keep + got, bits_of("tm")[1:] + bits_of("space"), upper_of(*core))
    other = trade(mine, *core)
    outs = call(
        functools.partial(finish_kernel, at_misc), "finish",
        (
            result(3, 3, 2 * C, C),
            result(3, 3, C, C),
            result(2 * OFF, C),
            result(7, 7, 2, C),
            result(C), result(C), result(C), result(C),
            result(2, C), result(1), result(2),
        ),
        [SMEM] + [VMEM] * 2, [pltpu.VMEM((grad_rows, C), BF)], 100_000_000,
        bits, mine, other,
        out_specs=(VMEM,) * 9 + (SMEM,) * 2,
    )
    joint, g_code, g_volume, g_flow, g_bv, g_bc, g_bf, g_bj, head, loss, g_b_head = outs
    return loss, flow_error[None], g_volume, g_bv, g_code, g_bc, g_flow, g_bf, joint, g_bj, head.T, g_b_head


def solution(mesh):
    placed = (
        P(("groups", "tm"), "space", None, None),
        P(("groups", "tm")),
        P(("groups", "tm"), None, "space", None),
        P(("groups", "tm"), None, "space", None),
    ) + (P(),) * 10
    return jax.shard_map(
        local,
        mesh=mesh,
        in_specs=placed,
        out_specs=(
            P("groups"),
            P(("groups", "tm"), None, "space", None),
            P("groups", None),
            P("groups"),
            P("groups", None, None, None),
            P("groups"),
            P("groups", None, None, None),
            P("groups"),
            P("groups", None, None, None),
            P("groups"),
            P("groups", None),
            P("groups"),
        ),
        check_vma=False,
    )
```

```python
import functools

import jax
import jax.numpy as jnp
from jax import lax
from jax.experimental import pallas as pl
from jax.experimental.pallas import tpu as pltpu
from jax.sharding import PartitionSpec as P

BF = jnp.bfloat16
F32 = jnp.float32
RADIUS = 4
SIDE = 2 * RADIUS + 1
OFF = SIDE * SIDE
HALO = 4
FLOW_HALO = 6
TARGET_HALO = 2
NT = (((1,), (1,)), ((), ()))
TN = (((0,), (0,)), ((), ()))

AT_CODE = 2304
AT_VOLUME = 3456
AT_FLOW = 3648
AT_END = 3760
HALF = 96
MOTION_BLOCK = 7
HIDDEN_BLOCK = 12
SLOPE_BLOCK = 10
CODE_BLOCK = 4
MISC_ROWS = 8


def dot(a, b):
    return jnp.dot(a, b, preferred_element_type=F32)


def dot_nt(a, b):
    return lax.dot_general(a, b, NT, preferred_element_type=F32)


def rows(start, count, unit):
    return pl.ds(pl.multiple_of(start * unit, unit), count * unit)


def split3(s, padded=False):
    hi = s.astype(BF).astype(F32)
    mid = (s - hi).astype(BF).astype(F32)
    terms = [hi, mid, s - hi - mid] + [jnp.zeros_like(s)] * padded
    return jnp.concatenate(terms, axis=0).astype(BF)


def silu_pair(v):
    s = jax.nn.sigmoid(v)
    return v * s, s * (1.0 + v * (1.0 - s))


def correlate(n_rows, n_cols, own, mid, top, bot, out, out_at, near, rows_f):
    n_chan = own.shape[1]
    halo = RADIUS * n_cols
    body = n_rows * n_cols
    near[0:halo, :] = top[...]
    near[halo : halo + body, :] = mid[...]
    near[halo + body :, :] = bot[...]
    W = n_cols
    j_at = lax.broadcasted_iota(jnp.int32, (W, 2 * W), 0)
    x_at = lax.broadcasted_iota(jnp.int32, (W, 2 * W), 1) & (W - 1)
    band = jnp.logical_and(j_at - x_at >= -RADIUS, j_at - x_at < RADIUS)
    edge = j_at - x_at == RADIUS
    turn = lax.broadcasted_iota(jnp.int32, (8, 2 * W), 1) + RADIUS
    scale = n_chan ** (-0.5)

    def fold(v):
        parts = [v[8 * g : 8 * g + 8] for g in range(W // 8)]
        while len(parts) > 1:
            parts = [parts[k] + parts[k + 1] for k in range(0, len(parts), 2)]
        return parts[0]

    def two_rows(b, carry):
        tile = own[rows(2 * b, 2, W), :]
        rows_f[...] = jnp.zeros_like(rows_f)
        for q in range(SIDE + 1):
            scores = lax.dot_general(
                near[rows(2 * b + q, 1, W), :], tile, NT, preferred_element_type=F32
            )
            inner = fold(jnp.where(band, scores, 0.0))
            outer = jnp.sum(fold(jnp.where(edge, scores, 0.0)), axis=0, keepdims=True)
            for bit in (1, 2, 4):
                inner = jnp.where((turn & bit) != 0, pltpu.roll(inner, 8 - bit, 0), inner)
            for u in range(2):
                dy = q - u
                if 0 <= dy < SIDE:
                    rows_f[8 * dy : 8 * dy + 8, u * W : (u + 1) * W] = inner[:, u * W : (u + 1) * W]
                    rows_f[72 + dy : 73 + dy, u * W : (u + 1) * W] = outer[:, u * W : (u + 1) * W]
        out[out_at, rows(2 * b, 2, W)] = (rows_f[...] * scale).astype(BF)
        return carry

    lax.fori_loop(0, n_rows // 2, two_rows, 0)


def near_kernel(
    n_rows, n_cols,
    own_hbm, flow_hbm, targets_hbm, volume_hbm, code_hbm, joint_hbm, w_flow_hbm, bv_hbm, bc_hbm, bf_hbm, bj_hbm,
    mid, top, bot, head,
    out, own, flow, targets, w_code, bias, wv, wcb, wj, wjb, wf, wht,
    near, rows_f, wide, w_volume, w_joint, w_flow, sems,
):
    loads = (
        (own_hbm, own), (flow_hbm, flow), (targets_hbm, targets), (volume_hbm, w_volume), (code_hbm, w_code),
        (joint_hbm, w_joint), (w_flow_hbm, w_flow), (bv_hbm, bias.at[0]), (bc_hbm, bias.at[1]),
        (bf_hbm, bias.at[2]), (bj_hbm, bias.at[3]),
    )
    copies = [pltpu.make_async_copy(src, dst, sems.at[k]) for k, (src, dst) in enumerate(loads)]
    for copy in copies:
        copy.start()
    copies[0].wait()
    correlate(n_rows, n_cols, own, mid, top, bot, out, slice(None), near, rows_f)
    for copy in copies[1:]:
        copy.wait()
    C = w_code.shape[3]
    wide[...] = jnp.zeros_like(wide)
    weight = w_volume[...].astype(F32)
    for half in range(2):
        for dy in range(SIDE):
            at = half * OFF + dy * SIDE
            wide[half * HALF + 8 * dy : half * HALF + 8 * dy + 8, :] = weight[at : at + 8]
            wide[half * HALF + 72 + dy : half * HALF + 73 + dy, :] = weight[at + 8 : at + 9]
    wv[...] = wide[...].astype(BF)
    wide[...] = jnp.zeros_like(wide)
    for i in range(7):
        for j in range(7):
            wide[16 * i + 2 * j : 16 * i + 2 * j + 2, :] = w_flow[i, j].astype(F32)
    wf[...] = wide[0:112, :].astype(BF)
    for i in range(3):
        for j in range(3):
            at = (3 * i + j) * C
            wcb[:, at : at + C] = w_code[i, j]
            wjb[:, at : at + C] = w_joint[i, j]
            for part in range(2):
                at = (2 * i + part) * 3 * C + j * C
                wj[at : at + C, :] = w_joint[i, j, part * C : (part + 1) * C, :]
    wide[...] = jnp.zeros_like(wide)
    for k in range(3):
        wide[16 * k : 16 * k + 2, :] = head[...].astype(F32)
    wht[...] = wide[0:48, :].astype(BF)


def code_kernel(
    n_rows, n_cols,
    order, own, mid, top, bot, near_vol, wv, bias, flow, targets,
    vol, code, up, dn,
    near, rows_f, edge,
):
    W = n_cols
    halo = HALO * W
    body = n_rows * W
    near_second = (order[0] != lax.axis_index("tm") % 2).astype(jnp.int32)
    near_at = pl.multiple_of(near_second * HALF, HALF)
    far_at = pl.multiple_of((1 - near_second) * HALF, HALF)
    vol[pl.ds(near_at, HALF), :] = near_vol[...]
    correlate(n_rows, n_cols, own, mid, top, bot, vol, pl.ds(far_at, HALF), near, rows_f)

    def one_code(r, carry):
        at = rows(r, CODE_BLOCK, W)
        pre = lax.dot_general(vol[:, at], wv[...], TN, preferred_element_type=F32) + bias[0:1, :]
        code[at, :] = (pre * jax.nn.sigmoid(pre)).astype(BF)
        return carry

    lax.fori_loop(0, n_rows // CODE_BLOCK, lambda r, c: one_code(CODE_BLOCK * r, c), 0)
    for ref, at, flow_at, target_at in (
        (up, 0, 0, 0),
        (dn, body - halo, n_rows - FLOW_HALO, n_rows - TARGET_HALO),
    ):
        ref[0:halo, :] = code[at : at + halo, :]
        for k in range(2):
            edge[8 * k : 8 * k + FLOW_HALO, :] = flow[k].astype(F32)[flow_at : flow_at + FLOW_HALO]
            edge[8 * k + FLOW_HALO : 8 * k + 8, :] = targets[k].astype(F32)[target_at : target_at + TARGET_HALO]
        ref[halo : halo + 16, :] = edge[...].astype(BF)


def frame_scale(n_tm, per):
    frame = lax.axis_index("tm")
    value = jnp.float32(per)
    for t in range(n_tm - 1):
        value = jnp.where(frame == t, jnp.float32(per * 0.25 ** ((n_tm - 1 - t) / (n_tm - 1))), value)
    return value


def code_slope_kernel(vol, wv, bias, code, d_code, code_t):
    pre = lax.dot_general(vol[...], wv[...], TN, preferred_element_type=F32) + bias[0:1, :]
    d_code[...] = silu_pair(pre)[1]
    code_t[...] = code[...].T


def inside_frame(n_rows, ext):
    at = lax.axis_index("space") * n_rows + ext
    return jnp.logical_and(at >= 0, at < lax.axis_size("space") * n_rows)


def store_stack(ref, at, v, cols):
    W, C = v.shape
    x_at = lax.broadcasted_iota(jnp.int32, (W, C), 0)
    left = jnp.where(x_at == 0, 0.0, pltpu.roll(v, 1, 0))
    right = jnp.where(x_at == W - 1, 0.0, pltpu.roll(v, W - 1, 0))
    for col, part in zip(cols, (left, v, right)):
        ref[rows(at, 1, W), col * C : (col + 1) * C] = part.astype(BF)


FWD = (0, 1, 2)
BWD = (2, 1, 0)


def flow_kernel(n_rows, n_cols, top, bot, flow, targets, wf, bias, jf, d_flow, xb, tgt, xf, xx):
    W = n_cols
    halo = HALO * W
    xx[...] = jnp.zeros_like(xx)
    above = top[halo : halo + 16, :].astype(F32)
    below = bot[halo : halo + 16, :].astype(F32)
    n_flow = n_rows + 2 * FLOW_HALO
    lane = lax.broadcasted_iota(jnp.int32, (n_flow, W), 1)
    for k in range(2):
        xf[0:FLOW_HALO, :] = above[8 * k : 8 * k + FLOW_HALO, :]
        xf[FLOW_HALO : FLOW_HALO + n_rows, :] = flow[k].astype(F32)
        xf[FLOW_HALO + n_rows : n_flow, :] = below[8 * k : 8 * k + FLOW_HALO, :]
        own_flow = xf[0:n_flow, :]
        for j in range(7):
            shift = (3 - j) % W
            moved = pltpu.roll(own_flow, shift, 1) if shift else own_flow
            ok = jnp.logical_and(lane + (j - 3) >= 0, lane + (j - 3) < W)
            xx[pl.ds(j * 2 + k, n_flow, stride=16), :] = jnp.where(ok, moved, 0.0)
    xb[...] = xx[...].astype(BF)
    tgt[...] = jnp.zeros_like(tgt)
    for k in range(2):
        for y in range(TARGET_HALO):
            tgt[k : k + 1, y * W : (y + 1) * W] = above[8 * k + 6 + y : 8 * k + 7 + y, :]
            lo = (TARGET_HALO + n_rows + y) * W
            tgt[k : k + 1, lo : lo + W] = below[8 * k + 6 + y : 8 * k + 7 + y, :]
        for y in range(n_rows):
            lo = (TARGET_HALO + y) * W
            tgt[k : k + 1, lo : lo + W] = targets[k, y : y + 1, :].astype(F32)

    def flow_rows(b, carry):
        y = b * MOTION_BLOCK
        patches = [xb[pl.ds(pl.multiple_of((y + u) * 16, 16), 112), :] for u in range(MOTION_BLOCK)]
        pre = lax.dot_general(jnp.concatenate(patches, axis=1), wf[...], TN, preferred_element_type=F32)
        for u in range(MOTION_BLOCK):
            value, slope = silu_pair(pre[u * W : (u + 1) * W] + bias[2:3, :])
            d_flow[rows(y + u, 1, W), :] = slope
            store_stack(jf, y + u, jnp.where(inside_frame(n_rows, y + u - 3), value, 0.0), FWD)
        return carry

    lax.fori_loop(0, (n_rows + 6) // MOTION_BLOCK, flow_rows, 0)


def hidden_kernel(
    n_rows, n_cols, n_tm,
    b_head, code, top, bot, jf, tgt, wc, wj, wht, bias,
    error_out, jt, s3, d_motion, misc,
    c3, jm, err, hid, g_head, acc,
):
    W = n_cols
    count = 2.0 * n_tm * lax.axis_size("space") * n_rows * n_cols
    slope_scale = frame_scale(n_tm, 2.0 / count)
    C = wc.shape[1]
    body = n_rows * W

    def load_halo(y, carry):
        store_stack(c3, y, top[rows(y, 1, W), :].astype(F32), FWD)
        store_stack(c3, y + HALO + n_rows, bot[rows(y, 1, W), :].astype(F32), FWD)
        return carry

    def load_code(y, carry):
        store_stack(c3, y + HALO, code[rows(y, 1, W), :].astype(F32), FWD)
        return carry

    lax.fori_loop(0, HALO, load_halo, 0)
    lax.fori_loop(0, n_rows, load_code, 0)

    def motion_rows(b, carry):
        y = b * MOTION_BLOCK
        taps = jnp.concatenate([c3[rows(y + i, MOTION_BLOCK, W), :] for i in range(3)], axis=1)
        pre = dot(taps, wc[...]) + bias[1:2, :]
        for u in range(MOTION_BLOCK):
            value, slope = silu_pair(pre[u * W : (u + 1) * W])
            d_motion[rows(y + u, 1, W), :] = slope
            store_stack(jm, y + u, jnp.where(inside_frame(n_rows, y + u - 3), value, 0.0), FWD)
        return carry

    lax.fori_loop(0, (n_rows + 6) // MOTION_BLOCK, motion_rows, 0)

    block = HIDDEN_BLOCK
    k_row = lax.broadcasted_iota(jnp.int32, (16, block * W), 0)
    b_col = jnp.where(k_row == 0, b_head[0], jnp.where(k_row == 1, b_head[1], 0.0))

    def hidden_rows(b, carry):
        y = b * block
        taps = [ref[rows(y + i, block, W), :] for i in range(3) for ref in (jm, jf)]
        pre = dot(jnp.concatenate(taps, axis=1), wj[...]) + bias[3:4, :]
        value, slope = silu_pair(pre)
        hidden = value.astype(BF)
        hid[rows(y, block, W), :] = hidden
        pred = lax.dot_general(wht[0:16, :], hidden, NT, preferred_element_type=F32)
        error = pred + b_col - tgt[:, rows(y, block, W)]
        err[:, rows(y, block, W)] = error
        back = lax.dot_general(split3(error * slope_scale), wht[...], TN, preferred_element_type=F32) * slope
        for u in range(block):
            v = jnp.where(inside_frame(n_rows, y + u - 2), back[u * W : (u + 1) * W], 0.0)
            store_stack(s3, y + u, v, BWD)
        return carry

    lax.fori_loop(0, (n_rows + 4) // block, hidden_rows, 0)

    acc[...] = jnp.zeros_like(acc)
    g_head[...] = jnp.zeros_like(g_head)

    def own_rows(b, carry):
        y = 2 * b
        g_head[...] += dot(split3(err[:, rows(y + 2, 2, W)] * slope_scale), hid[rows(y + 2, 2, W), :])
        part = s3[rows(y + 2, 2, W), C : 2 * C].astype(F32)
        acc[...] += jnp.sum(part.reshape(2 * W // 8, 8, C), axis=0)
        jt[0:C, rows(y, 2, W)] = jm[rows(y + 3, 2, W), C : 2 * C].T
        jt[C : 2 * C, rows(y, 2, W)] = jf[rows(y + 3, 2, W), C : 2 * C].T
        return carry

    lax.fori_loop(0, n_rows // 2, own_rows, 0)
    own = err[:, TARGET_HALO * W : TARGET_HALO * W + body]
    for k in range(2):
        for y in range(n_rows):
            error_out[k, y : y + 1, :] = own[k : k + 1, y * W : (y + 1) * W]
    g_b_head = jnp.sum(own * slope_scale, axis=1, keepdims=True)
    loss = jnp.sum(jnp.sum(own * own, axis=1, keepdims=True), axis=0, keepdims=True)
    loss = loss * frame_scale(n_tm, 1.0 / count)
    col = lax.broadcasted_iota(jnp.int32, (1, C), 1)
    tail = jnp.where(col == 0, loss, jnp.where(col == 1, g_b_head[0:1], jnp.where(col == 2, g_b_head[1:2], 0.0)))
    misc[0:3, :] = jnp.zeros((3, C), F32)
    misc[3:4, :] = jnp.sum(acc[...], axis=0, keepdims=True)
    misc[4:6, :] = g_head[0:2, :] + g_head[16:18, :] + g_head[32:34, :]
    misc[6:7, :] = tail
    misc[7:8, :] = jnp.zeros((1, C), F32)


def rest_kernel(
    n_rows, n_cols, at_misc,
    jt, s3, d_motion, d_flow, xb, vol, d_code, code_t, misc, wcb, wjb,
    keep, send,
    m3, s_flow, s_code, acc, grads,
):
    W = n_cols
    C = d_code.shape[1]
    body = n_rows * W

    def joint_slopes(b, carry):
        y = b * SLOPE_BLOCK
        taps = jnp.concatenate([s3[rows(y + 2 - i, SLOPE_BLOCK, W), :] for i in range(3)], axis=1)
        sj = dot_nt(taps, wjb[...])
        for u in range(SLOPE_BLOCK):
            part = sj[u * W : (u + 1) * W]
            v = part[:, 0:C] * d_motion[rows(y + u + 2, 1, W), :]
            store_stack(m3, y + u, jnp.where(inside_frame(n_rows, y + u - 1), v, 0.0), BWD)
            s_flow[rows(y + u, 1, W), :] = (part[:, C:] * d_flow[rows(y + u + 2, 1, W), :]).astype(BF)
        return carry

    lax.fori_loop(0, (n_rows + 2) // SLOPE_BLOCK, joint_slopes, 0)
    acc[...] = jnp.zeros_like(acc)

    def add_rows(k, v):
        acc[8 * k : 8 * k + 8, :] += jnp.sum(v.reshape(v.shape[0] // 8, 8, C), axis=0)

    def code_slopes(b, carry):
        y = b * CODE_BLOCK
        at = rows(y, CODE_BLOCK, W)
        taps = jnp.concatenate([m3[rows(y + 2 - i, CODE_BLOCK, W), :] for i in range(3)], axis=1)
        sc = dot_nt(taps, wcb[...])
        slope = (sc * d_code[at, :]).astype(BF)
        s_code[at, :] = slope
        add_rows(0, slope.astype(F32))
        add_rows(1, m3[rows(y + 1, CODE_BLOCK, W), C : 2 * C].astype(F32))
        add_rows(2, s_flow[rows(y + 1, CODE_BLOCK, W), :].astype(F32))
        return carry

    lax.fori_loop(0, n_rows // CODE_BLOCK, code_slopes, 0)

    for i in range(3):
        g = dot(jt[...], s3[(3 - i) * W : (3 - i) * W + body, :])
        for j in range(3):
            at = (i * 3 + j) * 2 * C
            grads[at : at + 2 * C, :] = g[:, j * C : (j + 1) * C]
    for i in range(3):
        g = dot(code_t[...], m3[(2 - i) * W : (2 - i) * W + body, :])
        for j in range(3):
            at = AT_CODE + (i * 3 + j) * C
            grads[at : at + C, :] = g[:, j * C : (j + 1) * C]
    grads[AT_VOLUME:AT_FLOW, :] = dot(vol[...], s_code[...])
    gf = jnp.zeros((112, C), F32)
    for y in range(n_rows):
        gf = gf + dot(xb[(y + 3) * 16 : (y + 3) * 16 + 112, :], s_flow[(y + 1) * W : (y + 2) * W, :])
    grads[AT_FLOW : AT_FLOW + 112, :] = gf
    if at_misc > AT_END:
        grads[AT_END:at_misc, :] = jnp.zeros((at_misc - AT_END, C), F32)
    for k in range(3):
        grads[at_misc + k : at_misc + k + 1, :] = jnp.sum(acc[8 * k : 8 * k + 8, :], axis=0, keepdims=True)
    grads[at_misc + 3 : at_misc + 8, :] = misc[3:8, :]
    grads[at_misc + 8 :, :] = jnp.zeros((grads.shape[0] - at_misc - 8, C), F32)
    half = keep.shape[0]
    core = lax.axis_index("tm") % 2
    keep[...] = pick(grads, core, half)
    send[...] = pick(grads, 1 - core, half)


VMEM = pl.BlockSpec(memory_space=pltpu.VMEM)
SMEM = pl.BlockSpec(memory_space=pltpu.SMEM)
HBM = pl.BlockSpec(memory_space=pltpu.HBM)


def bits_of(axis):
    bits = []
    bit = 1
    while bit < lax.axis_size(axis):
        bits.append((axis, bit))
        bit *= 2
    return bits


def trade(x, axis, bit):
    return lax.ppermute(x, axis, [(i, i ^ bit) for i in range(lax.axis_size(axis))])


def upper_of(axis, bit):
    return (lax.axis_index(axis) // bit) % 2


def three_terms(x, at, is_last):
    value = x[at : at + MISC_ROWS]
    mid = value - lax.reduce_precision(value, 8, 7)
    low = mid - lax.reduce_precision(mid, 8, 7)
    terms = jnp.concatenate([x[: at + MISC_ROWS], mid, low, x[at + 3 * MISC_ROWS :]])
    return jnp.where(is_last, terms, x).astype(BF)


def halving_reduce(x, steps, is_last):
    for axis, bit in steps:
        upper = upper_of(axis, bit)
        is_last = is_last * upper
        half = x.shape[0] // 2
        mine = lax.dynamic_slice_in_dim(x, upper * half, half, 0)
        other = lax.dynamic_slice_in_dim(x, (1 - upper) * half, half, 0)
        x = mine + trade(other, axis, bit)
    x = three_terms(x, 0, is_last == 1)
    for axis, bit in steps[::-1]:
        got = trade(x, axis, bit)
        x = jnp.where(upper_of(axis, bit) == 0, jnp.concatenate([x, got]), jnp.concatenate([got, x]))
    return x


def pick(ref, which, half):
    return ref[pl.ds(pl.multiple_of(which * half, 8), half), :]


def cut(x, which, n):
    return lax.dynamic_slice_in_dim(x, which * n, n, 0)


def ordered(mine, got, axis, bit):
    return jnp.where(upper_of(axis, bit) == 0, jnp.concatenate([mine, got]), jnp.concatenate([got, mine]))


def add_terms(x, got, at, holds):
    misc = x[at : at + MISC_ROWS] + sum(got[at + k * MISC_ROWS : at + (k + 1) * MISC_ROWS] for k in range(3))
    fixed = jnp.concatenate([misc, jnp.zeros((2 * MISC_ROWS, misc.shape[1]), F32)])
    x = x + got
    return jnp.concatenate([x[:at], jnp.where(holds, fixed, x[at : at + 3 * MISC_ROWS]), x[at + 3 * MISC_ROWS :]])


def paired_reduce(x_sum, at_misc):
    half = x_sum.shape[0]
    x, z, far_z = ("tm", 2), ("space", 1), ("space", 2)
    upper_x, upper_z, upper_far, core = upper_of(*x), upper_of(*z), upper_of(*far_z), upper_of("tm", 1)
    a, b = x_sum[: half // 2], x_sum[half // 2 :]
    n = half // 4
    at = at_misc - 2 * half + n
    sends = jnp.logical_and(core == 1, upper_z == 0)
    holds = jnp.logical_and(core == 1, upper_z == 1)
    a_got = trade(cut(a, 1 - upper_x, n).astype(BF), *x)
    b_got = trade(three_terms(cut(b, 1 - upper_z, n), at, sends), *z)
    a = cut(a, upper_x, n) + a_got.astype(F32)
    b = add_terms(cut(b, upper_z, n), b_got.astype(F32), at, holds)
    n = half // 8
    at = at_misc - (2 * half - n)
    a_got = trade(cut(a, 1 - upper_z, n).astype(BF), *z)
    b_got = trade(three_terms(cut(b, 1 - upper_x, n), at, core + upper_z - upper_x == 2), *x)
    a = cut(a, upper_z, n) + a_got.astype(F32)
    b = add_terms(cut(b, upper_x, n), b_got.astype(F32), at, core + upper_z + upper_x == 3)
    is_far = upper_far == 1
    corner = core + upper_x + upper_z
    sent = three_terms(jnp.where(is_far, a, b), at, corner - upper_far == 3)
    y = add_terms(jnp.where(is_far, b, a), trade(sent, *far_z).astype(F32), at, corner + upper_far == 4)
    y = three_terms(y, at, corner + upper_far == 4)
    got = trade(y, *far_z)
    a, b = jnp.where(is_far, got, y), jnp.where(is_far, y, got)
    a, b = ordered(a, trade(a, *z), *z), ordered(b, trade(b, *x), *x)
    a, b = ordered(a, trade(a, *x), *x), ordered(b, trade(b, *z), *z)
    return jnp.concatenate([a, b])


def finish_kernel(
    at_misc,
    bits, mine, other,
    joint, code, volume, flow, b_volume, b_code, b_flow, b_joint, head, loss, b_head,
    full,
):
    half, C = mine.shape
    full[pl.ds(pl.multiple_of(bits[0] * half, 16), half), :] = mine[...]
    full[pl.ds(pl.multiple_of((1 - bits[0]) * half, 16), half), :] = other[...]
    for i in range(3):
        for j in range(3):
            at = (i * 3 + j) * 2 * C
            joint[i, j, :, :] = full[at : at + 2 * C, :].astype(F32)
            at = AT_CODE + (i * 3 + j) * C
            code[i, j, :, :] = full[at : at + C, :].astype(F32)
    parts = full[AT_VOLUME:AT_FLOW, :].astype(F32)
    for half_at in range(2):
        for dy in range(SIDE):
            at, to = half_at * HALF, half_at * OFF + dy * SIDE
            volume[to : to + 8, :] = parts[at + 8 * dy : at + 8 * dy + 8]
            volume[to + 8 : to + 9, :] = parts[at + 72 + dy : at + 73 + dy]
    for i in range(7):
        part = full[AT_FLOW + 16 * i : AT_FLOW + 16 * i + 16, :].astype(F32)
        for j in range(7):
            flow[i, j, :, :] = part[2 * j : 2 * j + 2]
    terms = full[at_misc : at_misc + 32, :].astype(F32)
    misc = terms[0:8] + terms[8:16] + terms[16:24]
    for k, ref in enumerate((b_volume, b_code, b_flow, b_joint)):
        ref[...] = misc[k]
    head[...] = misc[4:6]
    lane = lax.broadcasted_iota(jnp.int32, (1, C), 1)
    loss[0] = jnp.sum(jnp.where(lane == 0, misc[6:7], 0.0))
    b_head[0] = jnp.sum(jnp.where(lane == 1, misc[6:7], 0.0))
    b_head[1] = jnp.sum(jnp.where(lane == 2, misc[6:7], 0.0))


def call(body, name, out_shape, in_specs, scratch, flops, *args, out_specs=None):
    held = [
        x if spec is SMEM else pltpu.with_memory_space_constraint(x, spec.memory_space)
        for x, spec in zip(args, in_specs, strict=True)
    ]
    return pl.pallas_call(
        body,
        out_shape=out_shape,
        in_specs=in_specs,
        out_specs=out_specs or jax.tree.map(lambda _: VMEM, out_shape),
        scratch_shapes=scratch,
        cost_estimate=pl.CostEstimate(flops=flops, bytes_accessed=flops // 300, transcendentals=0),
        compiler_params=pltpu.CompilerParams(vmem_limit_bytes=16 << 20),
        name=name,
    )(*held)


def local(
    features, pair_order, flow_now, targets, w_volume, b_volume, w_code, b_code,
    w_flow, b_flow, w_joint, b_joint, w_head, b_head,
):
    own = features[0]
    n_rows, n_cols, n_chan = own.shape
    n_code = w_code.shape[3]
    W, C = n_cols, n_code
    body = n_rows * n_cols
    halo = HALO * n_cols
    n_tm, n_space = lax.axis_size("tm"), lax.axis_size("space")
    flat = own.reshape(body, n_chan)
    both = ("tm", "space")

    def route(partner, ds):
        pairs = []
        for t in range(n_tm):
            for s in range(n_space):
                if 0 <= partner(t) < n_tm and 0 <= s + ds < n_space:
                    pairs.append((t * n_space + s, partner(t) * n_space + s + ds))
        return pairs

    def near(t):
        return t + 1 - 2 * (t % 2)

    def far(t):
        return t - 1 + 2 * (t % 2)

    first, last = flat[:halo], flat[body - halo :]
    near_mid = lax.ppermute(flat, both, route(near, 0))
    far_mid = lax.ppermute(flat, both, route(far, 0))
    near_top = lax.ppermute(last, both, route(near, 1))
    near_bot = lax.ppermute(first, both, route(near, -1))

    def down_column(ds):
        return [(a, b + ds) for a, b in route(lambda t: t, 0) if 0 <= far(a // n_space) < n_tm and 0 <= b % n_space + ds < n_space]

    far_top = lax.ppermute(far_mid[body - halo :], both, down_column(1))
    far_bot = lax.ppermute(far_mid[:halo], both, down_column(-1))

    def shape(*dims, dtype=BF):
        return pltpu.VMEM(dims, dtype)

    def result(*dims):
        return jax.ShapeDtypeStruct(dims, F32)

    near_vol, held, flow, held_targets, wc, bias, wv, wcb, wj, wjb, wf, wht = call(
        functools.partial(near_kernel, n_rows, n_cols), "near",
        (
            shape(HALF, body), shape(body, n_chan), shape(*flow_now.shape[1:]),
            shape(*targets.shape[1:], dtype=jnp.int32), shape(3, 3, C, C), shape(4, C, dtype=F32),
            shape(2 * HALF, C), shape(C, 9 * C), shape(18 * C, C),
            shape(2 * C, 9 * C), shape(112, C), shape(48, C),
        ),
        [HBM] * 11 + [VMEM] * 4,
        [
            pltpu.VMEM((body + 2 * halo, n_chan), BF),
            pltpu.VMEM((HALF, 2 * W), F32),
            pltpu.VMEM((2 * HALF, C), F32),
            pltpu.VMEM(w_volume.shape, BF),
            pltpu.VMEM(w_joint.shape, BF),
            pltpu.VMEM(w_flow.shape, BF),
            pltpu.SemaphoreType.DMA((11,)),
        ],
        4_000_000_000,
        flat, flow_now[0], targets[0], w_volume, w_code, w_joint, w_flow, b_volume, b_code, b_flow, b_joint,
        near_mid, near_top, near_bot, w_head.T,
    )
    vol, code, up, dn = call(
        functools.partial(code_kernel, n_rows, n_cols), "code",
        (shape(2 * HALF, body), shape(body, C), shape(halo + 16, C), shape(halo + 16, C)),
        [SMEM] + [VMEM] * 9,
        [
            pltpu.VMEM((body + 2 * halo, n_chan), BF),
            pltpu.VMEM((HALF, 2 * W), F32),
            pltpu.VMEM((16, W), F32),
        ],
        4_000_000_000,
        pair_order, held, far_mid, far_top, far_bot, near_vol, wv, bias, flow, held_targets,
    )
    top = lax.ppermute(dn, "space", [(s, s + 1) for s in range(n_space - 1)])
    bot = lax.ppermute(up, "space", [(s + 1, s) for s in range(n_space - 1)])

    d_code, code_t = call(
        code_slope_kernel, "slope", (shape(body, C, dtype=F32), shape(C, body)), [VMEM] * 4, [], 500_000_000,
        vol, wv, bias, code,
    )
    jf, d_flow, xb, tgt = call(
        functools.partial(flow_kernel, n_rows, n_cols), "flow",
        (
            shape((n_rows + 6) * W, 3 * C),
            shape((n_rows + 6) * W, C, dtype=F32),
            shape((n_rows + 12) * 16, W),
            shape(16, (n_rows + 4) * W, dtype=F32),
        ),
        [VMEM] * 6,
        [
            pltpu.VMEM((24, W), F32),
            pltpu.VMEM(((n_rows + 12) * 16, W), F32),
        ],
        1_000_000_000,
        top, bot, flow, held_targets, wf, bias,
    )
    flow_error, jt, s3, d_motion, misc = call(
        functools.partial(hidden_kernel, n_rows, n_cols, n_tm), "hidden",
        (
            result(2, n_rows, W),
            shape(2 * C, body),
            shape((n_rows + 4) * W, 3 * C),
            shape((n_rows + 6) * W, C, dtype=F32),
            shape(MISC_ROWS, C, dtype=F32),
        ),
        [SMEM] + [VMEM] * 9,
        [
            pltpu.VMEM(((n_rows + 8) * W, 3 * C), BF),
            pltpu.VMEM(((n_rows + 6) * W, 3 * C), BF),
            pltpu.VMEM((16, (n_rows + 4) * W), F32),
            pltpu.VMEM(((n_rows + 4) * W, C), BF),
            pltpu.VMEM((48, C), F32),
            pltpu.VMEM((8, C), F32),
        ],
        4_000_000_000,
        b_head, code, top, bot, jf, tgt, wc.reshape(9 * C, C), wj, wht, bias,
    )
    n_dev = n_tm * n_space
    paired = n_tm == 4 and n_space == 4
    if paired:
        grad_rows, at_misc = 3840, AT_END
    else:
        chunk = -(-max(pl.cdiv(AT_END, n_dev - 1), 3 * MISC_ROWS) // 16) * 16
        grad_rows, at_misc = n_dev * chunk, (n_dev - 1) * chunk
    keep, send = call(
        functools.partial(rest_kernel, n_rows, n_cols, at_misc), "rest",
        (shape(grad_rows // 2, C, dtype=F32), shape(grad_rows // 2, C, dtype=F32)),
        [VMEM] * 11,
        [
            pltpu.VMEM(((n_rows + 2) * W, 3 * C), BF),
            pltpu.VMEM(((n_rows + 2) * W, C), BF),
            pltpu.VMEM((body, C), BF),
            pltpu.VMEM((24, C), F32),
            pltpu.VMEM((grad_rows, C), F32),
        ],
        3_000_000_000,
        jt, s3, d_motion, d_flow, xb, vol, d_code, code_t, misc, wcb, wjb,
    )
    core = ("tm", 1)
    got = trade(send, *core)
    bits = jnp.stack([upper_of("tm", 1), upper_of("tm", 2), upper_of("space", 1), upper_of("space", 2)])
    bits = bits.astype(jnp.int32)
    if paired:
        mine = paired_reduce(keep + got, at_misc)
    else:
        mine = halving_reduce(keep + got, bits_of("tm")[1:] + bits_of("space"), upper_of(*core))
    other = trade(mine, *core)
    outs = call(
        functools.partial(finish_kernel, at_misc), "finish",
        (
            result(3, 3, 2 * C, C),
            result(3, 3, C, C),
            result(2 * OFF, C),
            result(7, 7, 2, C),
            result(C), result(C), result(C), result(C),
            result(2, C), result(1), result(2),
        ),
        [SMEM] + [VMEM] * 2, [pltpu.VMEM((grad_rows, C), BF)], 100_000_000,
        bits, mine, other,
        out_specs=(VMEM,) * 9 + (SMEM,) * 2,
    )
    joint, g_code, g_volume, g_flow, g_bv, g_bc, g_bf, g_bj, head, loss, g_b_head = outs
    return loss, flow_error[None], g_volume, g_bv, g_code, g_bc, g_flow, g_bf, joint, g_bj, head.T, g_b_head


def solution(mesh):
    placed = (
        P(("groups", "tm"), "space", None, None),
        P(("groups", "tm")),
        P(("groups", "tm"), None, "space", None),
        P(("groups", "tm"), None, "space", None),
    ) + (P(),) * 10
    return jax.shard_map(
        local,
        mesh=mesh,
        in_specs=placed,
        out_specs=(
            P("groups"),
            P(("groups", "tm"), None, "space", None),
            P("groups", None),
            P("groups"),
            P("groups", None, None, None),
            P("groups"),
            P("groups", None, None, None),
            P("groups"),
            P("groups", None, None, None),
            P("groups"),
            P("groups", None),
            P("groups"),
        ),
        check_vma=False,
    )
```
